256 devices in a mesh: ctx: 32 (over z, x), head: 8 (over y, core).
Axes of the slice: x: 4, y: 4, z: 8, core: 2. Of those that a mesh axis runs over, the one named last changes fastest.
Arguments:
- x_raw: bfloat16 [8192, 8192], P('ctx', 'head'), may hold values from -6 to 6
- bc_raw: bfloat16 [8192, 256], P('ctx'), may hold values from -6 to 6
- conv_x_w: bfloat16 [4, 8192], P(None, 'head'), may hold values from -3 to 3
- conv_bc_w: bfloat16 [4, 256], replicated, may hold values from -3 to 3
- dt_raw: float32 [128, 8192], P('head', 'ctx'), may hold values from -7 to 0
- a_log: float32 [128], P('head'), may hold values from -10 to 1
- d_skip: float32 [128], P('head'), may hold values from 0.5 to 1.5
- doc_starts: int32 [32], P('ctx'), may hold values from 0 to 256, as said below
- grad_y: bfloat16 [8192, 8192], P('ctx', 'head'), may hold values from -6 to 6
Outputs:
- y_out: bfloat16 [8192, 8192], P('ctx', 'head')
- grad_x_raw: bfloat16 [8192, 8192], P('ctx', 'head')
- grad_bc_raw: bfloat16 [8192, 256], P('ctx')
- grad_dt_raw: float32 [128, 8192], P('head', 'ctx')
The draws below stay inside these ranges and needn't reach their ends.
Inputs may be any that keep to these rules, and one draw needn't show every extreme that they name: Block b holds a document start at row 256 * b + doc_starts[b] when doc_starts[b] < 256, and none when doc_starts[b] = 256; doc_starts[0] = 0.
All inputs are finite; a program needn't handle non-finite values.
Results may differ from the reference program's by a relative error of at most 0.013.
Values may be sent and summed in bfloat16 or wider, within the bound.
No kernel may reach another device: no remote copies, remote signals or barrier semaphores. Data moves between devices by JAX's collectives and lax.ppermute only.
A program may use at most 128 MiB of HBM per device.

```python
import math
import jax
import jax.numpy as jnp
from jax import lax

ATTENTION_COUNT = 128
STATE = 128
KERNEL = 4
BLOCK = 256
TOK_DEV = 256
TOKEN_LENGTH = 8192
NBLOCKS = 32
CHANNELS = 8192


def draw_a_log(key, part):
    lowest = math.log(1.0 / TOK_DEV)
    highest = math.log(2.0)
    return jax.random.uniform(key, (ATTENTION_COUNT,), jnp.float32, lowest, highest)


def draw_dt_raw(key, part):
    key_base = jax.random.fold_in(key, 11)
    random_seed_batch = jax.random.fold_in(key, 12)
    key_level = jax.random.fold_in(key, 13)
    starting_index = jnp.clip(-4.0 + 0.7 * jax.random.normal(key_base, (ATTENTION_COUNT, TOKEN_LENGTH), jnp.float32), -6.5, -1.5)
    parallel_batch = jax.random.uniform(random_seed_batch, (ATTENTION_COUNT, TOKEN_LENGTH), jnp.float32) < 1.0 / 128.0
    layer_index = jax.random.uniform(key_level, (ATTENTION_COUNT, TOKEN_LENGTH), jnp.float32, -1.0, 0.0)
    return jnp.where(parallel_batch, layer_index, starting_index)


def draw_doc_starts(key, part):
    key_pick = jax.random.fold_in(key, 21)
    key_for_spot = jax.random.fold_in(key, 22)
    picked = jax.random.randint(key_pick, (NBLOCKS,), 0, 8)
    spot = jax.random.randint(key_for_spot, (NBLOCKS,), 0, BLOCK)
    values = jnp.where(picked == 0, spot, BLOCK)
    values = jnp.where(jnp.arange(NBLOCKS) == 0, 0, values)
    return values.astype(jnp.int32)


def block_levels(key, dims, split, low, top_value):
    gain, own = 1.0, jax.random.fold_in(key, 6)
    for axis_at, blocks in split:
        draws = jnp.exp(jax.random.uniform(jax.random.fold_in(own, axis_at), (blocks,), jnp.float32, low / len(split), top_value / len(split)))
        gain = gain * jnp.repeat(draws, dims[axis_at] // blocks).reshape([-1 if axis == axis_at else 1 for axis in range(len(dims))])
    return gain


def normal_values(stream_key, shape, spread, bound, split=(), held_as=jnp.bfloat16):
    values = spread * jax.random.normal(stream_key, shape, jnp.float32)
    if split:
        values = values * block_levels(stream_key, shape, split, -0.22, 0.18)
    return jnp.clip(values, -bound, bound).astype(held_as)


def setup_inputs(seed: int = 0) -> dict:
    key_list = jax.random.split(jax.random.key(seed), 10)
    x_raw = normal_values(key_list[0], (TOKEN_LENGTH, CHANNELS), 1.0, 6.0, ((0, 32), (1, 8)))
    bc_raw = normal_values(key_list[1], (TOKEN_LENGTH, 2 * STATE), 1.0, 6.0, ((0, 32),))
    conv_x_w = normal_values(key_list[2], (KERNEL, CHANNELS), KERNEL ** -0.5, 3.0, ((1, 8),))
    conv_bc_w = normal_values(key_list[3], (KERNEL, 2 * STATE), KERNEL ** -0.5, 3.0)
    dt_raw = draw_dt_raw(jax.random.fold_in(key_list[9], 71), 0)
    a_log = draw_a_log(jax.random.fold_in(key_list[9], 71), 0)
    d_skip = jnp.clip(0.5 + 1.0 * jax.random.uniform(key_list[6], (ATTENTION_COUNT,), jnp.float32) ** block_levels(key_list[6], (ATTENTION_COUNT,), ((0, 8),), -0.2, 0.2), 0.5, 1.5)
    doc_starts = draw_doc_starts(jax.random.fold_in(key_list[9], 71), 0)
    grad_y = normal_values(key_list[8], (TOKEN_LENGTH, CHANNELS), 1.0, 6.0, ((0, 32), (1, 8)))
    return dict(x_raw=x_raw, bc_raw=bc_raw, conv_x_w=conv_x_w, conv_bc_w=conv_bc_w, dt_raw=dt_raw, a_log=a_log, d_skip=d_skip, doc_starts=doc_starts, grad_y=grad_y)


def contract(pattern, first_op, second_op):
    return jnp.einsum(pattern, first_op.astype(jnp.float32), second_op.astype(jnp.float32))

def contract_exact(pattern, first_op, second_op):
    return jnp.einsum(pattern, first_op.astype(jnp.float32), second_op.astype(jnp.float32), precision=lax.Precision.HIGHEST)

def silu_grad(values):
    sigmoid_v = jax.nn.sigmoid(values)
    return sigmoid_v * (1.0 + values * (1.0 - sigmoid_v))

def causal_conv(tok_rows, before, weight):
    row_count = tok_rows.shape[0]
    tap_count = weight.shape[0]
    padded = jnp.concatenate([before, tok_rows], axis=0).astype(jnp.float32)
    weight_f = weight.astype(jnp.float32)
    running = jnp.zeros(tok_rows.shape, jnp.float32)
    for offset in range(tap_count):
        running = running + weight_f[offset] * padded[offset:offset + row_count]
    return running

def conv_back(gradient, following, weight):
    row_count = gradient.shape[0]
    tap_count = weight.shape[0]
    padded = jnp.concatenate([gradient, following], axis=0)
    weight_f = weight.astype(jnp.float32)
    running = jnp.zeros(gradient.shape, jnp.float32)
    for offset in range(tap_count):
        running = running + weight_f[tap_count - 1 - offset] * padded[offset:offset + row_count]
    return running

def block_prep(x_block, bc_block, step_block, decay_rate, reset_at):
    block_len = step_block.shape[1]
    nstate = bc_block.shape[1] // 2
    position = jnp.arange(block_len, dtype=jnp.int32)
    segment = position >= reset_at
    cumulated = jnp.cumsum(-decay_rate[:, None] * step_block, axis=1)
    causal = (segment[:, None] == segment[None, :]) & (position[:, None] >= position[None, :])
    kernel = jnp.exp(jnp.where(causal[None], cumulated[:, :, None] - cumulated[:, None, :], -jnp.inf))
    entering = jnp.where(segment[None, :], 0.0, jnp.exp(cumulated))
    final_cum = cumulated[:, block_len - 1:]
    leaving = jnp.where(segment[None, :] == segment[block_len - 1], jnp.exp(final_cum - cumulated), 0.0)
    carry_out = jnp.where(reset_at >= block_len, jnp.exp(cumulated[:, block_len - 1]), 0.0)
    b_matrix = bc_block[:, :nstate]
    c_matrix = bc_block[:, nstate:]
    gram_mat = contract('tn,sn->ts', c_matrix, b_matrix)
    mixing = (gram_mat[None] * kernel).astype(jnp.bfloat16)
    x_float = x_block.astype(jnp.float32)
    scaled_x = (x_float * jnp.transpose(step_block)[:, :, None]).astype(jnp.bfloat16)
    leaving_x = (x_float * jnp.transpose(leaving * step_block)[:, :, None]).astype(jnp.bfloat16)
    return dict(kernel=kernel, entering=entering, leaving=leaving, carry_out=carry_out, b_matrix=b_matrix, c_matrix=c_matrix, gram_mat=gram_mat, mixing=mixing, scaled_x=scaled_x, leaving_x=leaving_x)

def block_state(prepared):
    return contract('shp,sn->hpn', prepared['leaving_x'], prepared['b_matrix'])

def block_out(prepared, x_block, d_skip, state_in):
    state_q = state_in.astype(jnp.bfloat16)
    intra = contract('hts,shp->thp', prepared['mixing'], prepared['scaled_x'])
    y_state = contract('tn,hpn->thp', prepared['c_matrix'], state_q)
    result = intra + jnp.transpose(prepared['entering'])[:, :, None] * y_state + d_skip[None, :, None] * x_block.astype(jnp.float32)
    return (result.astype(jnp.bfloat16), y_state)

def block_bsum(prepared, output_grad_block):
    enter_dy = (output_grad_block.astype(jnp.float32) * jnp.transpose(prepared['entering'])[:, :, None]).astype(jnp.bfloat16)
    return (enter_dy, contract('thp,tn->hpn', enter_dy, prepared['c_matrix']))

def block_back(prepared, x_block, output_grad_block, enter_dy, y_state, state_in, dstate, decay_rate, d_skip, step_block):
    block_len = step_block.shape[1]
    kernel = prepared['kernel']
    dstate_q = dstate.astype(jnp.bfloat16)
    state_q = state_in.astype(jnp.bfloat16)
    response = contract('thp,shp->hts', output_grad_block, prepared['scaled_x'])
    weighed = response * kernel
    z_term = weighed * prepared['gram_mat'][None]
    d_gram = lax.optimization_barrier(jnp.sum(weighed, axis=0))
    grad_c = contract_exact('ts,sn->tn', d_gram, prepared['b_matrix']) + contract('thp,hpn->tn', enter_dy, state_q)
    grad_b = contract_exact('ts,tn->sn', d_gram, prepared['c_matrix']) + contract('shp,hpn->sn', prepared['leaving_x'], dstate_q)
    d_scaled = contract('hts,thp->shp', prepared['mixing'], output_grad_block)
    d_leaving = contract('sn,hpn->shp', prepared['b_matrix'], dstate_q)
    x_float = x_block.astype(jnp.float32)
    step_t = jnp.transpose(step_block)
    leave_t = jnp.transpose(prepared['leaving'])
    grad_xc = step_t[:, :, None] * d_scaled + (leave_t * step_t)[:, :, None] * d_leaving + d_skip[None, :, None] * output_grad_block.astype(jnp.float32)
    along_dt = jnp.transpose(lax.optimization_barrier(jnp.sum(x_float * d_scaled, axis=2)))
    along_leave = jnp.transpose(lax.optimization_barrier(jnp.sum(x_float * d_leaving, axis=2)))
    leave_term = prepared['leaving'] * step_block * along_leave
    enter_term = prepared['entering'] * jnp.transpose(lax.optimization_barrier(jnp.sum(output_grad_block.astype(jnp.float32) * y_state, axis=2)))
    final_term = lax.optimization_barrier(jnp.sum(leave_term, axis=1)) + prepared['carry_out'] * lax.optimization_barrier(jnp.sum(dstate * state_in, axis=(1, 2)))
    is_final = jnp.arange(block_len, dtype=jnp.int32) == block_len - 1
    d_cum = lax.optimization_barrier(jnp.sum(z_term, axis=2)) - lax.optimization_barrier(jnp.sum(z_term, axis=1)) + enter_term - leave_term
    d_cum = d_cum + jnp.where(is_final[None, :], final_term[:, None], 0.0)
    d_log = lax.cumsum(d_cum, axis=1, reverse=True)
    grad_step = along_dt + prepared['leaving'] * along_leave - decay_rate[:, None] * d_log
    return (grad_b, grad_c, grad_xc, grad_step)

def reference(x_raw, bc_raw, conv_x_w, conv_bc_w, dt_raw, a_log, d_skip, doc_starts, grad_y):
    seq_len, channels = x_raw.shape
    head_count = a_log.shape[0]
    head_dim = channels // head_count
    nstate = bc_raw.shape[1] // 2
    rim_rows = conv_x_w.shape[0] - 1
    x_pre = causal_conv(x_raw, jnp.zeros((rim_rows, channels), x_raw.dtype), conv_x_w)
    bc_pre = causal_conv(bc_raw, jnp.zeros((rim_rows, 2 * nstate), bc_raw.dtype), conv_bc_w)
    x_conv = jax.nn.silu(x_pre).astype(jnp.bfloat16)
    bc_conv = jax.nn.silu(bc_pre).astype(jnp.bfloat16)
    step_size = jax.nn.softplus(dt_raw)
    decay_rate = jnp.exp(a_log)
    nblock = seq_len // BLOCK
    x_blocks = x_conv.reshape(nblock, BLOCK, head_count, head_dim)
    bc_blocks = bc_conv.reshape(nblock, BLOCK, 2 * nstate)
    step_blocks = jnp.transpose(step_size.reshape(head_count, nblock, BLOCK), (1, 0, 2))
    dy_blocks = grad_y.reshape(nblock, BLOCK, head_count, head_dim)
    zero_state = jnp.zeros((head_count, head_dim, nstate), jnp.float32)

    def forward_step(state_in, inputs):
        x_block, bc_block, step_block, reset_at = inputs
        prepared = block_prep(x_block, bc_block, step_block, decay_rate, reset_at)
        y_block, unused_state = block_out(prepared, x_block, d_skip, state_in)
        state_out = prepared['carry_out'][:, None, None] * state_in + block_state(prepared)
        return (state_out, (y_block, state_in))
    unused_final, (y_blocks, state_blocks) = lax.scan(forward_step, zero_state, (x_blocks, bc_blocks, step_blocks, doc_starts))

    def backward_step(dstate, inputs):
        x_block, bc_block, step_block, reset_at, output_grad_block, state_in = inputs
        prepared = block_prep(x_block, bc_block, step_block, decay_rate, reset_at)
        enter_dy, back_part = block_bsum(prepared, output_grad_block)
        unused_y, y_state = block_out(prepared, x_block, d_skip, state_in)
        grads = block_back(prepared, x_block, output_grad_block, enter_dy, y_state, state_in, dstate, decay_rate, d_skip, step_block)
        dstate_in = prepared['carry_out'][:, None, None] * dstate + back_part
        return (dstate_in, grads)
    unused_first, (grad_bs, grad_cs, filtered_input_cotangents, grad_steps) = lax.scan(backward_step, zero_state, (x_blocks, bc_blocks, step_blocks, doc_starts, dy_blocks, state_blocks), reverse=True)
    grad_bc = jnp.concatenate([grad_bs.reshape(seq_len, nstate), grad_cs.reshape(seq_len, nstate)], axis=1)
    grad_bc_pre = grad_bc * silu_grad(bc_pre)
    grad_x_pre = filtered_input_cotangents.reshape(seq_len, channels) * silu_grad(x_pre)
    grad_x_raw = conv_back(grad_x_pre, jnp.zeros((rim_rows, channels), jnp.float32), conv_x_w).astype(jnp.bfloat16)
    grad_bc_raw = conv_back(grad_bc_pre, jnp.zeros((rim_rows, 2 * nstate), jnp.float32), conv_bc_w).astype(jnp.bfloat16)
    grad_step = jnp.transpose(grad_steps, (1, 0, 2)).reshape(head_count, seq_len)
    grad_dt_raw = grad_step * jax.nn.sigmoid(dt_raw)
    y_out = y_blocks.reshape(seq_len, channels)
    return (y_out, grad_x_raw, grad_bc_raw, grad_dt_raw)
```

```python
import functools

import jax
import jax.numpy as jnp
from jax import lax
from jax.experimental import pallas as pl
from jax.experimental.pallas import tpu as pltpu
from jax.sharding import PartitionSpec as P

F32 = jnp.float32
BF16 = jnp.bfloat16
LANES = 128
RIM = 8
VMEM_LIMIT = 48 * 1024 * 1024
HIGHEST = lax.Precision.HIGHEST


def dot(a, b, dims, precision=None):
    return lax.dot_general(a, b, (dims, ((), ())), precision=precision, preferred_element_type=F32)


def iota(shape, axis):
    return lax.broadcasted_iota(jnp.int32, shape, axis)


def halves(values):
    high = values.astype(BF16)
    return high, (values - high.astype(F32)).astype(BF16)


def sigmoid(values):
    return 1.0 / (1.0 + jnp.exp(-values))


def spread(values, slab, head_dim):
    heads = values.shape[0]
    high, low = halves(values)
    both = jnp.concatenate([high, low], axis=0)
    row = iota((2 * heads, LANES), 0)
    head = iota((2 * heads, LANES), 1) // head_dim + slab * (LANES // head_dim)
    chosen = jnp.where((row == head) | (row == head + heads), 1.0, 0.0).astype(BF16)
    return dot(both, chosen, ((0,), (0,)))


def head_sum(values, slab, head_dim, heads):
    high, low = halves(values)
    both = jnp.concatenate([high, low], axis=1)
    head = (iota((heads, 2 * LANES), 1) % LANES) // head_dim + slab * (LANES // head_dim)
    chosen = jnp.where(iota((heads, 2 * LANES), 0) == head, 1.0, 0.0).astype(BF16)
    return dot(chosen, both, ((1,), (1,)))


def per_head(ref, heads, rows):
    at = iota((heads, rows), 0)
    values = jnp.zeros((heads, rows), F32)
    for head in range(heads):
        values = jnp.where(at == head, ref[head], values)
    return values


def head_values(doc_ref, a_log_ref, dt_ref):
    heads, rows = dt_ref.shape
    doc = doc_ref[0]
    raw = dt_ref[...]
    step = jnp.maximum(raw, 0.0) + jnp.log(1.0 + jnp.exp(-jnp.abs(raw)))
    decay = jnp.exp(per_head(a_log_ref, heads, rows))
    upto = jnp.where(iota((rows, rows), 0) <= iota((rows, rows), 1), 1.0, 0.0)
    drop = -decay * step
    cum = dot(drop, upto, ((1,), (0,)), HIGHEST)
    final = cum[:, rows - 1 :]
    segment = iota((heads, rows), 1) >= doc
    entering = jnp.where(segment, 0.0, jnp.exp(cum))
    outside = jnp.logical_and(iota((heads, rows), 1) < doc, doc < rows)
    leaving = jnp.where(outside, 0.0, jnp.exp(final - cum))
    carry = jnp.where(doc >= rows, jnp.exp(jnp.broadcast_to(final, (heads, rows))), 0.0)
    return dict(
        step=step, decay=decay, drop=drop, cum=cum, entering=entering, leaving=leaving, carry=carry
    )


def load_ext(ext, halo_ref, x_ref, bc_ref):
    channels = x_ref.shape[1]
    rows = x_ref.shape[0]
    ext[0:RIM, :] = halo_ref[...].astype(F32)
    ext[RIM : RIM + rows, 0:channels] = x_ref[...].astype(F32)
    ext[RIM : RIM + rows, channels:] = bc_ref[...].astype(F32)


def filtered(ext, w_ref, at, w_at, rows):
    taps = w_ref.shape[0]
    lanes = pl.ds(at, LANES)
    w = w_ref[:, w_at : w_at + LANES].astype(F32)
    total = w[0:1] * ext[pl.ds(RIM - taps + 1, rows), lanes]
    for tap in range(1, taps):
        total = total + w[tap : tap + 1] * ext[pl.ds(RIM - taps + 1 + tap, rows), lanes]
    return total


def send_kernel(
    head_dim, doc_ref, a_log_ref, x_ref, halo_ref, bc_ref, wx_ref, wbc_ref, dt_ref, dy_ref, send_ref, ext
):
    rows, channels = x_ref.shape
    heads = dt_ref.shape[0]
    part = channels // send_ref.shape[0]
    per_slab = LANES // part
    v = head_values(doc_ref, a_log_ref, dt_ref)
    load_ext(ext, halo_ref, x_ref, bc_ref)
    bc = []
    for half in range(2):
        pre = filtered(ext, wbc_ref, channels + half * LANES, half * LANES, rows)
        bc.append((pre * sigmoid(pre)).astype(BF16))
    leave_step = v["leaving"] * v["step"]
    for slab in range(channels // LANES):
        lanes = slice(slab * LANES, (slab + 1) * LANES)
        pre = filtered(ext, wx_ref, slab * LANES, slab * LANES, rows)
        x_conv = (pre * sigmoid(pre)).astype(BF16).astype(F32)
        leaving_x = (x_conv * spread(leave_step, slab, head_dim)).astype(BF16)
        enter_dy = (dy_ref[:, lanes].astype(F32) * spread(v["entering"], slab, head_dim)).astype(BF16)
        forward = dot(leaving_x, bc[0], ((0,), (0,))).astype(BF16)
        backward = dot(enter_dy, bc[1], ((0,), (0,))).astype(BF16)
        own = slice(slab * per_slab, (slab + 1) * per_slab)
        send_ref[own, 0:part, :] = forward.reshape(per_slab, part, LANES)
        send_ref[own, part : 2 * part, :] = backward.reshape(per_slab, part, LANES)
    high, low = halves(v["carry"][:, 0:LANES])
    at = iota((RIM, LANES), 0)
    for chunk in range(send_ref.shape[0]):
        head = chunk * part // head_dim
        tile = jnp.where(
            at == 0,
            high[head : head + 1].astype(F32),
            jnp.where(at == 1, low[head : head + 1].astype(F32), 0.0),
        )
        send_ref[chunk, 2 * part : 2 * part + RIM, :] = tile.astype(BF16)


def scan_kernel(got_ref, out_ref):
    count, width, lanes = out_ref.shape
    part = width // 2
    forward = jnp.zeros((part, lanes), F32)
    backward = jnp.zeros((part, lanes), F32)

    def carry(at):
        tail = got_ref[at, width : width + RIM, :].astype(F32)
        return tail[0:1] + tail[1:2]

    for at in range(count):
        out_ref[at, 0:part, :] = forward.astype(BF16)
        forward = carry(at) * forward + got_ref[at, 0:part, :].astype(F32)
        back = count - 1 - at
        out_ref[back, part : 2 * part, :] = backward.astype(BF16)
        backward = carry(back) * backward + got_ref[back, part : 2 * part, :].astype(F32)


def intra_kernel(
    head_dim,
    doc_ref,
    a_log_ref,
    skip_ref,
    x_ref,
    halo_ref,
    bc_ref,
    wx_ref,
    wbc_ref,
    dt_ref,
    dy_ref,
    xc_ref,
    lx_ref,
    edy_ref,
    bcc_ref,
    yi_ref,
    gs_ref,
    ls_ref,
    gbc_ref,
    sbc_ref,
    hv_ref,
    ext,
    bias,
    dgram,
):
    rows, channels = x_ref.shape
    heads = dt_ref.shape[0]
    doc = doc_ref[0]
    v = head_values(doc_ref, a_log_ref, dt_ref)
    load_ext(ext, halo_ref, x_ref, bc_ref)
    for half in range(2):
        lanes = slice(half * LANES, (half + 1) * LANES)
        pre = filtered(ext, wbc_ref, channels + half * LANES, half * LANES, rows)
        gate = sigmoid(pre)
        bcc_ref[:, lanes] = (pre * gate).astype(BF16)
        sbc_ref[:, lanes] = gate * (1.0 + pre * (1.0 - gate))
    b_matrix = bcc_ref[:, 0:LANES]
    c_matrix = bcc_ref[:, LANES:]
    gram = dot(c_matrix, b_matrix, ((1,), (1,)))
    t_at, s_at = iota((rows, rows), 0), iota((rows, rows), 1)
    bias[...] = jnp.where((t_at >= s_at) & ((t_at >= doc) == (s_at >= doc)), 0.0, -1e30)
    dgram[...] = jnp.zeros_like(dgram)
    downto = jnp.where(t_at >= s_at, 1.0, 0.0)
    cum = v["cum"]
    cum_t = dot(downto, v["drop"], ((1,), (1,)), HIGHEST)
    skip = per_head(skip_ref, heads, rows)
    leave_step = v["leaving"] * v["step"]
    along_dt = jnp.zeros((heads, rows), F32)
    z_diff = jnp.zeros((heads, rows), F32)
    low_half = iota((rows, LANES), 1) < head_dim
    for slab in range(channels // LANES):
        lanes = slice(slab * LANES, (slab + 1) * LANES)
        pre = filtered(ext, wx_ref, slab * LANES, slab * LANES, rows)
        gate = sigmoid(pre)
        x_bf = (pre * gate).astype(BF16)
        silu_grad = gate * (1.0 + pre * (1.0 - gate))
        x_conv = x_bf.astype(F32)
        xc_ref[:, lanes] = x_bf
        step = spread(v["step"], slab, head_dim)
        leave = spread(leave_step, slab, head_dim)
        enter = spread(v["entering"], slab, head_dim)
        skips = spread(skip, slab, head_dim)
        dy_bf = dy_ref[:, lanes]
        dy = dy_bf.astype(F32)
        lx_ref[:, lanes] = (x_conv * leave).astype(BF16)
        edy_ref[:, lanes] = (dy * enter).astype(BF16)
        scaled = (x_conv * step).astype(BF16)
        intra = jnp.zeros((rows, LANES), F32)
        d_scaled = jnp.zeros((rows, LANES), F32)
        for side in range(LANES // head_dim):
            head = slab * (LANES // head_dim) + side
            mine = low_half if side == 0 else jnp.logical_not(low_half)
            scaled_h = jnp.where(mine, scaled.astype(F32), 0.0).astype(BF16)
            dy_h = jnp.where(mine, dy, 0.0).astype(BF16)
            kernel = jnp.exp((cum_t[:, head : head + 1] - cum[head : head + 1, :]) + bias[...])
            mixing = (gram * kernel).astype(BF16)
            response = dot(dy_h, scaled, ((1,), (1,)))
            dgram[...] += response * kernel
            intra = intra + dot(mixing, scaled_h, ((1,), (0,)))
            d_scaled = d_scaled + dot(mixing, dy_h, ((0,), (0,)))
        yi_ref[:, lanes] = intra + skips * x_conv
        gs_ref[:, lanes] = (step * d_scaled + skips * dy) * silu_grad
        ls_ref[:, lanes] = leave * silu_grad
        along_dt = along_dt + head_sum(x_conv * d_scaled, slab, head_dim, heads)
        z_diff = z_diff + head_sum(
            dy * intra - scaled.astype(F32) * d_scaled, slab, head_dim, heads
        )
    d_gram = dgram[...]
    gbc_ref[:, 0:LANES] = dot(d_gram, c_matrix.astype(F32), ((0,), (0,)), HIGHEST)
    gbc_ref[:, LANES:] = dot(d_gram, b_matrix.astype(F32), ((1,), (0,)), HIGHEST)
    small = [
        leave_step,
        v["leaving"],
        v["entering"],
        along_dt,
        z_diff,
        v["carry"],
        v["decay"],
        sigmoid(dt_ref[...]),
    ]
    for at, values in enumerate(small):
        hv_ref[at] = values


def state_of(st_ref, which):
    count, width, lanes = st_ref.shape
    part = width // 2
    return st_ref[:, which * part : (which + 1) * part, :].reshape(count * part, lanes)


def bc_kernel(
    core_ref, st_ref, lx_ref, edy_ref, b_ref, gbc_ref, sbc_ref, gs_ref, ls_ref, wbc_ref,
    keep_ref, give_ref, halo_ref, ext, total,
):
    rows = lx_ref.shape[0]
    taps = wbc_ref.shape[0]
    channels = lx_ref.shape[1]
    state, dstate = state_of(st_ref, 0), state_of(st_ref, 1)
    grad_b = gbc_ref[:, 0:LANES] + dot(lx_ref[...], dstate, ((1,), (0,)))
    grad_c = gbc_ref[:, LANES:] + dot(edy_ref[...], state, ((1,), (0,)))
    ext[0:rows, 0:LANES] = grad_b * sbc_ref[:, 0:LANES]
    ext[0:rows, LANES:] = grad_c * sbc_ref[:, LANES:]
    ext[rows:, :] = jnp.zeros((RIM, 2 * LANES), F32)
    w = wbc_ref[...].astype(F32)
    out = w[taps - 1 : taps] * ext[0:rows, :]
    for tap in range(taps - 1):
        out = out + w[tap : tap + 1] * ext[pl.ds(taps - 1 - tap, rows), :]
    total[...] = out
    half = rows // 2
    core = core_ref[0]
    keep_ref[...] = total[pl.ds(pl.multiple_of(core * half, half), half), :]
    give_ref[...] = total[pl.ds(pl.multiple_of((1 - core) * half, half), half), :].astype(BF16)
    d_leaving = dot(b_ref[...], dstate, ((1,), (1,)))[0:RIM]
    halo_ref[:, 0:channels] = gs_ref[...] + ls_ref[...] * d_leaving
    halo_ref[:, channels:] = ext[0:RIM, :]


def join_kernel(keep_ref, got_ref, halo_ref, wbc_ref, out_ref, ext):
    half = keep_ref.shape[0]
    taps = wbc_ref.shape[0]
    wide = keep_ref.shape[1]
    channels = halo_ref.shape[1] - wide
    out_ref[0:half, :] = (keep_ref[...] + got_ref[...].astype(F32)).astype(BF16)
    ext[0:RIM, :] = jnp.zeros((RIM, wide), F32)
    ext[RIM:, :] = halo_ref[:, channels:]
    w = wbc_ref[...].astype(F32)
    rim = jnp.zeros((RIM, wide), F32)
    for tap in range(taps - 1):
        rim = rim + w[tap : tap + 1] * ext[pl.ds(taps - 1 - tap, RIM), :]
    out_ref[half:, :] = rim.astype(BF16)


def sum_kernel(*refs):
    out_ref = refs[-1]
    total = refs[0][...].astype(F32)
    for ref in refs[1:-1]:
        total = total + ref[...].astype(F32)
    out_ref[...] = total.astype(BF16)


def last_kernel(core_ref, mine_ref, got_ref, out_ref, total):
    rows = out_ref.shape[0]
    half = rows // 2
    core = core_ref[0]
    total[pl.ds(pl.multiple_of(core * half, half), half), :] = mine_ref[0:half, :].astype(F32)
    total[pl.ds(pl.multiple_of((1 - core) * half, half), half), :] = got_ref[0:half, :].astype(F32)
    total[rows - RIM :, :] += mine_ref[half:, :].astype(F32) + got_ref[half:, :].astype(F32)
    out_ref[...] = total[...].astype(BF16)


def out_kernel(
    head_dim, st_ref, xc_ref, dy_ref, bcc_ref, yi_ref, gs_ref, ls_ref, hv_ref, halo_ref, wx_ref,
    y_ref, gx_ref, gdt_ref, ext,
):
    rows, channels = xc_ref.shape
    heads = hv_ref.shape[1]
    taps = wx_ref.shape[0]
    state, dstate = state_of(st_ref, 0), state_of(st_ref, 1)
    b_matrix, c_matrix = bcc_ref[:, 0:LANES], bcc_ref[:, LANES:]
    leave_step, leaving, entering, along_dt, z_diff, carry, decay, dt_gate = [
        hv_ref[at] for at in range(8)
    ]
    along_leave = jnp.zeros((heads, rows), F32)
    along_enter = jnp.zeros((heads, rows), F32)
    ext[rows:, :] = halo_ref[:, 0:channels]
    for slab in range(channels // LANES):
        lanes = slice(slab * LANES, (slab + 1) * LANES)
        y_state = dot(c_matrix, state[lanes], ((1,), (1,)))
        d_leaving = dot(b_matrix, dstate[lanes], ((1,), (1,)))
        y_ref[:, lanes] = (yi_ref[:, lanes] + spread(entering, slab, head_dim) * y_state).astype(BF16)
        along_leave = along_leave + head_sum(
            xc_ref[:, lanes].astype(F32) * d_leaving, slab, head_dim, heads
        )
        along_enter = along_enter + head_sum(
            dy_ref[:, lanes].astype(F32) * y_state, slab, head_dim, heads
        )
        ext[0:rows, lanes] = gs_ref[:, lanes] + ls_ref[:, lanes] * d_leaving
        w = wx_ref[:, lanes].astype(F32)
        out = w[taps - 1 : taps] * ext[0:rows, lanes]
        for tap in range(taps - 1):
            out = out + w[tap : tap + 1] * ext[pl.ds(taps - 1 - tap, rows), lanes]
        gx_ref[:, lanes] = out.astype(BF16)
    product = state.astype(F32) * dstate.astype(F32)
    owner = iota((heads, channels), 1) // head_dim
    chosen = jnp.where(iota((heads, channels), 0) == owner, 1.0, 0.0)
    overlap = jnp.sum(dot(chosen, product, ((1,), (0,)), HIGHEST), axis=1, keepdims=True)
    leave_term = leave_step * along_leave
    final = jnp.sum(leave_term, axis=1, keepdims=True) + carry * overlap
    d_cum = z_diff + entering * along_enter - leave_term
    d_cum = d_cum + jnp.where(iota((heads, rows), 1) == rows - 1, final, 0.0)
    after = jnp.where(iota((rows, rows), 0) >= iota((rows, rows), 1), 1.0, 0.0)
    d_log = dot(d_cum, after, ((1,), (0,)), HIGHEST)
    gdt_ref[...] = (along_dt + leaving * along_leave - decay * d_log) * dt_gate


def smem():
    return pl.BlockSpec(memory_space=pltpu.SMEM)


def whole(shape):
    return pl.BlockSpec(shape, lambda i: (0,) * len(shape))


def call(kernel, name, out, scalars, arrays, scratch=(), blocks=None):
    blocks = blocks or {}
    many = isinstance(out, list)
    out = [jax.ShapeDtypeStruct(s, d) for s, d in (out if many else [out])]
    specs = [whole(o.shape) for o in out]
    return pl.pallas_call(
        kernel,
        name=name,
        out_shape=out if many else out[0],
        grid=(1,),
        in_specs=[smem() for _ in scalars]
        + [whole(blocks.get(i, a.shape)) for i, a in enumerate(arrays)],
        out_specs=specs if many else specs[0],
        scratch_shapes=list(scratch),
        compiler_params=pltpu.CompilerParams(vmem_limit_bytes=VMEM_LIMIT),
    )(*scalars, *arrays)


def shift_ctx(values, by):
    size = lax.axis_size("ctx")
    pairs = [(i, i + by) for i in range(size) if 0 <= i + by < size]
    return lax.ppermute(values, "ctx", pairs)


def swap_core(values):
    size = lax.axis_size("head")
    return lax.ppermute(values, "head", [(i, i ^ 1) for i in range(size)])


def around(values, by):
    size = lax.axis_size("head")
    return lax.ppermute(values, "head", [(i, (i + 2 * by) % size) for i in range(size)])


def body(x_raw, bc_raw, conv_x_w, conv_bc_w, dt_raw, a_log, d_skip, doc_starts, grad_y):
    rows, channels = x_raw.shape
    heads = a_log.shape[0]
    head_dim = channels // heads
    wide = bc_raw.shape[1]
    count = lax.axis_size("ctx")
    part = channels // count
    core = (lax.axis_index("head") % 2).astype(jnp.int32).reshape(1)
    halo = shift_ctx(jnp.concatenate([x_raw[rows - RIM :], bc_raw[rows - RIM :]], axis=1), 1)
    ext = pltpu.VMEM((rows + RIM, channels + wide), F32)
    send = call(
        functools.partial(send_kernel, head_dim),
        "send",
        ((count, 2 * part + RIM, LANES), BF16),
        [doc_starts, a_log],
        [x_raw, halo, bc_raw, conv_x_w, conv_bc_w, dt_raw, grad_y],
        [ext],
    )
    got = lax.all_to_all(send, "ctx", 0, 0)
    xc, lx, edy, bcc, yi, gs, ls, gbc, sbc, hv = call(
        functools.partial(intra_kernel, head_dim),
        "intra",
        [
            ((rows, channels), BF16),
            ((rows, channels), BF16),
            ((rows, channels), BF16),
            ((rows, wide), BF16),
            ((rows, channels), F32),
            ((rows, channels), F32),
            ((rows, channels), F32),
            ((rows, wide), F32),
            ((rows, wide), F32),
            ((8, heads, rows), F32),
        ],
        [doc_starts, a_log, d_skip],
        [x_raw, halo, bc_raw, conv_x_w, conv_bc_w, dt_raw, grad_y],
        [ext, pltpu.VMEM((rows, rows), F32), pltpu.VMEM((rows, rows), F32)],
    )
    scanned = call(scan_kernel, "scan", ((count, 2 * part, LANES), BF16), [], [got])
    st = lax.all_to_all(scanned, "ctx", 0, 0)
    half = rows // 2
    keep, give, rim = call(
        bc_kernel,
        "grad_bc",
        [((half, wide), F32), ((half, wide), BF16), ((RIM, channels + wide), F32)],
        [core],
        [st, lx, edy, bcc, gbc, sbc, gs, ls, conv_bc_w],
        [pltpu.VMEM((rows + RIM, wide), F32), pltpu.VMEM((rows, wide), F32)],
        {3: (2 * RIM, LANES), 6: (RIM, channels), 7: (RIM, channels)},
    )
    next_rim = shift_ctx(rim, -1)
    other = swap_core(give)
    joined = call(
        join_kernel,
        "join",
        ((half + RIM, wide), BF16),
        [],
        [keep, other, next_rim, conv_bc_w],
        [pltpu.VMEM((2 * RIM, wide), F32)],
    )
    ring = lax.axis_size("head") // 2
    pieces = [joined] + [around(joined, by) for by in range(1, ring)]
    y_out, grad_x, grad_dt = call(
        functools.partial(out_kernel, head_dim),
        "out",
        [((rows, channels), BF16), ((rows, channels), BF16), ((heads, rows), F32)],
        [],
        [st, xc, grad_y, bcc, yi, gs, ls, hv, next_rim, conv_x_w],
        [pltpu.VMEM((rows + RIM, channels), F32)],
    )
    summed = call(sum_kernel, "sum", ((half + RIM, wide), BF16), [], pieces)
    swapped = swap_core(summed)
    grad_bc = call(
        last_kernel,
        "last",
        ((rows, wide), BF16),
        [core],
        [summed, swapped],
        [pltpu.VMEM((rows, wide), F32)],
    )
    return (y_out, grad_x, grad_bc, grad_dt)


def solution(mesh):
    in_specs = (
        P("ctx", "head"),
        P("ctx", None),
        P(None, "head"),
        P(),
        P("head", "ctx"),
        P("head"),
        P("head"),
        P("ctx"),
        P("ctx", "head"),
    )
    out_specs = (P("ctx", "head"), P("ctx", "head"), P("ctx", None), P("head", "ctx"))
    return jax.shard_map(body, mesh=mesh, in_specs=in_specs, out_specs=out_specs, check_vma=False)
```

```python
import functools

import jax
import jax.numpy as jnp
from jax import lax
from jax.experimental import pallas as pl
from jax.experimental.pallas import tpu as pltpu
from jax.sharding import PartitionSpec as P

F32 = jnp.float32
BF16 = jnp.bfloat16
LANES = 128
RIM = 8
VMEM_LIMIT = 24 * 1024 * 1024
HIGHEST = lax.Precision.HIGHEST


def dot(a, b, dims, precision=None):
    return lax.dot_general(a, b, (dims, ((), ())), precision=precision, preferred_element_type=F32)


def iota(shape, axis):
    return lax.broadcasted_iota(jnp.int32, shape, axis)


def halves(values):
    high = values.astype(BF16)
    return high, (values - high.astype(F32)).astype(BF16)


def sigmoid(values):
    return 1.0 / (1.0 + jnp.exp(-values))


def spread(values, slab, head_dim):
    heads = values.shape[0]
    high, low = halves(values)
    both = jnp.concatenate([high, low], axis=0)
    row = iota((2 * heads, LANES), 0)
    head = iota((2 * heads, LANES), 1) // head_dim + slab * (LANES // head_dim)
    chosen = jnp.where((row == head) | (row == head + heads), 1.0, 0.0).astype(BF16)
    return dot(both, chosen, ((0,), (0,)))


def head_sum(values, slab, head_dim, heads):
    high, low = halves(values)
    both = jnp.concatenate([high, low], axis=1)
    head = (iota((heads, 2 * LANES), 1) % LANES) // head_dim + slab * (LANES // head_dim)
    chosen = jnp.where(iota((heads, 2 * LANES), 0) == head, 1.0, 0.0).astype(BF16)
    return dot(chosen, both, ((1,), (1,)))


def per_head(ref, heads, rows):
    at = iota((heads, rows), 0)
    values = jnp.zeros((heads, rows), F32)
    for head in range(heads):
        values = jnp.where(at == head, ref[head], values)
    return values


def head_values(doc_ref, a_log_ref, dt_ref):
    heads, rows = dt_ref.shape
    doc = doc_ref[0]
    raw = dt_ref[...]
    step = jnp.maximum(raw, 0.0) + jnp.log(1.0 + jnp.exp(-jnp.abs(raw)))
    decay = jnp.exp(per_head(a_log_ref, heads, rows))
    upto = jnp.where(iota((rows, rows), 0) <= iota((rows, rows), 1), 1.0, 0.0)
    drop = -decay * step
    cum = dot(drop, upto, ((1,), (0,)), HIGHEST)
    final = cum[:, rows - 1 :]
    segment = iota((heads, rows), 1) >= doc
    entering = jnp.where(segment, 0.0, jnp.exp(cum))
    outside = jnp.logical_and(iota((heads, rows), 1) < doc, doc < rows)
    leaving = jnp.where(outside, 0.0, jnp.exp(final - cum))
    carry = jnp.where(doc >= rows, jnp.exp(jnp.broadcast_to(final, (heads, rows))), 0.0)
    return dict(
        step=step, decay=decay, drop=drop, cum=cum, entering=entering, leaving=leaving, carry=carry
    )


def lanes_of(slab):
    return slice(slab * LANES, (slab + 1) * LANES)


def fetch(source, target, sems):
    copies = []
    for slab in range(source.shape[1] // LANES):
        part = (slice(None), lanes_of(slab))
        copies.append(pltpu.make_async_copy(source.at[part], target.at[part], sems.at[slab]))
        copies[-1].start()
    return copies


def put(source, target, sem, at):
    copy = pltpu.make_async_copy(source.at[at], target.at[at], sem)
    copy.start()
    return copy


def load_ext(ext, halo_ref, values, at, lanes):
    ext[0:RIM, at] = halo_ref[:, at].astype(F32)
    ext[RIM : RIM + values.shape[0], at] = values[:, lanes].astype(F32)


def filtered(ext, w_ref, at, w_at, rows):
    taps = w_ref.shape[0]
    lanes = pl.ds(at, LANES)
    w = w_ref[:, w_at : w_at + LANES].astype(F32)
    total = w[0:1] * ext[pl.ds(RIM - taps + 1, rows), lanes]
    for tap in range(1, taps):
        total = total + w[tap : tap + 1] * ext[pl.ds(RIM - taps + 1 + tap, rows), lanes]
    return total


def send_kernel(
    head_dim, doc_ref, a_log_ref, x_hbm, dy_hbm, bc_hbm, halo_ref, wx_ref, wbc_ref, dt_ref,
    send_hbm, x_ref, dy_ref, bc_ref, send_ref, ext, x_sems, dy_sems, bc_sems, out_sems,
):
    rows, channels = x_ref.shape
    part = channels // send_ref.shape[0]
    per_slab = LANES // part
    bc_in = fetch(bc_hbm, bc_ref, bc_sems)
    x_in = fetch(x_hbm, x_ref, x_sems)
    dy_in = fetch(dy_hbm, dy_ref, dy_sems)
    v = head_values(doc_ref, a_log_ref, dt_ref)
    leave_step = v["leaving"] * v["step"]
    high, low = halves(v["carry"][:, 0:LANES])
    at = iota((RIM, LANES), 0)
    bc = []
    for half in range(2):
        bc_in[half].wait()
        load_ext(ext, halo_ref, bc_ref, lanes_of(channels // LANES + half), lanes_of(half))
        pre = filtered(ext, wbc_ref, channels + half * LANES, half * LANES, rows)
        bc.append((pre * sigmoid(pre)).astype(BF16))
    sent = []
    for slab in range(channels // LANES):
        lanes = lanes_of(slab)
        x_in[slab].wait()
        load_ext(ext, halo_ref, x_ref, lanes, lanes)
        pre = filtered(ext, wx_ref, slab * LANES, slab * LANES, rows)
        x_conv = (pre * sigmoid(pre)).astype(BF16).astype(F32)
        leaving_x = (x_conv * spread(leave_step, slab, head_dim)).astype(BF16)
        dy_in[slab].wait()
        enter_dy = (dy_ref[:, lanes].astype(F32) * spread(v["entering"], slab, head_dim)).astype(BF16)
        forward = dot(leaving_x, bc[0], ((0,), (0,))).astype(BF16)
        backward = dot(enter_dy, bc[1], ((0,), (0,))).astype(BF16)
        own = slice(slab * per_slab, (slab + 1) * per_slab)
        send_ref[own, 0:part, :] = forward.reshape(per_slab, part, LANES)
        send_ref[own, part : 2 * part, :] = backward.reshape(per_slab, part, LANES)
        for chunk in range(slab * per_slab, (slab + 1) * per_slab):
            head = chunk * part // head_dim
            tile = jnp.where(
                at == 0,
                high[head : head + 1].astype(F32),
                jnp.where(at == 1, low[head : head + 1].astype(F32), 0.0),
            )
            send_ref[chunk, 2 * part : 2 * part + RIM, :] = tile.astype(BF16)
        sent.append(put(send_ref, send_hbm, out_sems.at[slab], (own,)))
    for copy in sent:
        copy.wait()


def scan_kernel(got_ref, out_hbm, out_ref, sems):
    count, width, lanes = out_ref.shape
    part = width // 2
    forward = jnp.zeros((part, lanes), F32)
    backward = jnp.zeros((part, lanes), F32)

    def carry(at):
        tail = got_ref[at, width : width + RIM, :].astype(F32)
        return tail[0:1] + tail[1:2]

    sent = []
    for at in range(count):
        out_ref[at, 0:part, :] = forward.astype(BF16)
        forward = carry(at) * forward + got_ref[at, 0:part, :].astype(F32)
        back = count - 1 - at
        out_ref[back, part : 2 * part, :] = backward.astype(BF16)
        backward = carry(back) * backward + got_ref[back, part : 2 * part, :].astype(F32)
        low, high = min(at, back), max(at, back)
        if at >= count // 2 and (at + 1) % 4 == 0:
            sent.append(put(out_ref, out_hbm, sems.at[len(sent)], (slice(high - 3, high + 1),)))
            sent.append(put(out_ref, out_hbm, sems.at[len(sent)], (slice(low, low + 4),)))
    for copy in sent:
        copy.wait()


def intra_kernel(
    head_dim, doc_ref, a_log_ref, skip_ref, x_hbm, dy_hbm, bc_hbm, halo_ref, wx_ref, wbc_ref, dt_ref,
    xc_hbm, yi_hbm, gs_hbm, ls_hbm,
    lx_ref, edy_ref, bcc_ref, gbc_ref, sbc_ref, hv_ref, rim_ref,
    x_ref, dy_ref, bc_ref, xc_ref, yi_ref, gs_ref, ls_ref, ext, bias, dgram,
    x_sems, dy_sems, bc_sems, out_sems,
):
    rows, channels = x_ref.shape
    heads = dt_ref.shape[0]
    doc = doc_ref[0]
    bc_in = fetch(bc_hbm, bc_ref, bc_sems)
    x_in = fetch(x_hbm, x_ref, x_sems)
    dy_in = fetch(dy_hbm, dy_ref, dy_sems)
    v = head_values(doc_ref, a_log_ref, dt_ref)
    for half in range(2):
        lanes = lanes_of(half)
        bc_in[half].wait()
        load_ext(ext, halo_ref, bc_ref, lanes_of(channels // LANES + half), lanes)
        pre = filtered(ext, wbc_ref, channels + half * LANES, half * LANES, rows)
        gate = sigmoid(pre)
        bcc_ref[:, lanes] = (pre * gate).astype(BF16)
        sbc_ref[:, lanes] = gate * (1.0 + pre * (1.0 - gate))
    b_matrix = bcc_ref[:, 0:LANES]
    c_matrix = bcc_ref[:, LANES:]
    gram = dot(c_matrix, b_matrix, ((1,), (1,)))
    t_at, s_at = iota((rows, rows), 0), iota((rows, rows), 1)
    bias[...] = jnp.where((t_at >= s_at) & ((t_at >= doc) == (s_at >= doc)), 0.0, -1e30)
    dgram[...] = jnp.zeros_like(dgram)
    downto = jnp.where(t_at >= s_at, 1.0, 0.0)
    cum = v["cum"]
    cum_t = dot(downto, v["drop"], ((1,), (1,)), HIGHEST)
    skip = per_head(skip_ref, heads, rows)
    leave_step = v["leaving"] * v["step"]
    along_dt = jnp.zeros((heads, rows), F32)
    z_diff = jnp.zeros((heads, rows), F32)
    low_half = iota((rows, LANES), 1) < head_dim
    sent = []
    for slab in range(channels // LANES):
        lanes = lanes_of(slab)
        x_in[slab].wait()
        load_ext(ext, halo_ref, x_ref, lanes, lanes)
        dy_in[slab].wait()
        pre = filtered(ext, wx_ref, slab * LANES, slab * LANES, rows)
        gate = sigmoid(pre)
        x_bf = (pre * gate).astype(BF16)
        silu_grad = gate * (1.0 + pre * (1.0 - gate))
        x_conv = x_bf.astype(F32)
        xc_ref[:, lanes] = x_bf
        step = spread(v["step"], slab, head_dim)
        leave = spread(leave_step, slab, head_dim)
        enter = spread(v["entering"], slab, head_dim)
        skips = spread(skip, slab, head_dim)
        dy_bf = dy_ref[:, lanes]
        dy = dy_bf.astype(F32)
        lx_ref[:, lanes] = (x_conv * leave).astype(BF16)
        edy_ref[:, lanes] = (dy * enter).astype(BF16)
        scaled = (x_conv * step).astype(BF16)
        intra = jnp.zeros((rows, LANES), F32)
        d_scaled = jnp.zeros((rows, LANES), F32)
        for side in range(LANES // head_dim):
            head = slab * (LANES // head_dim) + side
            mine = low_half if side == 0 else jnp.logical_not(low_half)
            scaled_h = jnp.where(mine, scaled.astype(F32), 0.0).astype(BF16)
            dy_h = jnp.where(mine, dy, 0.0).astype(BF16)
            kernel = jnp.exp((cum_t[:, head : head + 1] - cum[head : head + 1, :]) + bias[...])
            mixing = (gram * kernel).astype(BF16)
            response = dot(dy_h, scaled, ((1,), (1,)))
            dgram[...] += response * kernel
            intra = intra + dot(mixing, scaled_h, ((1,), (0,)))
            d_scaled = d_scaled + dot(mixing, dy_h, ((0,), (0,)))
        yi_ref[:, lanes] = intra + skips * x_conv
        gs_ref[:, lanes] = (step * d_scaled + skips * dy) * silu_grad
        ls_ref[:, lanes] = leave * silu_grad
        rim_ref[0, :, lanes] = gs_ref[0:RIM, lanes]
        rim_ref[1, :, lanes] = ls_ref[0:RIM, lanes]
        at = (slice(None), lanes)
        for which, (mine, out) in enumerate(
            ((xc_ref, xc_hbm), (yi_ref, yi_hbm), (gs_ref, gs_hbm), (ls_ref, ls_hbm))
        ):
            sent.append(put(mine, out, out_sems.at[slab * 4 + which], at))
        along_dt = along_dt + head_sum(x_conv * d_scaled, slab, head_dim, heads)
        z_diff = z_diff + head_sum(
            dy * intra - scaled.astype(F32) * d_scaled, slab, head_dim, heads
        )
    d_gram = dgram[...]
    gbc_ref[:, 0:LANES] = dot(d_gram, c_matrix.astype(F32), ((0,), (0,)), HIGHEST)
    gbc_ref[:, LANES:] = dot(d_gram, b_matrix.astype(F32), ((1,), (0,)), HIGHEST)
    small = [
        leave_step,
        v["leaving"],
        v["entering"],
        along_dt,
        z_diff,
        v["carry"],
        v["decay"],
        sigmoid(dt_ref[...]),
    ]
    for at, values in enumerate(small):
        hv_ref[at] = values
    for copy in sent:
        copy.wait()


def state_of(st_ref, which):
    count, width, lanes = st_ref.shape
    part = width // 2
    return st_ref[:, which * part : (which + 1) * part, :].reshape(count * part, lanes)


def bc_kernel(
    core_ref, st_ref, lx_ref, edy_ref, b_ref, gbc_ref, sbc_ref, rim_ref, wbc_ref,
    keep_ref, give_ref, halo_ref, ext, total,
):
    rows = lx_ref.shape[0]
    taps = wbc_ref.shape[0]
    channels = lx_ref.shape[1]
    state, dstate = state_of(st_ref, 0), state_of(st_ref, 1)
    grad_b = gbc_ref[:, 0:LANES] + dot(lx_ref[...], dstate, ((1,), (0,)))
    grad_c = gbc_ref[:, LANES:] + dot(edy_ref[...], state, ((1,), (0,)))
    ext[0:rows, 0:LANES] = grad_b * sbc_ref[:, 0:LANES]
    ext[0:rows, LANES:] = grad_c * sbc_ref[:, LANES:]
    ext[rows:, :] = jnp.zeros((RIM, 2 * LANES), F32)
    w = wbc_ref[...].astype(F32)
    out = w[taps - 1 : taps] * ext[0:rows, :]
    for tap in range(taps - 1):
        out = out + w[tap : tap + 1] * ext[pl.ds(taps - 1 - tap, rows), :]
    total[...] = out
    half = rows // 2
    core = core_ref[0]
    keep_ref[...] = total[pl.ds(pl.multiple_of(core * half, half), half), :]
    give_ref[...] = total[pl.ds(pl.multiple_of((1 - core) * half, half), half), :].astype(BF16)
    d_leaving = dot(b_ref[0 : 2 * RIM, 0:LANES], dstate, ((1,), (1,)))[0:RIM]
    halo_ref[:, 0:channels] = rim_ref[0] + rim_ref[1] * d_leaving
    halo_ref[:, channels:] = ext[0:RIM, :]


def join_kernel(keep_ref, got_ref, halo_ref, wbc_ref, out_ref, ext):
    half = keep_ref.shape[0]
    taps = wbc_ref.shape[0]
    wide = keep_ref.shape[1]
    channels = halo_ref.shape[1] - wide
    out_ref[0:half, :] = (keep_ref[...] + got_ref[...].astype(F32)).astype(BF16)
    ext[0:RIM, :] = jnp.zeros((RIM, wide), F32)
    ext[RIM:, :] = halo_ref[:, channels:]
    w = wbc_ref[...].astype(F32)
    rim = jnp.zeros((RIM, wide), F32)
    for tap in range(taps - 1):
        rim = rim + w[tap : tap + 1] * ext[pl.ds(taps - 1 - tap, RIM), :]
    out_ref[half:, :] = rim.astype(BF16)


def sum_kernel(*refs):
    out_ref = refs[-1]
    total = refs[0][...].astype(F32)
    for ref in refs[1:-1]:
        total = total + ref[...].astype(F32)
    out_ref[...] = total.astype(BF16)


def last_kernel(core_ref, mine_ref, got_ref, out_ref, total):
    rows = out_ref.shape[0]
    half = rows // 2
    core = core_ref[0]
    total[pl.ds(pl.multiple_of(core * half, half), half), :] = mine_ref[0:half, :].astype(F32)
    total[pl.ds(pl.multiple_of((1 - core) * half, half), half), :] = got_ref[0:half, :].astype(F32)
    total[rows - RIM :, :] += mine_ref[half:, :].astype(F32) + got_ref[half:, :].astype(F32)
    out_ref[...] = total[...].astype(BF16)


def out_kernel(
    head_dim, xc_hbm, dy_hbm, yi_hbm, gs_hbm, ls_hbm, st_ref, bcc_ref, hv_ref, halo_ref, wx_ref,
    y_hbm, gx_hbm, gdt_ref,
    xc_ref, dy_ref, yi_ref, gs_ref, ls_ref, y_ref, gx_ref, ext,
    xc_sems, dy_sems, yi_sems, gs_sems, ls_sems, out_sems,
):
    rows, channels = xc_ref.shape
    heads = hv_ref.shape[1]
    taps = wx_ref.shape[0]
    yi_in = fetch(yi_hbm, yi_ref, yi_sems)
    gs_in = fetch(gs_hbm, gs_ref, gs_sems)
    ls_in = fetch(ls_hbm, ls_ref, ls_sems)
    xc_in = fetch(xc_hbm, xc_ref, xc_sems)
    dy_in = fetch(dy_hbm, dy_ref, dy_sems)
    state, dstate = state_of(st_ref, 0), state_of(st_ref, 1)
    b_matrix, c_matrix = bcc_ref[:, 0:LANES], bcc_ref[:, LANES:]
    leave_step, leaving, entering, along_dt, z_diff, carry, decay, dt_gate = [
        hv_ref[at] for at in range(8)
    ]
    along_leave = jnp.zeros((heads, rows), F32)
    along_enter = jnp.zeros((heads, rows), F32)
    ext[rows:, :] = halo_ref[:, 0:channels]
    sent = []
    for slab in range(channels // LANES):
        lanes = lanes_of(slab)
        at = (slice(None), lanes)
        y_state = dot(c_matrix, state[lanes], ((1,), (1,)))
        d_leaving = dot(b_matrix, dstate[lanes], ((1,), (1,)))
        yi_in[slab].wait()
        y_ref[at] = (yi_ref[at] + spread(entering, slab, head_dim) * y_state).astype(BF16)
        sent.append(put(y_ref, y_hbm, out_sems.at[2 * slab], at))
        gs_in[slab].wait()
        ls_in[slab].wait()
        ext[0:rows, lanes] = gs_ref[at] + ls_ref[at] * d_leaving
        w = wx_ref[:, lanes].astype(F32)
        out = w[taps - 1 : taps] * ext[0:rows, lanes]
        for tap in range(taps - 1):
            out = out + w[tap : tap + 1] * ext[pl.ds(taps - 1 - tap, rows), lanes]
        gx_ref[at] = out.astype(BF16)
        sent.append(put(gx_ref, gx_hbm, out_sems.at[2 * slab + 1], at))
        xc_in[slab].wait()
        dy_in[slab].wait()
        along_leave = along_leave + head_sum(
            xc_ref[at].astype(F32) * d_leaving, slab, head_dim, heads
        )
        along_enter = along_enter + head_sum(dy_ref[at].astype(F32) * y_state, slab, head_dim, heads)
    product = state.astype(F32) * dstate.astype(F32)
    owner = iota((heads, channels), 1) // head_dim
    chosen = jnp.where(iota((heads, channels), 0) == owner, 1.0, 0.0)
    overlap = jnp.sum(dot(chosen, product, ((1,), (0,)), HIGHEST), axis=1, keepdims=True)
    leave_term = leave_step * along_leave
    final = jnp.sum(leave_term, axis=1, keepdims=True) + carry * overlap
    d_cum = z_diff + entering * along_enter - leave_term
    d_cum = d_cum + jnp.where(iota((heads, rows), 1) == rows - 1, final, 0.0)
    after = jnp.where(iota((rows, rows), 0) >= iota((rows, rows), 1), 1.0, 0.0)
    d_log = dot(d_cum, after, ((1,), (0,)), HIGHEST)
    gdt_ref[...] = (along_dt + leaving * along_leave - decay * d_log) * dt_gate
    for copy in sent:
        copy.wait()


def smem():
    return pl.BlockSpec(memory_space=pltpu.SMEM)


def vmem():
    return pl.BlockSpec(memory_space=pltpu.VMEM)


def hbm():
    return pl.BlockSpec(memory_space=pltpu.HBM)


def call(kernel, name, scalars, far, near, far_out, near_out, scratch=()):
    far = [pltpu.with_memory_space_constraint(a, pltpu.HBM) for a in far]
    out = [pltpu.HBM(s, d) for s, d in far_out] + [jax.ShapeDtypeStruct(s, d) for s, d in near_out]
    specs = [hbm() for _ in far_out] + [vmem() for _ in near_out]
    many = len(out) > 1
    return pl.pallas_call(
        kernel,
        name=name,
        out_shape=out if many else out[0],
        in_specs=[smem() for _ in scalars] + [hbm() for _ in far] + [vmem() for _ in near],
        out_specs=specs if many else specs[0],
        scratch_shapes=list(scratch),
        compiler_params=pltpu.CompilerParams(vmem_limit_bytes=VMEM_LIMIT),
    )(*scalars, *far, *near)


def shift_ctx(values, by):
    size = lax.axis_size("ctx")
    pairs = [(i, i + by) for i in range(size) if 0 <= i + by < size]
    return lax.ppermute(values, "ctx", pairs)


def swap_core(values):
    size = lax.axis_size("head")
    return lax.ppermute(values, "head", [(i, i ^ 1) for i in range(size)])


def around(values, by):
    size = lax.axis_size("head")
    return lax.ppermute(values, "head", [(i, (i + 2 * by) % size) for i in range(size)])


def body(x_raw, bc_raw, conv_x_w, conv_bc_w, dt_raw, a_log, d_skip, doc_starts, grad_y):
    rows, channels = x_raw.shape
    heads = a_log.shape[0]
    head_dim = channels // heads
    wide = bc_raw.shape[1]
    count = lax.axis_size("ctx")
    part = channels // count
    core = (lax.axis_index("head") % 2).astype(jnp.int32).reshape(1)
    halo = shift_ctx(jnp.concatenate([x_raw[rows - RIM :], bc_raw[rows - RIM :]], axis=1), 1)
    slabs = channels // LANES
    wide_bf, wide_f = ((rows, channels), BF16), ((rows, channels), F32)
    sems = pltpu.SemaphoreType.DMA
    inputs = [pltpu.VMEM(*wide_bf), pltpu.VMEM(*wide_bf), pltpu.VMEM((rows, wide), BF16)]
    input_sems = [sems((slabs,)), sems((slabs,)), sems((wide // LANES,))]
    ext = pltpu.VMEM((rows + RIM, channels + wide), F32)
    sent = ((count, 2 * part + RIM, LANES), BF16)
    states = ((count, 2 * part, LANES), BF16)
    send = call(
        functools.partial(send_kernel, head_dim),
        "send",
        [doc_starts, a_log],
        [x_raw, grad_y, bc_raw],
        [halo, conv_x_w, conv_bc_w, dt_raw],
        [sent],
        [],
        [*inputs, pltpu.VMEM(*sent), ext, *input_sems, sems((slabs,))],
    )
    got = lax.all_to_all(send, "ctx", 0, 0)
    xc, yi, gs, ls, lx, edy, bcc, gbc, sbc, hv, first = call(
        functools.partial(intra_kernel, head_dim),
        "intra",
        [doc_starts, a_log, d_skip],
        [x_raw, grad_y, bc_raw],
        [halo, conv_x_w, conv_bc_w, dt_raw],
        [wide_bf, wide_f, wide_f, wide_f],
        [
            wide_bf,
            wide_bf,
            ((rows, wide), BF16),
            ((rows, wide), F32),
            ((rows, wide), F32),
            ((8, heads, rows), F32),
            ((2, RIM, channels), F32),
        ],
        [
            *inputs,
            pltpu.VMEM(*wide_bf),
            pltpu.VMEM(*wide_f),
            pltpu.VMEM(*wide_f),
            pltpu.VMEM(*wide_f),
            ext,
            pltpu.VMEM((rows, rows), F32),
            pltpu.VMEM((rows, rows), F32),
            *input_sems,
            sems((4 * slabs,)),
        ],
    )
    got, hv = lax.optimization_barrier((got, hv))
    scanned = call(
        scan_kernel, "scan", [], [], [got], [states], [], [pltpu.VMEM(*states), sems((count // 4,))]
    )
    st = lax.all_to_all(scanned, "ctx", 0, 0)
    half = rows // 2
    keep, give, rim = call(
        bc_kernel,
        "grad_bc",
        [core],
        [],
        [st, lx, edy, bcc, gbc, sbc, first, conv_bc_w],
        [],
        [((half, wide), F32), ((half, wide), BF16), ((RIM, channels + wide), F32)],
        [pltpu.VMEM((rows + RIM, wide), F32), pltpu.VMEM((rows, wide), F32)],
    )
    next_rim = shift_ctx(rim, -1)
    other = swap_core(give)
    message = ((half + RIM, wide), BF16)
    joined = call(
        join_kernel,
        "join",
        [],
        [],
        [keep, other, next_rim, conv_bc_w],
        [],
        [message],
        [pltpu.VMEM((2 * RIM, wide), F32)],
    )
    ring = lax.axis_size("head") // 2
    pieces = [joined] + [around(joined, by) for by in range(1, ring)]
    y_out, grad_x, grad_dt = call(
        functools.partial(out_kernel, head_dim),
        "out",
        [],
        [xc, grad_y, yi, gs, ls],
        [st, bcc, hv, next_rim, conv_x_w],
        [wide_bf, wide_bf],
        [((heads, rows), F32)],
        [
            pltpu.VMEM(*wide_bf),
            pltpu.VMEM(*wide_bf),
            pltpu.VMEM(*wide_f),
            pltpu.VMEM(*wide_f),
            pltpu.VMEM(*wide_f),
            pltpu.VMEM(*wide_bf),
            pltpu.VMEM(*wide_bf),
            pltpu.VMEM((rows + RIM, channels), F32),
            *[sems((slabs,)) for _ in range(5)],
            sems((2 * slabs,)),
        ],
    )
    pieces, grad_dt = lax.optimization_barrier((pieces, grad_dt))
    summed = call(sum_kernel, "sum", [], [], pieces, [], [message])
    swapped = swap_core(summed)
    grad_bc = call(
        last_kernel,
        "last",
        [core],
        [],
        [summed, swapped],
        [],
        [((rows, wide), BF16)],
        [pltpu.VMEM((rows, wide), F32)],
    )
    return (y_out, grad_x, grad_bc, grad_dt)


def solution(mesh):
    in_specs = (
        P("ctx", "head"),
        P("ctx", None),
        P(None, "head"),
        P(),
        P("head", "ctx"),
        P("head"),
        P("head"),
        P("ctx"),
        P("ctx", "head"),
    )
    out_specs = (P("ctx", "head"), P("ctx", "head"), P("ctx", None), P("head", "ctx"))
    return jax.shard_map(body, mesh=mesh, in_specs=in_specs, out_specs=out_specs, check_vma=False)
```

```python
import functools

import jax
import jax.numpy as jnp
from jax import lax
from jax.experimental import pallas as pl
from jax.experimental.pallas import tpu as pltpu
from jax.sharding import PartitionSpec as P

F32 = jnp.float32
BF16 = jnp.bfloat16
LANES = 128
RIM = 8
VMEM_LIMIT = 24 * 1024 * 1024
HIGHEST = lax.Precision.HIGHEST


def dot(a, b, dims, precision=None):
    return lax.dot_general(a, b, (dims, ((), ())), precision=precision, preferred_element_type=F32)


def iota(shape, axis):
    return lax.broadcasted_iota(jnp.int32, shape, axis)


def halves(values):
    high = values.astype(BF16)
    return high, (values - high.astype(F32)).astype(BF16)


def sigmoid(values):
    return 1.0 / (1.0 + jnp.exp(-values))


def spread(values, slab, head_dim):
    heads = values.shape[0]
    high, low = halves(values)
    both = jnp.concatenate([high, low], axis=0)
    row = iota((2 * heads, LANES), 0)
    head = iota((2 * heads, LANES), 1) // head_dim + slab * (LANES // head_dim)
    chosen = jnp.where((row == head) | (row == head + heads), 1.0, 0.0).astype(BF16)
    return dot(both, chosen, ((0,), (0,)))


def head_sum(values, slab, head_dim, heads):
    high, low = halves(values)
    both = jnp.concatenate([high, low], axis=1)
    head = (iota((heads, 2 * LANES), 1) % LANES) // head_dim + slab * (LANES // head_dim)
    chosen = jnp.where(iota((heads, 2 * LANES), 0) == head, 1.0, 0.0).astype(BF16)
    return dot(chosen, both, ((1,), (1,)))


def per_head(ref, heads, rows):
    at = iota((heads, rows), 0)
    values = jnp.zeros((heads, rows), F32)
    for head in range(heads):
        values = jnp.where(at == head, ref[head], values)
    return values


def head_values(doc_ref, a_log_ref, dt_ref):
    heads, rows = dt_ref.shape
    doc = doc_ref[0]
    raw = dt_ref[...]
    step = jnp.maximum(raw, 0.0) + jnp.log(1.0 + jnp.exp(-jnp.abs(raw)))
    decay = jnp.exp(per_head(a_log_ref, heads, rows))
    upto = jnp.where(iota((rows, rows), 0) <= iota((rows, rows), 1), 1.0, 0.0)
    drop = -decay * step
    cum = dot(drop, upto, ((1,), (0,)), HIGHEST)
    final = cum[:, rows - 1 :]
    segment = iota((heads, rows), 1) >= doc
    entering = jnp.where(segment, 0.0, jnp.exp(cum))
    outside = jnp.logical_and(iota((heads, rows), 1) < doc, doc < rows)
    leaving = jnp.where(outside, 0.0, jnp.exp(final - cum))
    carry = jnp.where(doc >= rows, jnp.exp(jnp.broadcast_to(final, (heads, rows))), 0.0)
    return dict(
        step=step, decay=decay, drop=drop, cum=cum, entering=entering, leaving=leaving, carry=carry
    )


def lanes_of(slab):
    return slice(slab * LANES, (slab + 1) * LANES)


def fetch(source, target, sems):
    pieces = sems.shape[0]
    width = source.shape[1] // pieces
    copies = {}
    for piece in range(pieces):
        at = (slice(None), slice(piece * width, (piece + 1) * width))
        copy = pltpu.make_async_copy(source.at[at], target.at[at], sems.at[piece])
        copy.start()
        copies[piece * width // LANES] = copy
    return copies


def arrived(copies, slab):
    if slab in copies:
        copies[slab].wait()


def put(source, target, sem, at):
    copy = pltpu.make_async_copy(source.at[at], target.at[at], sem)
    copy.start()
    return copy


def load_ext(ext, halo_ref, values, at, lanes):
    if halo_ref is None:
        ext[0:RIM, at] = jnp.zeros((RIM, LANES), F32)
    else:
        ext[0:RIM, at] = halo_ref[:, at].astype(F32)
    ext[RIM : RIM + values.shape[0], at] = values[:, lanes].astype(F32)


def filtered(ext, w_ref, at, w_at, rows):
    taps = w_ref.shape[0]
    lanes = pl.ds(at, LANES)
    w = w_ref[:, w_at : w_at + LANES].astype(F32)
    total = w[0:1] * ext[pl.ds(RIM - taps + 1, rows), lanes]
    for tap in range(1, taps):
        total = total + w[tap : tap + 1] * ext[pl.ds(RIM - taps + 1 + tap, rows), lanes]
    return total


def gather_kernel(
    head_dim, part, doc_ref, a_log_ref, x_hbm, dy_hbm, bc_hbm, wx_ref, wbc_ref, dt_ref,
    sum_ref, ls_ref, edy_ref, top_ref, tail_ref,
    x_ref, dy_ref, bc_ref, ext, x_sems, dy_sems, bc_sems,
):
    rows, channels = x_ref.shape
    bc_in = fetch(bc_hbm, bc_ref, bc_sems)
    x_in = fetch(x_hbm, x_ref, x_sems)
    dy_in = fetch(dy_hbm, dy_ref, dy_sems)
    v = head_values(doc_ref, a_log_ref, dt_ref)
    leave_step = v["leaving"] * v["step"]
    high, low = halves(v["carry"][:, 0:LANES])
    at = iota((RIM, LANES), 0)
    below = iota((rows, LANES), 0) >= RIM
    for chunk in range(tail_ref.shape[0]):
        head = chunk * part // head_dim
        tile = jnp.where(
            at == 0,
            high[head : head + 1].astype(F32),
            jnp.where(at == 1, low[head : head + 1].astype(F32), 0.0),
        )
        tail_ref[chunk] = tile.astype(BF16)
    bc = []
    for half in range(2):
        arrived(bc_in, half)
        load_ext(ext, None, bc_ref, lanes_of(channels // LANES + half), lanes_of(half))
        pre = filtered(ext, wbc_ref, channels + half * LANES, half * LANES, rows)
        bc.append((pre * sigmoid(pre)).astype(BF16))
    for slab in range(channels // LANES):
        lanes = lanes_of(slab)
        arrived(x_in, slab)
        load_ext(ext, None, x_ref, lanes, lanes)
        pre = filtered(ext, wx_ref, slab * LANES, slab * LANES, rows)
        x_conv = (pre * sigmoid(pre)).astype(BF16).astype(F32)
        leave = spread(leave_step, slab, head_dim)
        leaving_x = jnp.where(below, x_conv * leave, 0.0).astype(BF16)
        arrived(dy_in, slab)
        enter_dy = dy_ref[:, lanes].astype(F32) * spread(v["entering"], slab, head_dim)
        sum_ref[0, lanes, :] = dot(leaving_x, bc[0], ((0,), (0,)))
        sum_ref[1, lanes, :] = dot(jnp.where(below, enter_dy, 0.0).astype(BF16), bc[1], ((0,), (0,)))
        ls_ref[:, lanes] = leave[0:RIM]
        edy_ref[:, lanes] = enter_dy[0:RIM]
    top_ref[...] = ext[RIM : 2 * RIM, :]


def send_kernel(
    halo_ref, sum_ref, ls_ref, edy_ref, top_ref, tail_ref, wx_ref, wbc_ref,
    send_hbm, send_ref, ext, sems,
):
    channels = ls_ref.shape[1]
    part = channels // send_ref.shape[0]
    per_slab = LANES // part
    ext[0:RIM, :] = halo_ref[...].astype(F32)
    ext[RIM:, :] = top_ref[...]
    none = jnp.zeros((RIM, LANES), F32)

    def conv(w_ref, at, w_at):
        pre = filtered(ext, w_ref, at, w_at, RIM)
        return (pre * sigmoid(pre)).astype(BF16).astype(F32)

    bc = [
        jnp.concatenate([conv(wbc_ref, channels + at, at), none], axis=0).astype(BF16)
        for at in (0, LANES)
    ]
    slabs = channels // LANES
    sent = []
    for slab in range(slabs):
        lanes = lanes_of(slab)
        leaving_x = conv(wx_ref, slab * LANES, slab * LANES) * ls_ref[:, lanes]
        leaving_x = jnp.concatenate([leaving_x, none], axis=0).astype(BF16)
        enter_dy = jnp.concatenate([edy_ref[:, lanes], none], axis=0).astype(BF16)
        forward = (sum_ref[0, lanes, :] + dot(leaving_x, bc[0], ((0,), (0,)))).astype(BF16)
        backward = (sum_ref[1, lanes, :] + dot(enter_dy, bc[1], ((0,), (0,)))).astype(BF16)
        own = slice(slab * per_slab, (slab + 1) * per_slab)
        send_ref[own, 0:part, :] = forward.reshape(per_slab, part, LANES)
        send_ref[own, part : 2 * part, :] = backward.reshape(per_slab, part, LANES)
        send_ref[own, 2 * part : 2 * part + RIM, :] = tail_ref[own]
        group = slabs // sems.shape[0]
        if slab % group == group - 1:
            ready = slice((slab + 1 - group) * per_slab, (slab + 1) * per_slab)
            sent.append(put(send_ref, send_hbm, sems.at[slab // group], (ready,)))
    for copy in sent:
        copy.wait()


def scan_kernel(got_ref, out_hbm, out_ref, sems):
    count, width, lanes = out_ref.shape
    part = width // 2
    forward = jnp.zeros((part, lanes), F32)
    backward = jnp.zeros((part, lanes), F32)

    def carry(at):
        tail = got_ref[at, width : width + RIM, :].astype(F32)
        return tail[0:1] + tail[1:2]

    sent = []
    for at in range(count):
        out_ref[at, 0:part, :] = forward.astype(BF16)
        forward = carry(at) * forward + got_ref[at, 0:part, :].astype(F32)
        back = count - 1 - at
        out_ref[back, part : 2 * part, :] = backward.astype(BF16)
        backward = carry(back) * backward + got_ref[back, part : 2 * part, :].astype(F32)
        low, high = min(at, back), max(at, back)
        if at >= count // 2 and (at + 1) % 4 == 0:
            sent.append(put(out_ref, out_hbm, sems.at[len(sent)], (slice(high - 3, high + 1),)))
            sent.append(put(out_ref, out_hbm, sems.at[len(sent)], (slice(low, low + 4),)))
    for copy in sent:
        copy.wait()


def intra_kernel(
    head_dim, doc_ref, a_log_ref, skip_ref, x_hbm, dy_hbm, bc_hbm, halo_ref, wx_ref, wbc_ref, dt_ref,
    xc_hbm, yi_hbm, gs_hbm, ls_hbm,
    lx_ref, edy_ref, bcc_ref, gbc_ref, sbc_ref, hv_ref, rim_ref,
    x_ref, dy_ref, bc_ref, xc_ref, yi_ref, gs_ref, ls_ref, ext, bias, dgram,
    x_sems, dy_sems, bc_sems, out_sems,
):
    rows, channels = x_ref.shape
    heads = dt_ref.shape[0]
    doc = doc_ref[0]
    bc_in = fetch(bc_hbm, bc_ref, bc_sems)
    x_in = fetch(x_hbm, x_ref, x_sems)
    dy_in = fetch(dy_hbm, dy_ref, dy_sems)
    v = head_values(doc_ref, a_log_ref, dt_ref)
    for half in range(2):
        lanes = lanes_of(half)
        arrived(bc_in, half)
        load_ext(ext, halo_ref, bc_ref, lanes_of(channels // LANES + half), lanes)
        pre = filtered(ext, wbc_ref, channels + half * LANES, half * LANES, rows)
        gate = sigmoid(pre)
        bcc_ref[:, lanes] = (pre * gate).astype(BF16)
        sbc_ref[:, lanes] = gate * (1.0 + pre * (1.0 - gate))
    b_matrix = bcc_ref[:, 0:LANES]
    c_matrix = bcc_ref[:, LANES:]
    gram = dot(c_matrix, b_matrix, ((1,), (1,)))
    t_at, s_at = iota((rows, rows), 0), iota((rows, rows), 1)
    bias[...] = jnp.where((t_at >= s_at) & ((t_at >= doc) == (s_at >= doc)), 0.0, -1e30)
    dgram[...] = jnp.zeros_like(dgram)
    downto = jnp.where(t_at >= s_at, 1.0, 0.0)
    cum = v["cum"]
    cum_t = dot(downto, v["drop"], ((1,), (1,)), HIGHEST)
    skip = per_head(skip_ref, heads, rows)
    leave_step = v["leaving"] * v["step"]
    along_dt = jnp.zeros((heads, rows), F32)
    z_diff = jnp.zeros((heads, rows), F32)
    low_half = iota((rows, LANES), 1) < head_dim
    sent = []
    for slab in range(channels // LANES):
        lanes = lanes_of(slab)
        arrived(x_in, slab)
        load_ext(ext, halo_ref, x_ref, lanes, lanes)
        arrived(dy_in, slab)
        pre = filtered(ext, wx_ref, slab * LANES, slab * LANES, rows)
        gate = sigmoid(pre)
        x_bf = (pre * gate).astype(BF16)
        silu_grad = gate * (1.0 + pre * (1.0 - gate))
        x_conv = x_bf.astype(F32)
        xc_ref[:, lanes] = x_bf
        step = spread(v["step"], slab, head_dim)
        leave = spread(leave_step, slab, head_dim)
        enter = spread(v["entering"], slab, head_dim)
        skips = spread(skip, slab, head_dim)
        dy_bf = dy_ref[:, lanes]
        dy = dy_bf.astype(F32)
        lx_ref[:, lanes] = (x_conv * leave).astype(BF16)
        edy_ref[:, lanes] = (dy * enter).astype(BF16)
        scaled = (x_conv * step).astype(BF16)
        intra = jnp.zeros((rows, LANES), F32)
        d_scaled = jnp.zeros((rows, LANES), F32)
        for side in range(LANES // head_dim):
            head = slab * (LANES // head_dim) + side
            mine = low_half if side == 0 else jnp.logical_not(low_half)
            scaled_h = jnp.where(mine, scaled.astype(F32), 0.0).astype(BF16)
            dy_h = jnp.where(mine, dy, 0.0).astype(BF16)
            kernel = jnp.exp((cum_t[:, head : head + 1] - cum[head : head + 1, :]) + bias[...])
            mixing = (gram * kernel).astype(BF16)
            response = dot(dy_h, scaled, ((1,), (1,)))
            dgram[...] += response * kernel
            intra = intra + dot(mixing, scaled_h, ((1,), (0,)))
            d_scaled = d_scaled + dot(mixing, dy_h, ((0,), (0,)))
        yi_ref[:, lanes] = intra + skips * x_conv
        gs_ref[:, lanes] = (step * d_scaled + skips * dy) * silu_grad
        ls_ref[:, lanes] = leave * silu_grad
        rim_ref[0, :, lanes] = gs_ref[0:RIM, lanes]
        rim_ref[1, :, lanes] = ls_ref[0:RIM, lanes]
        group = channels // LANES // (out_sems.shape[0] // 4)
        if slab % group == group - 1:
            at = (slice(None), slice((slab + 1 - group) * LANES, (slab + 1) * LANES))
            for which, (mine, out) in enumerate(
                ((xc_ref, xc_hbm), (yi_ref, yi_hbm), (gs_ref, gs_hbm), (ls_ref, ls_hbm))
            ):
                sent.append(put(mine, out, out_sems.at[slab // group * 4 + which], at))
        along_dt = along_dt + head_sum(x_conv * d_scaled, slab, head_dim, heads)
        z_diff = z_diff + head_sum(
            dy * intra - scaled.astype(F32) * d_scaled, slab, head_dim, heads
        )
    d_gram = dgram[...]
    gbc_ref[:, 0:LANES] = dot(d_gram, c_matrix.astype(F32), ((0,), (0,)), HIGHEST)
    gbc_ref[:, LANES:] = dot(d_gram, b_matrix.astype(F32), ((1,), (0,)), HIGHEST)
    small = [
        leave_step,
        v["leaving"],
        v["entering"],
        along_dt,
        z_diff,
        v["carry"],
        v["decay"],
        sigmoid(dt_ref[...]),
    ]
    for at, values in enumerate(small):
        hv_ref[at] = values
    for copy in sent:
        copy.wait()


def state_of(st_ref, which):
    count, width, lanes = st_ref.shape
    part = width // 2
    return st_ref[:, which * part : (which + 1) * part, :].reshape(count * part, lanes)


def bc_kernel(
    core_ref, st_ref, lx_ref, edy_ref, b_ref, gbc_ref, sbc_ref, rim_ref, wbc_ref,
    keep_ref, give_ref, halo_ref, ext, total,
):
    rows = lx_ref.shape[0]
    taps = wbc_ref.shape[0]
    state, dstate = state_of(st_ref, 0), state_of(st_ref, 1)
    grad_b = gbc_ref[:, 0:LANES] + dot(lx_ref[...], dstate, ((1,), (0,)))
    grad_c = gbc_ref[:, LANES:] + dot(edy_ref[...], state, ((1,), (0,)))
    ext[0:rows, 0:LANES] = grad_b * sbc_ref[:, 0:LANES]
    ext[0:rows, LANES:] = grad_c * sbc_ref[:, LANES:]
    ext[rows:, :] = jnp.zeros((RIM, 2 * LANES), F32)
    w = wbc_ref[...].astype(F32)
    out = w[taps - 1 : taps] * ext[0:rows, :]
    for tap in range(taps - 1):
        out = out + w[tap : tap + 1] * ext[pl.ds(taps - 1 - tap, rows), :]
    total[...] = out
    half = rows // 2
    core = core_ref[0]
    keep_ref[...] = total[pl.ds(pl.multiple_of(core * half, half), half), :]
    give_ref[...] = total[pl.ds(pl.multiple_of((1 - core) * half, half), half), :].astype(BF16)
    d_leaving = dot(b_ref[0 : 2 * RIM, 0:LANES], dstate, ((1,), (1,)))[0:RIM]
    channels = rim_ref.shape[2]
    halo_ref[:, 0:channels] = rim_ref[0] + rim_ref[1] * d_leaving
    halo_ref[:, channels:] = ext[0:RIM, :]


def join_kernel(keep_ref, got_ref, halo_ref, wbc_ref, out_ref, ext):
    half = keep_ref.shape[0]
    taps = wbc_ref.shape[0]
    wide = keep_ref.shape[1]
    out_ref[0:half, :] = (keep_ref[...] + got_ref[...].astype(F32)).astype(BF16)
    ext[0:RIM, :] = jnp.zeros((RIM, wide), F32)
    ext[RIM:, :] = halo_ref[:, halo_ref.shape[1] - wide :]
    w = wbc_ref[...].astype(F32)
    rim = jnp.zeros((RIM, wide), F32)
    for tap in range(taps - 1):
        rim = rim + w[tap : tap + 1] * ext[pl.ds(taps - 1 - tap, RIM), :]
    out_ref[half:, :] = rim.astype(BF16)


def sum_kernel(*refs):
    out_ref = refs[-1]
    total = refs[0][...].astype(F32)
    for ref in refs[1:-1]:
        total = total + ref[...].astype(F32)
    out_ref[...] = total.astype(BF16)


def last_kernel(core_ref, mine_ref, got_ref, out_ref, total):
    rows = out_ref.shape[0]
    half = rows // 2
    core = core_ref[0]
    total[pl.ds(pl.multiple_of(core * half, half), half), :] = mine_ref[0:half, :].astype(F32)
    total[pl.ds(pl.multiple_of((1 - core) * half, half), half), :] = got_ref[0:half, :].astype(F32)
    total[rows - RIM :, :] += mine_ref[half:, :].astype(F32) + got_ref[half:, :].astype(F32)
    out_ref[...] = total[...].astype(BF16)


def y_kernel(
    head_dim, dy_hbm, yi_hbm, st_ref, bcc_ref, hv_ref,
    y_hbm, enter_ref, dy_ref, yi_ref, y_ref, dy_sems, yi_sems, sems,
):
    rows, channels = dy_ref.shape
    heads = hv_ref.shape[1]
    slabs = channels // LANES
    yi_in = fetch(yi_hbm, yi_ref, yi_sems)
    dy_in = fetch(dy_hbm, dy_ref, dy_sems)
    state = state_of(st_ref, 0)
    c_matrix = bcc_ref[:, LANES:]
    entering = hv_ref[2]
    along_enter = jnp.zeros((heads, rows), F32)
    sent = []
    for slab in range(slabs):
        lanes = lanes_of(slab)
        y_state = dot(c_matrix, state[lanes], ((1,), (1,)))
        arrived(yi_in, slab)
        y_ref[:, lanes] = (yi_ref[:, lanes] + spread(entering, slab, head_dim) * y_state).astype(BF16)
        group = slabs // sems.shape[0]
        if slab % group == group - 1:
            at = (slice(None), slice((slab + 1 - group) * LANES, (slab + 1) * LANES))
            sent.append(put(y_ref, y_hbm, sems.at[slab // group], at))
        arrived(dy_in, slab)
        along_enter = along_enter + head_sum(
            dy_ref[:, lanes].astype(F32) * y_state, slab, head_dim, heads
        )
    enter_ref[...] = along_enter
    for copy in sent:
        copy.wait()


def x_kernel(
    head_dim, xc_hbm, gs_hbm, ls_hbm, st_ref, bcc_ref, hv_ref, enter_ref, halo_ref, wx_ref,
    gx_hbm, gdt_ref, xc_ref, gs_ref, ls_ref, gx_ref, ext, xc_sems, gs_sems, ls_sems, sems,
):
    rows, channels = xc_ref.shape
    heads = hv_ref.shape[1]
    taps = wx_ref.shape[0]
    slabs = channels // LANES
    gs_in = fetch(gs_hbm, gs_ref, gs_sems)
    ls_in = fetch(ls_hbm, ls_ref, ls_sems)
    xc_in = fetch(xc_hbm, xc_ref, xc_sems)
    state, dstate = state_of(st_ref, 0), state_of(st_ref, 1)
    b_matrix = bcc_ref[:, 0:LANES]
    leave_step, leaving, entering, along_dt, z_diff, carry, decay, dt_gate = [
        hv_ref[at] for at in range(8)
    ]
    along_enter = enter_ref[...]
    along_leave = jnp.zeros((heads, rows), F32)
    ext[rows:, :] = halo_ref[:, 0:channels]
    sent = []
    for slab in range(slabs):
        lanes = lanes_of(slab)
        d_leaving = dot(b_matrix, dstate[lanes], ((1,), (1,)))
        arrived(gs_in, slab)
        arrived(ls_in, slab)
        ext[0:rows, lanes] = gs_ref[:, lanes] + ls_ref[:, lanes] * d_leaving
        w = wx_ref[:, lanes].astype(F32)
        out = w[taps - 1 : taps] * ext[0:rows, lanes]
        for tap in range(taps - 1):
            out = out + w[tap : tap + 1] * ext[pl.ds(taps - 1 - tap, rows), lanes]
        gx_ref[:, lanes] = out.astype(BF16)
        group = slabs // sems.shape[0]
        if slab % group == group - 1:
            at = (slice(None), slice((slab + 1 - group) * LANES, (slab + 1) * LANES))
            sent.append(put(gx_ref, gx_hbm, sems.at[slab // group], at))
        arrived(xc_in, slab)
        along_leave = along_leave + head_sum(
            xc_ref[:, lanes].astype(F32) * d_leaving, slab, head_dim, heads
        )
    product = state.astype(F32) * dstate.astype(F32)
    owner = iota((heads, channels), 1) // head_dim
    chosen = jnp.where(iota((heads, channels), 0) == owner, 1.0, 0.0)
    overlap = jnp.sum(dot(chosen, product, ((1,), (0,)), HIGHEST), axis=1, keepdims=True)
    leave_term = leave_step * along_leave
    final = jnp.sum(leave_term, axis=1, keepdims=True) + carry * overlap
    d_cum = z_diff + entering * along_enter - leave_term
    d_cum = d_cum + jnp.where(iota((heads, rows), 1) == rows - 1, final, 0.0)
    after = jnp.where(iota((rows, rows), 0) >= iota((rows, rows), 1), 1.0, 0.0)
    d_log = dot(d_cum, after, ((1,), (0,)), HIGHEST)
    gdt_ref[...] = (along_dt + leaving * along_leave - decay * d_log) * dt_gate
    for copy in sent:
        copy.wait()


def smem():
    return pl.BlockSpec(memory_space=pltpu.SMEM)


def vmem():
    return pl.BlockSpec(memory_space=pltpu.VMEM)


def hbm():
    return pl.BlockSpec(memory_space=pltpu.HBM)


def call(kernel, name, scalars, far, near, far_out, near_out, scratch=()):
    far = [pltpu.with_memory_space_constraint(a, pltpu.HBM) for a in far]
    out = [pltpu.HBM(s, d) for s, d in far_out] + [jax.ShapeDtypeStruct(s, d) for s, d in near_out]
    specs = [hbm() for _ in far_out] + [vmem() for _ in near_out]
    many = len(out) > 1
    return pl.pallas_call(
        kernel,
        name=name,
        out_shape=out if many else out[0],
        in_specs=[smem() for _ in scalars] + [hbm() for _ in far] + [vmem() for _ in near],
        out_specs=specs if many else specs[0],
        scratch_shapes=list(scratch),
        compiler_params=pltpu.CompilerParams(vmem_limit_bytes=VMEM_LIMIT),
    )(*scalars, *far, *near)


def shift_ctx(values, by):
    size = lax.axis_size("ctx")
    pairs = [(i, i + by) for i in range(size) if 0 <= i + by < size]
    return lax.ppermute(values, "ctx", pairs)


def swap_core(values):
    size = lax.axis_size("head")
    return lax.ppermute(values, "head", [(i, i ^ 1) for i in range(size)])


def around(values, by):
    size = lax.axis_size("head")
    return lax.ppermute(values, "head", [(i, (i + 2 * by) % size) for i in range(size)])


def body(x_raw, bc_raw, conv_x_w, conv_bc_w, dt_raw, a_log, d_skip, doc_starts, grad_y):
    rows, channels = x_raw.shape
    heads = a_log.shape[0]
    head_dim = channels // heads
    wide = bc_raw.shape[1]
    count = lax.axis_size("ctx")
    part = channels // count
    core = (lax.axis_index("head") % 2).astype(jnp.int32).reshape(1)
    halo = shift_ctx(jnp.concatenate([x_raw[rows - RIM :], bc_raw[rows - RIM :]], axis=1), 1)
    wide_bf, wide_f = ((rows, channels), BF16), ((rows, channels), F32)
    sems = pltpu.SemaphoreType.DMA
    two = sems((2,))
    inputs = [pltpu.VMEM(*wide_bf), pltpu.VMEM(*wide_bf), pltpu.VMEM((rows, wide), BF16)]
    input_sems = [two, two, sems((1,))]
    ext = pltpu.VMEM((rows + RIM, channels + wide), F32)
    sent = ((count, 2 * part + RIM, LANES), BF16)
    states = ((count, 2 * part, LANES), BF16)
    sums, leave_top, dy_top, top, tail = call(
        functools.partial(gather_kernel, head_dim, part),
        "gather",
        [doc_starts, a_log],
        [x_raw, grad_y, bc_raw],
        [conv_x_w, conv_bc_w, dt_raw],
        [],
        [
            ((2, channels, LANES), F32),
            ((RIM, channels), F32),
            ((RIM, channels), F32),
            ((RIM, channels + wide), F32),
            ((count, RIM, LANES), BF16),
        ],
        [*inputs, ext, *input_sems],
    )
    send = call(
        send_kernel,
        "send",
        [],
        [],
        [halo, sums, leave_top, dy_top, top, tail, conv_x_w, conv_bc_w],
        [sent],
        [],
        [pltpu.VMEM(*sent), pltpu.VMEM((2 * RIM, channels + wide), F32), two],
    )
    got = lax.all_to_all(send, "ctx", 0, 0)
    xc, yi, gs, ls, lx, edy, bcc, gbc, sbc, hv, first = call(
        functools.partial(intra_kernel, head_dim),
        "intra",
        [doc_starts, a_log, d_skip],
        [x_raw, grad_y, bc_raw],
        [halo, conv_x_w, conv_bc_w, dt_raw],
        [wide_bf, wide_f, wide_f, wide_f],
        [
            wide_bf,
            wide_bf,
            ((rows, wide), BF16),
            ((rows, wide), F32),
            ((rows, wide), F32),
            ((8, heads, rows), F32),
            ((2, RIM, channels), F32),
        ],
        [
            *inputs,
            pltpu.VMEM(*wide_bf),
            pltpu.VMEM(*wide_f),
            pltpu.VMEM(*wide_f),
            pltpu.VMEM(*wide_f),
            ext,
            pltpu.VMEM((rows, rows), F32),
            pltpu.VMEM((rows, rows), F32),
            *input_sems,
            sems((8,)),
        ],
    )
    got, hv = lax.optimization_barrier((got, hv))
    scanned = call(
        scan_kernel, "scan", [], [], [got], [states], [], [pltpu.VMEM(*states), sems((count // 4,))]
    )
    st = lax.all_to_all(scanned, "ctx", 0, 0)
    half = rows // 2
    keep, give, rim = call(
        bc_kernel,
        "grad_bc",
        [core],
        [],
        [st, lx, edy, bcc, gbc, sbc, first, conv_bc_w],
        [],
        [
            ((half, wide), F32),
            ((half, wide), BF16),
            ((RIM, channels + wide), F32),
        ],
        [pltpu.VMEM((rows + RIM, wide), F32), pltpu.VMEM((rows, wide), F32)],
    )
    next_rim = shift_ctx(rim, -1)
    other = swap_core(give)
    st, keep = lax.optimization_barrier((st, keep))
    y_out, along_enter = call(
        functools.partial(y_kernel, head_dim),
        "y_out",
        [],
        [grad_y, yi],
        [st, bcc, hv],
        [wide_bf],
        [((heads, rows), F32)],
        [
            pltpu.VMEM(*wide_bf),
            pltpu.VMEM(*wide_f),
            pltpu.VMEM(*wide_bf),
            two,
            two,
            two,
        ],
    )
    other, next_rim, along_enter = lax.optimization_barrier((other, next_rim, along_enter))
    message = ((half + RIM, wide), BF16)
    joined = call(
        join_kernel,
        "join",
        [],
        [],
        [keep, other, next_rim, conv_bc_w],
        [],
        [message],
        [pltpu.VMEM((2 * RIM, wide), F32)],
    )
    ring = lax.axis_size("head") // 2
    pieces = [joined] + [around(joined, by) for by in range(1, ring)]
    grad_x, grad_dt = call(
        functools.partial(x_kernel, head_dim),
        "grad_x",
        [],
        [xc, gs, ls],
        [st, bcc, hv, along_enter, next_rim, conv_x_w],
        [wide_bf],
        [((heads, rows), F32)],
        [
            pltpu.VMEM(*wide_bf),
            pltpu.VMEM(*wide_f),
            pltpu.VMEM(*wide_f),
            pltpu.VMEM(*wide_bf),
            pltpu.VMEM((rows + RIM, channels), F32),
            two,
            two,
            two,
            two,
        ],
    )
    pieces, grad_dt = lax.optimization_barrier((pieces, grad_dt))
    summed = call(sum_kernel, "sum", [], [], pieces, [], [message])
    swapped = swap_core(summed)
    grad_bc = call(
        last_kernel,
        "last",
        [core],
        [],
        [summed, swapped],
        [],
        [((rows, wide), BF16)],
        [pltpu.VMEM((rows, wide), F32)],
    )
    return (y_out, grad_x, grad_bc, grad_dt)


def solution(mesh):
    in_specs = (
        P("ctx", "head"),
        P("ctx", None),
        P(None, "head"),
        P(),
        P("head", "ctx"),
        P("head"),
        P("head"),
        P("ctx"),
        P("ctx", "head"),
    )
    out_specs = (P("ctx", "head"), P("ctx", "head"), P("ctx", None), P("head", "ctx"))
    return jax.shard_map(body, mesh=mesh, in_specs=in_specs, out_specs=out_specs, check_vma=False)
```

```python
import functools

import jax
import jax.numpy as jnp
from jax import lax
from jax.experimental import pallas as pl
from jax.experimental.pallas import tpu as pltpu
from jax.sharding import PartitionSpec as P

F32 = jnp.float32
BF16 = jnp.bfloat16
LANES = 128
RIM = 8
VMEM_LIMIT = 24 * 1024 * 1024
HIGHEST = lax.Precision.HIGHEST


def dot(a, b, dims, precision=None):
    return lax.dot_general(a, b, (dims, ((), ())), precision=precision, preferred_element_type=F32)


def iota(shape, axis):
    return lax.broadcasted_iota(jnp.int32, shape, axis)


def halves(values):
    high = values.astype(BF16)
    return high, (values - high.astype(F32)).astype(BF16)


def sigmoid(values):
    return 0.5 * jnp.tanh(0.5 * values) + 0.5


def diagonal(size):
    return jnp.where(iota((size, size), 0) == iota((size, size), 1), 1.0, 0.0).astype(BF16)


def columns(values):
    both = jnp.concatenate(halves(values), axis=0)
    return dot(diagonal(values.shape[1]), both, ((1,), (1,))).astype(BF16)


def spread(pairs, slab, head_dim):
    heads = pairs.shape[1] // 2
    row = iota((2 * heads, LANES), 0)
    head = iota((2 * heads, LANES), 1) // head_dim + slab * (LANES // head_dim)
    chosen = jnp.where((row == head) | (row == head + heads), 1.0, 0.0).astype(BF16)
    return dot(pairs, chosen, ((1,), (0,)))


def head_sum(values, slab, head_dim, heads):
    high, low = halves(values)
    both = jnp.concatenate([high, low], axis=1)
    head = (iota((heads, 2 * LANES), 1) % LANES) // head_dim + slab * (LANES // head_dim)
    chosen = jnp.where(iota((heads, 2 * LANES), 0) == head, 1.0, 0.0).astype(BF16)
    return dot(chosen, both, ((1,), (1,)))


def per_head(ref, heads, rows):
    at = iota((heads, rows), 0)
    values = jnp.zeros((heads, rows), F32)
    for head in range(heads):
        values = jnp.where(at == head, ref[head], values)
    return values


def head_values(doc_ref, a_log_ref, dt_ref):
    heads, rows = dt_ref.shape
    doc = doc_ref[0]
    raw = dt_ref[...]
    step = jnp.maximum(raw, 0.0) + jnp.log(1.0 + jnp.exp(-jnp.abs(raw)))
    decay = jnp.exp(per_head(a_log_ref, heads, rows))
    upto = jnp.where(iota((rows, rows), 0) <= iota((rows, rows), 1), 1.0, 0.0)
    drop = -decay * step
    cum = dot(drop, upto, ((1,), (0,)), HIGHEST)
    final = cum[:, rows - 1 :]
    segment = iota((heads, rows), 1) >= doc
    entering = jnp.where(segment, 0.0, jnp.exp(cum))
    outside = jnp.logical_and(iota((heads, rows), 1) < doc, doc < rows)
    leaving = jnp.where(outside, 0.0, jnp.exp(final - cum))
    carry = jnp.where(doc >= rows, jnp.exp(jnp.broadcast_to(final, (heads, rows))), 0.0)
    return dict(
        step=step, decay=decay, drop=drop, cum=cum, entering=entering, leaving=leaving, carry=carry
    )


def lanes_of(slab):
    return slice(slab * LANES, (slab + 1) * LANES)


def fetch(source, target, sems):
    pieces = sems.shape[0]
    width = source.shape[1] // pieces
    copies = {}
    for piece in range(pieces):
        at = (slice(None), slice(piece * width, (piece + 1) * width))
        copy = pltpu.make_async_copy(source.at[at], target.at[at], sems.at[piece])
        copy.start()
        copies[piece * width // LANES] = copy
    return copies


def arrived(copies, slab):
    if slab in copies:
        copies[slab].wait()


def put(source, target, sem, at):
    copy = pltpu.make_async_copy(source.at[at], target.at[at], sem)
    copy.start()
    return copy


def load_ext(ext, halo_ref, values, at, lanes):
    if halo_ref is None:
        ext[0:RIM, at] = jnp.zeros((RIM, LANES), F32)
    else:
        ext[0:RIM, at] = halo_ref[:, at].astype(F32)
    ext[RIM : RIM + values.shape[0], at] = values[:, lanes].astype(F32)


def filtered(ext, w_ref, at, w_at, rows):
    taps = w_ref.shape[0]
    lanes = pl.ds(at, LANES)
    w = w_ref[:, w_at : w_at + LANES].astype(F32)
    total = w[0:1] * ext[pl.ds(RIM - taps + 1, rows), lanes]
    for tap in range(1, taps):
        total = total + w[tap : tap + 1] * ext[pl.ds(RIM - taps + 1 + tap, rows), lanes]
    return total


def gather_kernel(
    head_dim, doc_ref, a_log_ref, x_hbm, dy_hbm, bc_hbm, wx_ref, wbc_ref, dt_ref,
    sum_ref, ls_ref, edy_ref, top_ref, tail_ref,
    x_ref, dy_ref, bc_ref, ext, x_sems, dy_sems, bc_sems,
):
    rows, channels = x_ref.shape
    bc_in = fetch(bc_hbm, bc_ref, bc_sems)
    x_in = fetch(x_hbm, x_ref, x_sems)
    dy_in = fetch(dy_hbm, dy_ref, dy_sems)
    v = head_values(doc_ref, a_log_ref, dt_ref)
    leave_step = columns(v["leaving"] * v["step"])
    entering = columns(v["entering"])
    heads = dt_ref.shape[0]
    own = iota((heads, LANES), 0) == iota((heads, LANES), 1)
    carry = jnp.sum(jnp.where(own, v["carry"][:, 0:LANES], 0.0), axis=0, keepdims=True)
    high, low = [half.astype(F32) for half in halves(carry)]
    at = iota((RIM, LANES), 0)
    tail_ref[...] = jnp.where(at == 0, high, jnp.where(at == 1, low, 0.0)).astype(BF16)
    below = iota((rows, LANES), 0) >= RIM
    bc = []
    for half in range(2):
        arrived(bc_in, half)
        load_ext(ext, None, bc_ref, lanes_of(channels // LANES + half), lanes_of(half))
        pre = filtered(ext, wbc_ref, channels + half * LANES, half * LANES, rows)
        bc.append((pre * sigmoid(pre)).T.astype(BF16))
    for slab in range(channels // LANES):
        lanes = lanes_of(slab)
        arrived(x_in, slab)
        load_ext(ext, None, x_ref, lanes, lanes)
        pre = filtered(ext, wx_ref, slab * LANES, slab * LANES, rows)
        x_conv = (pre * sigmoid(pre)).astype(BF16).astype(F32)
        leave = spread(leave_step, slab, head_dim)
        leaving_x = jnp.where(below, x_conv * leave, 0.0).astype(BF16)
        arrived(dy_in, slab)
        enter_dy = dy_ref[:, lanes].astype(F32) * spread(entering, slab, head_dim)
        sum_ref[0, :, lanes] = dot(bc[0], leaving_x, ((1,), (0,)))
        masked = jnp.where(below, enter_dy, 0.0).astype(BF16)
        sum_ref[1, :, lanes] = dot(bc[1], masked, ((1,), (0,)))
        ls_ref[:, lanes] = leave[0:RIM]
        edy_ref[:, lanes] = enter_dy[0:RIM]
    top_ref[...] = ext[RIM : 2 * RIM, :]


def chunk_of(across, side, which):
    return 16 * across + 2 * side + which


def send_kernel(
    halo_ref, sum_ref, ls_ref, edy_ref, top_ref, tail_ref, wx_ref, wbc_ref, send_ref, ext,
):
    channels = ls_ref.shape[1]
    count = send_ref.shape[0]
    tall = 2 * RIM
    ext[0:RIM, :] = halo_ref[...].astype(F32)
    ext[RIM:, :] = top_ref[...]
    none = jnp.zeros((RIM, LANES), F32)

    def conv(w_ref, at, w_at):
        pre = filtered(ext, w_ref, at, w_at, RIM)
        return (pre * sigmoid(pre)).astype(BF16).astype(F32)

    bc = []
    for at in (0, LANES):
        top = jnp.concatenate([conv(wbc_ref, channels + at, at), none], axis=0).astype(BF16)
        bc.append(dot(top, diagonal(tall), ((0,), (0,))).astype(BF16))
    tail = tail_ref[...]
    for chunk in range(count):
        send_ref[chunk, send_ref.shape[1] - RIM :, :] = tail
    slabs = channels // LANES
    for slab in range(slabs):
        lanes = lanes_of(slab)
        across, tile = slab // (slabs // 2), slab % (slabs // 2)
        leaving_x = conv(wx_ref, slab * LANES, slab * LANES) * ls_ref[:, lanes]
        enter_dy = edy_ref[:, lanes]
        for which, top in enumerate((leaving_x, enter_dy)):
            top = jnp.concatenate([top, none], axis=0).astype(BF16)
            total = (sum_ref[which, :, lanes] + dot(bc[which], top, ((1,), (0,)))).astype(BF16)
            for side in range(LANES // tall):
                piece = total[side * tall : (side + 1) * tall]
                send_ref[chunk_of(across, side, which), tile * tall : (tile + 1) * tall, :] = piece


def scan_kernel(head_dim, got_ref, out_hbm, out_ref, tails, carries, sems):
    count, width, lanes = out_ref.shape
    tall = 2 * RIM
    tiles = width // tall
    me = lax.axis_index("ctx")
    backward = lax.rem(me, 2)
    across = me // (count // 2)
    for at in range(count):
        tails[RIM * at : RIM * (at + 1), :] = got_ref[at, width : width + RIM, :].astype(F32)
    shape = (lanes, tiles * lanes)
    head = iota(shape, 1) // head_dim + across * (tiles * lanes // head_dim)
    chosen = jnp.where(iota(shape, 0) == head, 1.0, 0.0).astype(BF16)
    carries[...] = dot(tails[...].astype(BF16), chosen, ((1,), (0,)))
    states = [jnp.zeros((tall, lanes), F32) for _ in range(tiles)]
    sent = []
    pieces = sems.shape[0]
    group = count // pieces
    for step in range(count):
        at = jnp.where(backward == 1, count - 1 - step, step)
        carry = carries[pl.ds(pl.multiple_of(at * RIM, RIM), RIM), :]
        carry = carry[0:1] + carry[1:2]
        for tile in range(tiles):
            rows = slice(tile * tall, (tile + 1) * tall)
            out_ref[at, rows, :] = states[tile].astype(BF16)
            states[tile] = carry[:, lanes_of(tile)] * states[tile] + got_ref[at, rows, :].astype(F32)
        if step % group == group - 1:
            first = jnp.where(backward == 1, count - 1 - step, step + 1 - group)
            sent.append(put(out_ref, out_hbm, sems.at[step // group], (pl.ds(first, group),)))
    for copy in sent:
        copy.wait()


def intra_kernel(
    head_dim, doc_ref, a_log_ref, skip_ref, x_hbm, dy_hbm, bc_hbm, halo_ref, wx_ref, wbc_ref, dt_ref,
    gs_hbm, ls_hbm, yi_ref,
    lx_ref, edy_ref, bcc_ref, gbc_ref, sbc_ref, hv_ref, rim_ref,
    x_ref, dy_ref, bc_ref, gs_ref, ls_ref, ext, bias, dgram,
    x_sems, dy_sems, bc_sems, out_sems,
):
    rows, channels = x_ref.shape
    heads = dt_ref.shape[0]
    doc = doc_ref[0]
    bc_in = fetch(bc_hbm, bc_ref, bc_sems)
    x_in = fetch(x_hbm, x_ref, x_sems)
    dy_in = fetch(dy_hbm, dy_ref, dy_sems)
    v = head_values(doc_ref, a_log_ref, dt_ref)
    for half in range(2):
        lanes = lanes_of(half)
        arrived(bc_in, half)
        load_ext(ext, halo_ref, bc_ref, lanes_of(channels // LANES + half), lanes)
        pre = filtered(ext, wbc_ref, channels + half * LANES, half * LANES, rows)
        gate = sigmoid(pre)
        bcc_ref[:, lanes] = (pre * gate).astype(BF16)
        sbc_ref[:, lanes] = gate * (1.0 + pre * (1.0 - gate))
    b_matrix = bcc_ref[:, 0:LANES]
    c_matrix = bcc_ref[:, LANES:]
    gram = dot(c_matrix, b_matrix, ((1,), (1,)))
    t_at, s_at = iota((rows, rows), 0), iota((rows, rows), 1)
    bias[...] = jnp.where((t_at >= s_at) & ((t_at >= doc) == (s_at >= doc)), 0.0, -1e30)
    dgram[...] = jnp.zeros_like(dgram)
    downto = jnp.where(t_at >= s_at, 1.0, 0.0)
    cum = v["cum"]
    cum_t = dot(downto, v["drop"], ((1,), (1,)), HIGHEST)
    skip = per_head(skip_ref, heads, rows)
    leave_step = columns(v["leaving"] * v["step"])
    entering, steps = columns(v["entering"]), columns(v["step"])
    skip = columns(skip)
    along_dt = jnp.zeros((heads, rows), F32)
    z_diff = jnp.zeros((heads, rows), F32)
    low_half = iota((rows, LANES), 1) < head_dim
    sent = []
    for slab in range(channels // LANES):
        lanes = lanes_of(slab)
        arrived(x_in, slab)
        load_ext(ext, halo_ref, x_ref, lanes, lanes)
        arrived(dy_in, slab)
        pre = filtered(ext, wx_ref, slab * LANES, slab * LANES, rows)
        gate = sigmoid(pre)
        x_bf = (pre * gate).astype(BF16)
        silu_grad = gate * (1.0 + pre * (1.0 - gate))
        x_conv = x_bf.astype(F32)
        step = spread(steps, slab, head_dim)
        leave = spread(leave_step, slab, head_dim)
        enter = spread(entering, slab, head_dim)
        skips = spread(skip, slab, head_dim)
        dy_bf = dy_ref[:, lanes]
        dy = dy_bf.astype(F32)
        lx_ref[:, lanes] = (x_conv * leave).astype(BF16)
        edy_ref[:, lanes] = (dy * enter).astype(BF16)
        scaled = (x_conv * step).astype(BF16)
        intra = jnp.zeros((rows, LANES), F32)
        d_scaled = jnp.zeros((rows, LANES), F32)
        for side in range(LANES // head_dim):
            head = slab * (LANES // head_dim) + side
            mine = low_half if side == 0 else jnp.logical_not(low_half)
            scaled_h = jnp.where(mine, scaled.astype(F32), 0.0).astype(BF16)
            dy_h = jnp.where(mine, dy, 0.0).astype(BF16)
            kernel = jnp.exp((cum_t[:, head : head + 1] - cum[head : head + 1, :]) + bias[...])
            mixing = (gram * kernel).astype(BF16)
            response = dot(dy_h, scaled, ((1,), (1,)))
            dgram[...] += response * kernel
            intra = intra + dot(mixing, scaled_h, ((1,), (0,)))
            d_scaled = d_scaled + dot(mixing, dy_h, ((0,), (0,)))
        yi_ref[:, lanes] = intra + skips * x_conv
        gs_ref[:, lanes] = (step * d_scaled + skips * dy) * silu_grad
        ls_ref[:, lanes] = leave * silu_grad
        rim_ref[0, :, lanes] = gs_ref[0:RIM, lanes]
        rim_ref[1, :, lanes] = ls_ref[0:RIM, lanes]
        group = channels // LANES // (out_sems.shape[0] // 2)
        if slab % group == group - 1:
            at = (slice(None), slice((slab + 1 - group) * LANES, (slab + 1) * LANES))
            sent.append(put(gs_ref, gs_hbm, out_sems.at[slab // group * 2], at))
            sent.append(put(ls_ref, ls_hbm, out_sems.at[slab // group * 2 + 1], at))
        along_dt = along_dt + head_sum(x_conv * d_scaled, slab, head_dim, heads)
        z_diff = z_diff + head_sum(
            dy * intra - scaled.astype(F32) * d_scaled, slab, head_dim, heads
        )
    d_gram = dgram[...]
    gbc_ref[:, 0:LANES] = dot(d_gram, c_matrix.astype(F32), ((0,), (0,)), HIGHEST)
    gbc_ref[:, LANES:] = dot(d_gram, b_matrix.astype(F32), ((1,), (0,)), HIGHEST)
    small = [
        v["step"],
        v["entering"],
        along_dt,
        z_diff,
        v["carry"],
        v["decay"],
        1.0 / (1.0 + jnp.exp(-dt_ref[...])),
    ]
    for at, values in enumerate(small):
        hv_ref[at] = values
    for copy in sent:
        copy.wait()


def state_of(st_ref, which, slab):
    tall = 2 * RIM
    tiles = st_ref.shape[1] // tall
    across, tile = slab // tiles, slab % tiles
    sides = LANES // tall
    rows = slice(tile * tall, (tile + 1) * tall)
    return jnp.concatenate(
        [st_ref[chunk_of(across, side, which), rows, :] for side in range(sides)], axis=0
    )


def bc_kernel(
    core_ref, st_ref, lx_ref, edy_ref, b_ref, gbc_ref, sbc_ref, rim_ref, wbc_ref,
    keep_ref, give_ref, halo_ref, ext, total,
):
    rows = lx_ref.shape[0]
    taps = wbc_ref.shape[0]
    slabs = lx_ref.shape[1] // LANES
    state, dstate = [
        jnp.concatenate([state_of(st_ref, which, slab) for slab in range(slabs)], axis=1)
        for which in range(2)
    ]
    grad_b = gbc_ref[:, 0:LANES] + dot(lx_ref[...], dstate, ((1,), (1,)))
    grad_c = gbc_ref[:, LANES:] + dot(edy_ref[...], state, ((1,), (1,)))
    ext[0:rows, 0:LANES] = grad_b * sbc_ref[:, 0:LANES]
    ext[0:rows, LANES:] = grad_c * sbc_ref[:, LANES:]
    ext[rows:, :] = jnp.zeros((RIM, 2 * LANES), F32)
    w = wbc_ref[...].astype(F32)
    out = w[taps - 1 : taps] * ext[0:rows, :]
    for tap in range(taps - 1):
        out = out + w[tap : tap + 1] * ext[pl.ds(taps - 1 - tap, rows), :]
    total[...] = out
    half = rows // 2
    core = core_ref[0]
    keep_ref[...] = total[pl.ds(pl.multiple_of(core * half, half), half), :]
    give_ref[...] = total[pl.ds(pl.multiple_of((1 - core) * half, half), half), :].astype(BF16)
    d_leaving = dot(b_ref[0 : 2 * RIM, 0:LANES], dstate, ((1,), (0,)))[0:RIM]
    channels = rim_ref.shape[2]
    halo_ref[:, 0:channels] = rim_ref[0] + rim_ref[1] * d_leaving
    halo_ref[:, channels:] = ext[0:RIM, :]


def join_kernel(keep_ref, got_ref, halo_ref, wbc_ref, out_ref, ext):
    half = keep_ref.shape[0]
    taps = wbc_ref.shape[0]
    wide = keep_ref.shape[1]
    out_ref[0:half, :] = (keep_ref[...] + got_ref[...].astype(F32)).astype(BF16)
    ext[0:RIM, :] = jnp.zeros((RIM, wide), F32)
    ext[RIM:, :] = halo_ref[:, halo_ref.shape[1] - wide :]
    w = wbc_ref[...].astype(F32)
    rim = jnp.zeros((RIM, wide), F32)
    for tap in range(taps - 1):
        rim = rim + w[tap : tap + 1] * ext[pl.ds(taps - 1 - tap, RIM), :]
    out_ref[half:, :] = rim.astype(BF16)


def sum_kernel(*refs):
    out_ref = refs[-1]
    total = refs[0][...].astype(F32)
    for ref in refs[1:-1]:
        total = total + ref[...].astype(F32)
    out_ref[...] = total.astype(BF16)


def last_kernel(core_ref, mine_ref, got_ref, out_ref, total):
    rows = out_ref.shape[0]
    half = rows // 2
    core = core_ref[0]
    total[pl.ds(pl.multiple_of(core * half, half), half), :] = mine_ref[0:half, :].astype(F32)
    total[pl.ds(pl.multiple_of((1 - core) * half, half), half), :] = got_ref[0:half, :].astype(F32)
    total[rows - RIM :, :] += mine_ref[half:, :].astype(F32) + got_ref[half:, :].astype(F32)
    out_ref[...] = total[...].astype(BF16)


def y_kernel(head_dim, st_ref, bcc_ref, hv_ref, yi_ref, edy_ref, y_hbm, enter_ref, y_ref, ys_ref, sems):
    rows, channels = edy_ref.shape
    heads = hv_ref.shape[1]
    slabs = channels // LANES
    group = slabs // sems.shape[0]
    c_matrix = bcc_ref[:, LANES:]
    entering = columns(hv_ref[1])
    sent = []
    for slab in range(slabs):
        lanes = lanes_of(slab)
        y_state = dot(c_matrix, state_of(st_ref, 0, slab), ((1,), (0,)))
        ys_ref[:, lanes] = y_state
        y_ref[:, lanes] = (yi_ref[:, lanes] + spread(entering, slab, head_dim) * y_state).astype(BF16)
        if slab % group == group - 1:
            at = (slice(None), slice((slab + 1 - group) * LANES, (slab + 1) * LANES))
            sent.append(put(y_ref, y_hbm, sems.at[slab // group], at))
    enter_term = jnp.zeros((heads, rows), F32)
    for slab in range(slabs):
        lanes = lanes_of(slab)
        enter_term = enter_term + head_sum(
            edy_ref[:, lanes].astype(F32) * ys_ref[:, lanes], slab, head_dim, heads
        )
    enter_ref[...] = enter_term
    for copy in sent:
        copy.wait()


def x_kernel(
    head_dim, gs_hbm, ls_hbm, st_ref, bcc_ref, hv_ref, lx_ref, enter_ref, halo_ref, wx_ref,
    gx_hbm, gdt_ref, gs_ref, ls_ref, gx_ref, ext, gs_sems, ls_sems, sems,
):
    rows, channels = lx_ref.shape
    heads = hv_ref.shape[1]
    taps = wx_ref.shape[0]
    slabs = channels // LANES
    group = slabs // sems.shape[0]
    gs_in = fetch(gs_hbm, gs_ref, gs_sems)
    ls_in = fetch(ls_hbm, ls_ref, ls_sems)
    b_matrix = bcc_ref[:, 0:LANES]
    step, _, along_dt, z_diff, carry, decay, dt_gate = [hv_ref[at] for at in range(7)]
    leave_term = jnp.zeros((heads, rows), F32)
    overlap = jnp.zeros((heads, LANES), F32)
    for slab in range(slabs):
        lanes = lanes_of(slab)
        dstate = state_of(st_ref, 1, slab)
        product = state_of(st_ref, 0, slab).astype(F32) * dstate.astype(F32)
        head = iota((heads, LANES), 1) // head_dim + slab * (LANES // head_dim)
        own = iota((heads, LANES), 0) == head
        overlap = overlap + jnp.where(own, jnp.sum(product, axis=0, keepdims=True), 0.0)
        d_leaving = dot(b_matrix, dstate, ((1,), (0,)))
        ext[0:rows, lanes] = d_leaving
        leave_term = leave_term + head_sum(
            lx_ref[:, lanes].astype(F32) * d_leaving, slab, head_dim, heads
        )
    final = jnp.sum(leave_term, axis=1, keepdims=True) + carry * jnp.sum(overlap, axis=1, keepdims=True)
    d_cum = z_diff + enter_ref[...] - leave_term
    d_cum = d_cum + jnp.where(iota((heads, rows), 1) == rows - 1, final, 0.0)
    after = jnp.where(iota((rows, rows), 0) >= iota((rows, rows), 1), 1.0, 0.0)
    d_log = dot(d_cum, after, ((1,), (0,)), HIGHEST)
    gdt_ref[...] = (along_dt + leave_term / step - decay * d_log) * dt_gate
    ext[rows:, :] = halo_ref[:, 0:channels]
    sent = []
    for slab in range(slabs):
        lanes = lanes_of(slab)
        arrived(gs_in, slab)
        arrived(ls_in, slab)
        ext[0:rows, lanes] = gs_ref[:, lanes] + ls_ref[:, lanes] * ext[0:rows, lanes]
        w = wx_ref[:, lanes].astype(F32)
        out = w[taps - 1 : taps] * ext[0:rows, lanes]
        for tap in range(taps - 1):
            out = out + w[tap : tap + 1] * ext[pl.ds(taps - 1 - tap, rows), lanes]
        gx_ref[:, lanes] = out.astype(BF16)
        if slab % group == group - 1:
            at = (slice(None), slice((slab + 1 - group) * LANES, (slab + 1) * LANES))
            sent.append(put(gx_ref, gx_hbm, sems.at[slab // group], at))
    for copy in sent:
        copy.wait()


def smem():
    return pl.BlockSpec(memory_space=pltpu.SMEM)


def vmem():
    return pl.BlockSpec(memory_space=pltpu.VMEM)


def hbm():
    return pl.BlockSpec(memory_space=pltpu.HBM)


def call(kernel, name, scalars, far, near, far_out, near_out, scratch=()):
    far = [pltpu.with_memory_space_constraint(a, pltpu.HBM) for a in far]
    out = [pltpu.HBM(s, d) for s, d in far_out] + [jax.ShapeDtypeStruct(s, d) for s, d in near_out]
    specs = [hbm() for _ in far_out] + [vmem() for _ in near_out]
    many = len(out) > 1
    return pl.pallas_call(
        kernel,
        name=name,
        out_shape=out if many else out[0],
        in_specs=[smem() for _ in scalars] + [hbm() for _ in far] + [vmem() for _ in near],
        out_specs=specs if many else specs[0],
        scratch_shapes=list(scratch),
        compiler_params=pltpu.CompilerParams(vmem_limit_bytes=VMEM_LIMIT),
    )(*scalars, *far, *near)


def shift_ctx(values, by):
    size = lax.axis_size("ctx")
    pairs = [(i, i + by) for i in range(size) if 0 <= i + by < size]
    return lax.ppermute(values, "ctx", pairs)


def swap_core(values):
    size = lax.axis_size("head")
    return lax.ppermute(values, "head", [(i, i ^ 1) for i in range(size)])


def around(values, by):
    size = lax.axis_size("head")
    return lax.ppermute(values, "head", [(i, (i + 2 * by) % size) for i in range(size)])


def body(x_raw, bc_raw, conv_x_w, conv_bc_w, dt_raw, a_log, d_skip, doc_starts, grad_y):
    rows, channels = x_raw.shape
    heads = a_log.shape[0]
    head_dim = channels // heads
    wide = bc_raw.shape[1]
    count = lax.axis_size("ctx")
    part = channels // count
    core = (lax.axis_index("head") % 2).astype(jnp.int32).reshape(1)
    halo = shift_ctx(jnp.concatenate([x_raw[rows - RIM :], bc_raw[rows - RIM :]], axis=1), 1)
    wide_bf, wide_f = ((rows, channels), BF16), ((rows, channels), F32)
    sems = pltpu.SemaphoreType.DMA
    two = sems((2,))
    inputs = [pltpu.VMEM(*wide_bf), pltpu.VMEM(*wide_bf), pltpu.VMEM((rows, wide), BF16)]
    input_sems = [two, two, sems((1,))]
    ext = pltpu.VMEM((rows + RIM, channels + wide), F32)
    sent = ((count, 2 * part + RIM, LANES), BF16)
    states = ((count, 2 * part, LANES), BF16)
    sums, leave_top, dy_top, top, tail = call(
        functools.partial(gather_kernel, head_dim),
        "gather",
        [doc_starts, a_log],
        [x_raw, grad_y, bc_raw],
        [conv_x_w, conv_bc_w, dt_raw],
        [],
        [
            ((2, LANES, channels), F32),
            ((RIM, channels), F32),
            ((RIM, channels), F32),
            ((RIM, channels + wide), F32),
            ((RIM, LANES), BF16),
        ],
        [*inputs, ext, *input_sems],
    )
    send = call(
        send_kernel,
        "send",
        [],
        [],
        [halo, sums, leave_top, dy_top, top, tail, conv_x_w, conv_bc_w],
        [],
        [sent],
        [pltpu.VMEM((2 * RIM, channels + wide), F32)],
    )
    got = lax.all_to_all(send, "ctx", 0, 0)
    scanned = call(
        functools.partial(scan_kernel, head_dim),
        "scan",
        [],
        [],
        [got],
        [states],
        [],
        [
            pltpu.VMEM(*states),
            pltpu.VMEM((count * RIM, LANES), F32),
            pltpu.VMEM((count * RIM, channels // 2), F32),
            sems((4,)),
        ],
    )
    scanned, dt_later = lax.optimization_barrier((scanned, dt_raw))
    gs, ls, yi, lx, edy, bcc, gbc, sbc, hv, first = call(
        functools.partial(intra_kernel, head_dim),
        "intra",
        [doc_starts, a_log, d_skip],
        [x_raw, grad_y, bc_raw],
        [halo, conv_x_w, conv_bc_w, dt_later],
        [wide_f, wide_f],
        [
            wide_f,
            wide_bf,
            wide_bf,
            ((rows, wide), BF16),
            ((rows, wide), F32),
            ((rows, wide), F32),
            ((7, heads, rows), F32),
            ((2, RIM, channels), F32),
        ],
        [
            *inputs,
            pltpu.VMEM(*wide_f),
            pltpu.VMEM(*wide_f),
            ext,
            pltpu.VMEM((rows, rows), F32),
            pltpu.VMEM((rows, rows), F32),
            *input_sems,
            sems((4,)),
        ],
    )
    st = lax.all_to_all(scanned, "ctx", 0, 0)
    half = rows // 2
    keep, give, rim = call(
        bc_kernel,
        "grad_bc",
        [core],
        [],
        [st, lx, edy, bcc, gbc, sbc, first, conv_bc_w],
        [],
        [
            ((half, wide), F32),
            ((half, wide), BF16),
            ((RIM, channels + wide), F32),
        ],
        [pltpu.VMEM((rows + RIM, wide), F32), pltpu.VMEM((rows, wide), F32)],
    )
    next_rim = shift_ctx(rim, -1)
    other = swap_core(give)
    st, keep = lax.optimization_barrier((st, keep))
    y_out, enter_term = call(
        functools.partial(y_kernel, head_dim),
        "y_out",
        [],
        [],
        [st, bcc, hv, yi, edy],
        [wide_bf],
        [((heads, rows), F32)],
        [pltpu.VMEM(*wide_bf), pltpu.VMEM(*wide_f), two],
    )
    other, next_rim, enter_term = lax.optimization_barrier((other, next_rim, enter_term))
    message = ((half + RIM, wide), BF16)
    joined = call(
        join_kernel,
        "join",
        [],
        [],
        [keep, other, next_rim, conv_bc_w],
        [],
        [message],
        [pltpu.VMEM((2 * RIM, wide), F32)],
    )
    ring = lax.axis_size("head") // 2
    pieces = [joined] + [around(joined, by) for by in range(1, ring)]
    grad_x, grad_dt = call(
        functools.partial(x_kernel, head_dim),
        "grad_x",
        [],
        [gs, ls],
        [st, bcc, hv, lx, enter_term, next_rim, conv_x_w],
        [wide_bf],
        [((heads, rows), F32)],
        [
            pltpu.VMEM(*wide_f),
            pltpu.VMEM(*wide_f),
            pltpu.VMEM(*wide_bf),
            pltpu.VMEM((rows + RIM, channels), F32),
            two,
            two,
            two,
        ],
    )
    pieces, grad_dt = lax.optimization_barrier((pieces, grad_dt))
    summed = call(sum_kernel, "sum", [], [], pieces, [], [message])
    swapped = swap_core(summed)
    grad_bc = call(
        last_kernel,
        "last",
        [core],
        [],
        [summed, swapped],
        [],
        [((rows, wide), BF16)],
        [pltpu.VMEM((rows, wide), F32)],
    )
    return (y_out, grad_x, grad_bc, grad_dt)


def solution(mesh):
    in_specs = (
        P("ctx", "head"),
        P("ctx", None),
        P(None, "head"),
        P(),
        P("head", "ctx"),
        P("head"),
        P("head"),
        P("ctx"),
        P("ctx", "head"),
    )
    out_specs = (P("ctx", "head"), P("ctx", "head"), P("ctx", None), P("head", "ctx"))
    return jax.shard_map(body, mesh=mesh, in_specs=in_specs, out_specs=out_specs, check_vma=False)
```

```python
import functools

import jax
import jax.numpy as jnp
from jax import lax
from jax.experimental import pallas as pl
from jax.experimental.pallas import tpu as pltpu
from jax.sharding import PartitionSpec as P

F32 = jnp.float32
BF16 = jnp.bfloat16
LANES = 128
RIM = 8
VMEM_LIMIT = 24 * 1024 * 1024
HIGHEST = lax.Precision.HIGHEST


def dot(a, b, dims, precision=None):
    return lax.dot_general(a, b, (dims, ((), ())), precision=precision, preferred_element_type=F32)


def iota(shape, axis):
    return lax.broadcasted_iota(jnp.int32, shape, axis)


def halves(values):
    high = values.astype(BF16)
    return high, (values - high.astype(F32)).astype(BF16)


def sigmoid(values):
    return 0.5 * jnp.tanh(0.5 * values) + 0.5


def diagonal(size):
    return jnp.where(iota((size, size), 0) == iota((size, size), 1), 1.0, 0.0).astype(BF16)


def columns(values):
    both = jnp.concatenate(halves(values), axis=0)
    return dot(diagonal(values.shape[1]), both, ((1,), (1,))).astype(BF16)


def spread(pairs, slab, head_dim, width=LANES):
    heads = pairs.shape[1] // 2
    row = iota((2 * heads, width), 0)
    head = iota((2 * heads, width), 1) // head_dim + slab * (width // head_dim)
    chosen = jnp.where((row == head) | (row == head + heads), 1.0, 0.0).astype(BF16)
    return dot(pairs, chosen, ((1,), (0,)))


def head_sum(values, slab, head_dim, heads):
    width = values.shape[1]
    head = (iota((heads, width), 1) % LANES) // head_dim + slab * (LANES // head_dim)
    chosen = jnp.where(iota((heads, width), 0) == head, 1.0, 0.0).astype(BF16)
    return dot(chosen, values.astype(BF16), ((1,), (1,)))


def head_sum_exact(values, slab, head_dim, heads):
    return head_sum(jnp.concatenate(halves(values), axis=1), slab, head_dim, heads)


def per_head(ref, heads, rows):
    at = iota((heads, rows), 0)
    values = jnp.zeros((heads, rows), F32)
    for head in range(heads):
        values = jnp.where(at == head, ref[head], values)
    return values


def head_values(doc_ref, a_log_ref, dt_ref):
    heads, rows = dt_ref.shape
    doc = doc_ref[0]
    raw = dt_ref[...]
    step = jnp.maximum(raw, 0.0) + jnp.log(1.0 + jnp.exp(-jnp.abs(raw)))
    decay = jnp.exp(per_head(a_log_ref, heads, rows))
    upto = jnp.where(iota((rows, rows), 0) <= iota((rows, rows), 1), 1.0, 0.0)
    drop = -decay * step
    cum = dot(drop, upto, ((1,), (0,)), HIGHEST)
    final = cum[:, rows - 1 :]
    segment = iota((heads, rows), 1) >= doc
    entering = jnp.where(segment, 0.0, jnp.exp(cum))
    outside = jnp.logical_and(iota((heads, rows), 1) < doc, doc < rows)
    leaving = jnp.where(outside, 0.0, jnp.exp(final - cum))
    carry = jnp.where(doc >= rows, jnp.exp(jnp.broadcast_to(final, (heads, rows))), 0.0)
    return dict(
        step=step, decay=decay, drop=drop, cum=cum, entering=entering, leaving=leaving, carry=carry
    )


def lanes_of(slab):
    return slice(slab * LANES, (slab + 1) * LANES)


def fetch(source, target, sems):
    pieces = sems.shape[0]
    width = source.shape[1] // pieces
    copies = {}
    for piece in range(pieces):
        at = (slice(None), slice(piece * width, (piece + 1) * width))
        copy = pltpu.make_async_copy(source.at[at], target.at[at], sems.at[piece])
        copy.start()
        copies[piece * width // LANES] = copy
    return copies


def arrived(copies, slab):
    if slab in copies:
        copies[slab].wait()


def put(source, target, sem, at):
    copy = pltpu.make_async_copy(source.at[at], target.at[at], sem)
    copy.start()
    return copy


def load_ext(ext, halo_ref, values, at, lanes):
    if halo_ref is None:
        ext[0:RIM, at] = jnp.zeros((RIM, at.stop - at.start), F32)
    else:
        ext[0:RIM, at] = halo_ref[:, at].astype(F32)
    ext[RIM : RIM + values.shape[0], at] = values[:, lanes].astype(F32)


def filtered(ext, w_ref, at, w_at, rows, width=LANES):
    taps = w_ref.shape[0]
    lanes = pl.ds(at, width)
    w = w_ref[:, w_at : w_at + width].astype(F32)
    total = w[0:1] * ext[pl.ds(RIM - taps + 1, rows), lanes]
    for tap in range(1, taps):
        total = total + w[tap : tap + 1] * ext[pl.ds(RIM - taps + 1 + tap, rows), lanes]
    return total


def gather_kernel(
    head_dim, doc_ref, a_log_ref, x_hbm, dy_hbm, bc_hbm, wx_ref, wbc_ref, dt_ref,
    sum_ref, ls_ref, edy_ref, top_ref, tail_ref,
    x_ref, dy_ref, bc_ref, ext, x_sems, dy_sems, bc_sems,
):
    rows, channels = x_ref.shape
    bc_in = fetch(bc_hbm, bc_ref, bc_sems)
    x_in = fetch(x_hbm, x_ref, x_sems)
    dy_in = fetch(dy_hbm, dy_ref, dy_sems)
    v = head_values(doc_ref, a_log_ref, dt_ref)
    leave_step = columns(v["leaving"] * v["step"])
    entering = columns(v["entering"])
    heads = dt_ref.shape[0]
    own = iota((heads, LANES), 0) == iota((heads, LANES), 1)
    carry = jnp.sum(jnp.where(own, v["carry"][:, 0:LANES], 0.0), axis=0, keepdims=True)
    high, low = [half.astype(F32) for half in halves(carry)]
    at = iota((RIM, LANES), 0)
    tail_ref[...] = jnp.where(at == 0, high, jnp.where(at == 1, low, 0.0)).astype(BF16)
    bc = []
    for half in range(2):
        arrived(bc_in, half)
        load_ext(ext, None, bc_ref, lanes_of(channels // LANES + half), lanes_of(half))
        pre = filtered(ext, wbc_ref, channels + half * LANES, half * LANES, rows)
        bc.append((pre * sigmoid(pre)).T.astype(BF16))
    width = LANES
    below = iota((rows, width), 0) >= RIM
    for slab in range(channels // width):
        lanes = slice(slab * width, (slab + 1) * width)
        arrived(x_in, slab)
        load_ext(ext, None, x_ref, lanes, lanes)
        pre = filtered(ext, wx_ref, slab * width, slab * width, rows, width)
        x_conv = (pre * sigmoid(pre)).astype(BF16).astype(F32)
        leave = spread(leave_step, slab, head_dim, width)
        leaving_x = jnp.where(below, x_conv * leave, 0.0).astype(BF16)
        sum_ref[0, :, lanes] = dot(bc[0], leaving_x, ((1,), (0,)))
        arrived(dy_in, slab)
        enter_dy = dy_ref[:, lanes].astype(F32) * spread(entering, slab, head_dim, width)
        masked = jnp.where(below, enter_dy, 0.0).astype(BF16)
        sum_ref[1, :, lanes] = dot(bc[1], masked, ((1,), (0,)))
        ls_ref[:, lanes] = leave[0:RIM]
        edy_ref[:, lanes] = enter_dy[0:RIM]
    top_ref[...] = ext[RIM : 2 * RIM, :]


def chunk_of(across, side, which):
    return 16 * across + 2 * side + which


def send_kernel(
    halo_ref, sum_ref, ls_ref, edy_ref, top_ref, tail_ref, wx_ref, wbc_ref, send_ref, ext,
):
    channels = ls_ref.shape[1]
    count = send_ref.shape[0]
    tall = 2 * RIM
    ext[0:RIM, :] = halo_ref[...].astype(F32)
    ext[RIM:, :] = top_ref[...]
    none = jnp.zeros((RIM, LANES), F32)

    def conv(w_ref, at, w_at):
        pre = filtered(ext, w_ref, at, w_at, RIM)
        return (pre * sigmoid(pre)).astype(BF16).astype(F32)

    bc = []
    for at in (0, LANES):
        top = jnp.concatenate([conv(wbc_ref, channels + at, at), none], axis=0).astype(BF16)
        bc.append(dot(top, diagonal(tall), ((0,), (0,))).astype(BF16))
    tail = tail_ref[...]
    for chunk in range(count):
        send_ref[chunk, send_ref.shape[1] - RIM :, :] = tail
    slabs = channels // LANES
    for slab in range(slabs):
        lanes = lanes_of(slab)
        across, tile = slab // (slabs // 2), slab % (slabs // 2)
        leaving_x = conv(wx_ref, slab * LANES, slab * LANES) * ls_ref[:, lanes]
        enter_dy = edy_ref[:, lanes]
        for which, top in enumerate((leaving_x, enter_dy)):
            top = jnp.concatenate([top, none], axis=0).astype(BF16)
            total = (sum_ref[which, :, lanes] + dot(bc[which], top, ((1,), (0,)))).astype(BF16)
            for side in range(LANES // tall):
                piece = total[side * tall : (side + 1) * tall]
                send_ref[chunk_of(across, side, which), tile * tall : (tile + 1) * tall, :] = piece


def scan_kernel(head_dim, got_ref, out_hbm, out_ref, tails, carries, sems):
    count, width, lanes = out_ref.shape
    tall = 2 * RIM
    tiles = width // tall
    me = lax.axis_index("ctx")
    backward = lax.rem(me, 2)
    across = me // (count // 2)
    for at in range(count):
        tails[RIM * at : RIM * (at + 1), :] = got_ref[at, width : width + RIM, :].astype(F32)
    shape = (lanes, tiles * lanes)
    head = iota(shape, 1) // head_dim + across * (tiles * lanes // head_dim)
    chosen = jnp.where(iota(shape, 0) == head, 1.0, 0.0).astype(BF16)
    carries[...] = dot(tails[...].astype(BF16), chosen, ((1,), (0,)))
    states = [jnp.zeros((tall, lanes), F32) for _ in range(tiles)]
    sent = []
    pieces = sems.shape[0]
    group = count // pieces
    for step in range(count):
        at = jnp.where(backward == 1, count - 1 - step, step)
        carry = carries[pl.ds(pl.multiple_of(at * RIM, RIM), RIM), :]
        carry = carry[0:1] + carry[1:2]
        for tile in range(tiles):
            rows = slice(tile * tall, (tile + 1) * tall)
            out_ref[at, rows, :] = states[tile].astype(BF16)
            states[tile] = carry[:, lanes_of(tile)] * states[tile] + got_ref[at, rows, :].astype(F32)
        if step % group == group - 1:
            first = jnp.where(backward == 1, count - 1 - step, step + 1 - group)
            sent.append(put(out_ref, out_hbm, sems.at[step // group], (pl.ds(first, group),)))
    for copy in sent:
        copy.wait()


def intra_kernel(
    head_dim, doc_ref, a_log_ref, skip_ref, x_hbm, dy_hbm, bc_hbm, halo_ref, wx_ref, wbc_ref, dt_ref,
    gs_hbm, ls_hbm, yi_ref,
    lx_ref, edy_ref, bcc_ref, gbc_ref, sbc_ref, hv_ref, rim_ref,
    x_ref, dy_ref, bc_ref, gs_ref, ls_ref, ext, bias, dgram,
    x_sems, dy_sems, bc_sems, out_sems,
):
    rows, channels = x_ref.shape
    heads = dt_ref.shape[0]
    doc = doc_ref[0]
    bc_in = fetch(bc_hbm, bc_ref, bc_sems)
    x_in = fetch(x_hbm, x_ref, x_sems)
    dy_in = fetch(dy_hbm, dy_ref, dy_sems)
    v = head_values(doc_ref, a_log_ref, dt_ref)
    for half in range(2):
        lanes = lanes_of(half)
        arrived(bc_in, half)
        load_ext(ext, halo_ref, bc_ref, lanes_of(channels // LANES + half), lanes)
        pre = filtered(ext, wbc_ref, channels + half * LANES, half * LANES, rows)
        gate = sigmoid(pre)
        bcc_ref[:, lanes] = (pre * gate).astype(BF16)
        sbc_ref[:, lanes] = gate * (1.0 + pre * (1.0 - gate))
    b_matrix = bcc_ref[:, 0:LANES]
    c_matrix = bcc_ref[:, LANES:]
    gram = dot(c_matrix, b_matrix, ((1,), (1,)))
    t_at, s_at = iota((rows, rows), 0), iota((rows, rows), 1)
    bias[...] = jnp.where((t_at >= s_at) & ((t_at >= doc) == (s_at >= doc)), 0.0, -1e30)
    dgram[...] = jnp.zeros_like(dgram)
    downto = jnp.where(t_at >= s_at, 1.0, 0.0)
    cum = v["cum"]
    cum_t = dot(downto, v["drop"], ((1,), (1,)), HIGHEST)
    skip = per_head(skip_ref, heads, rows)
    leave_step = columns(v["leaving"] * v["step"])
    entering, steps = columns(v["entering"]), columns(v["step"])
    skip = columns(skip)
    along_dt = jnp.zeros((heads, rows), F32)
    z_diff = jnp.zeros((heads, rows), F32)
    low_half = iota((rows, LANES), 1) < head_dim
    sent = []
    for slab in range(channels // LANES):
        lanes = lanes_of(slab)
        arrived(x_in, slab)
        load_ext(ext, halo_ref, x_ref, lanes, lanes)
        arrived(dy_in, slab)
        pre = filtered(ext, wx_ref, slab * LANES, slab * LANES, rows)
        gate = sigmoid(pre)
        x_bf = (pre * gate).astype(BF16)
        silu_grad = gate * (1.0 + pre * (1.0 - gate))
        x_conv = x_bf.astype(F32)
        step = spread(steps, slab, head_dim)
        leave = spread(leave_step, slab, head_dim)
        enter = spread(entering, slab, head_dim)
        skips = spread(skip, slab, head_dim)
        dy_bf = dy_ref[:, lanes]
        dy = dy_bf.astype(F32)
        lx_ref[:, lanes] = (x_conv * leave).astype(BF16)
        edy_ref[:, lanes] = (dy * enter).astype(BF16)
        scaled = (x_conv * step).astype(BF16)
        intra = jnp.zeros((rows, LANES), F32)
        d_scaled = jnp.zeros((rows, LANES), F32)
        for side in range(LANES // head_dim):
            head = slab * (LANES // head_dim) + side
            mine = low_half if side == 0 else jnp.logical_not(low_half)
            scaled_h = jnp.where(mine, scaled.astype(F32), 0.0).astype(BF16)
            dy_h = jnp.where(mine, dy, 0.0).astype(BF16)
            kernel = jnp.exp((cum_t[:, head : head + 1] - cum[head : head + 1, :]) + bias[...])
            mixing = (gram * kernel).astype(BF16)
            response = dot(dy_h, scaled, ((1,), (1,)))
            dgram[...] += response * kernel
            intra = intra + dot(mixing, scaled_h, ((1,), (0,)))
            d_scaled = d_scaled + dot(mixing, dy_h, ((0,), (0,)))
        yi_ref[:, lanes] = intra + skips * x_conv
        gs_ref[:, lanes] = (step * d_scaled + skips * dy) * silu_grad
        ls_ref[:, lanes] = leave * silu_grad
        rim_ref[0, :, lanes] = gs_ref[0:RIM, lanes]
        rim_ref[1, :, lanes] = ls_ref[0:RIM, lanes]
        group = channels // LANES // (out_sems.shape[0] // 2)
        if slab % group == group - 1:
            at = (slice(None), slice((slab + 1 - group) * LANES, (slab + 1) * LANES))
            sent.append(put(gs_ref, gs_hbm, out_sems.at[slab // group * 2], at))
            sent.append(put(ls_ref, ls_hbm, out_sems.at[slab // group * 2 + 1], at))
        along_dt = along_dt + head_sum_exact(x_conv * d_scaled, slab, head_dim, heads)
        z_diff = z_diff + head_sum_exact(
            dy * intra - scaled.astype(F32) * d_scaled, slab, head_dim, heads
        )
    d_gram = dgram[...]
    gbc_ref[:, 0:LANES] = dot(d_gram, c_matrix.astype(F32), ((0,), (0,)), HIGHEST)
    gbc_ref[:, LANES:] = dot(d_gram, b_matrix.astype(F32), ((1,), (0,)), HIGHEST)
    small = [
        v["step"],
        v["entering"],
        along_dt,
        z_diff,
        v["carry"],
        v["decay"],
        1.0 / (1.0 + jnp.exp(-dt_ref[...])),
    ]
    for at, values in enumerate(small):
        hv_ref[at] = values
    for copy in sent:
        copy.wait()


def state_of(st_ref, which, slab):
    tall = 2 * RIM
    tiles = st_ref.shape[1] // tall
    across, tile = slab // tiles, slab % tiles
    sides = LANES // tall
    rows = slice(tile * tall, (tile + 1) * tall)
    return jnp.concatenate(
        [st_ref[chunk_of(across, side, which), rows, :] for side in range(sides)], axis=0
    )


def bc_kernel(
    core_ref, st_ref, lx_ref, edy_ref, b_ref, gbc_ref, sbc_ref, rim_ref, wbc_ref,
    keep_ref, give_ref, halo_ref, ext, total,
):
    rows = lx_ref.shape[0]
    taps = wbc_ref.shape[0]
    slabs = lx_ref.shape[1] // LANES
    state, dstate = [
        jnp.concatenate([state_of(st_ref, which, slab) for slab in range(slabs)], axis=1)
        for which in range(2)
    ]
    grad_b = gbc_ref[:, 0:LANES] + dot(lx_ref[...], dstate, ((1,), (1,)))
    grad_c = gbc_ref[:, LANES:] + dot(edy_ref[...], state, ((1,), (1,)))
    ext[0:rows, 0:LANES] = grad_b * sbc_ref[:, 0:LANES]
    ext[0:rows, LANES:] = grad_c * sbc_ref[:, LANES:]
    ext[rows:, :] = jnp.zeros((RIM, 2 * LANES), F32)
    w = wbc_ref[...].astype(F32)
    out = w[taps - 1 : taps] * ext[0:rows, :]
    for tap in range(taps - 1):
        out = out + w[tap : tap + 1] * ext[pl.ds(taps - 1 - tap, rows), :]
    total[...] = out
    half = rows // 2
    core = core_ref[0]
    keep_ref[...] = total[pl.ds(pl.multiple_of(core * half, half), half), :]
    give_ref[...] = total[pl.ds(pl.multiple_of((1 - core) * half, half), half), :].astype(BF16)
    d_leaving = dot(b_ref[0 : 2 * RIM, 0:LANES], dstate, ((1,), (0,)))[0:RIM]
    channels = rim_ref.shape[2]
    halo_ref[:, 0:channels] = rim_ref[0] + rim_ref[1] * d_leaving
    halo_ref[:, channels:] = ext[0:RIM, :]


def join_kernel(keep_ref, got_ref, halo_ref, wbc_ref, out_ref, ext):
    half = keep_ref.shape[0]
    taps = wbc_ref.shape[0]
    wide = keep_ref.shape[1]
    out_ref[0:half, :] = (keep_ref[...] + got_ref[...].astype(F32)).astype(BF16)
    ext[0:RIM, :] = jnp.zeros((RIM, wide), F32)
    ext[RIM:, :] = halo_ref[:, halo_ref.shape[1] - wide :]
    w = wbc_ref[...].astype(F32)
    rim = jnp.zeros((RIM, wide), F32)
    for tap in range(taps - 1):
        rim = rim + w[tap : tap + 1] * ext[pl.ds(taps - 1 - tap, RIM), :]
    out_ref[half:, :] = rim.astype(BF16)


def sum_kernel(*refs):
    out_ref = refs[-1]
    total = refs[0][...].astype(F32)
    for ref in refs[1:-1]:
        total = total + ref[...].astype(F32)
    out_ref[...] = total.astype(BF16)


def last_kernel(core_ref, mine_ref, got_ref, out_ref, total):
    rows = out_ref.shape[0]
    half = rows // 2
    core = core_ref[0]
    total[pl.ds(pl.multiple_of(core * half, half), half), :] = mine_ref[0:half, :].astype(F32)
    total[pl.ds(pl.multiple_of((1 - core) * half, half), half), :] = got_ref[0:half, :].astype(F32)
    total[rows - RIM :, :] += mine_ref[half:, :].astype(F32) + got_ref[half:, :].astype(F32)
    out_ref[...] = total[...].astype(BF16)


def y_kernel(head_dim, st_ref, bcc_ref, hv_ref, yi_ref, edy_ref, y_hbm, enter_ref, y_ref, ys_ref, sems):
    rows, channels = edy_ref.shape
    heads = hv_ref.shape[1]
    slabs = channels // LANES
    group = slabs // sems.shape[0]
    c_matrix = bcc_ref[:, LANES:]
    entering = columns(hv_ref[1])
    sent = []
    for slab in range(slabs):
        lanes = lanes_of(slab)
        y_state = dot(c_matrix, state_of(st_ref, 0, slab), ((1,), (0,)))
        ys_ref[:, lanes] = y_state
        y_ref[:, lanes] = (yi_ref[:, lanes] + spread(entering, slab, head_dim) * y_state).astype(BF16)
        if slab % group == group - 1:
            at = (slice(None), slice((slab + 1 - group) * LANES, (slab + 1) * LANES))
            sent.append(put(y_ref, y_hbm, sems.at[slab // group], at))
    enter_term = jnp.zeros((heads, rows), F32)
    for slab in range(slabs):
        lanes = lanes_of(slab)
        enter_term = enter_term + head_sum(
            edy_ref[:, lanes].astype(F32) * ys_ref[:, lanes], slab, head_dim, heads
        )
    enter_ref[...] = enter_term
    for copy in sent:
        copy.wait()


def xc_kernel(
    head_dim, gs_hbm, ls_hbm, st_ref, bcc_ref, lx_ref,
    g_ref, leave_ref, overlap_ref, gs_ref, ls_ref, gs_sems, ls_sems,
):
    rows, channels = lx_ref.shape
    heads = leave_ref.shape[0]
    slabs = channels // LANES
    gs_in = fetch(gs_hbm, gs_ref, gs_sems)
    ls_in = fetch(ls_hbm, ls_ref, ls_sems)
    b_matrix = bcc_ref[:, 0:LANES]
    leave_term = jnp.zeros((heads, rows), F32)
    overlap = jnp.zeros((heads, LANES), F32)
    for slab in range(slabs):
        lanes = lanes_of(slab)
        dstate = state_of(st_ref, 1, slab)
        product = state_of(st_ref, 0, slab).astype(F32) * dstate.astype(F32)
        head = iota((heads, LANES), 1) // head_dim + slab * (LANES // head_dim)
        own = iota((heads, LANES), 0) == head
        overlap = overlap + jnp.where(own, jnp.sum(product, axis=0, keepdims=True), 0.0)
        d_leaving = dot(b_matrix, dstate, ((1,), (0,)))
        g_ref[:, lanes] = d_leaving
        leave_term = leave_term + head_sum(
            lx_ref[:, lanes].astype(F32) * d_leaving, slab, head_dim, heads
        )
    leave_ref[...] = leave_term
    overlap_ref[...] = overlap
    for slab in range(slabs):
        lanes = lanes_of(slab)
        arrived(gs_in, slab)
        arrived(ls_in, slab)
        g_ref[:, lanes] = gs_ref[:, lanes] + ls_ref[:, lanes] * g_ref[:, lanes]


def x_kernel(g_ref, halo_ref, wx_ref, gx_hbm, gx_ref, ext, sems):
    rows, channels = g_ref.shape
    taps = wx_ref.shape[0]
    slabs = channels // LANES
    group = slabs // sems.shape[0]
    low = rows - RIM
    ext[0:RIM, :] = g_ref[low:, :]
    ext[RIM:, :] = halo_ref[:, 0:channels]
    sent = []
    for slab in range(slabs):
        lanes = lanes_of(slab)
        w = wx_ref[:, lanes].astype(F32)
        body = w[taps - 1 : taps] * g_ref[0:low, lanes]
        edge = w[taps - 1 : taps] * ext[0:RIM, lanes]
        for tap in range(taps - 1):
            ahead = taps - 1 - tap
            body = body + w[tap : tap + 1] * g_ref[pl.ds(ahead, low), lanes]
            edge = edge + w[tap : tap + 1] * ext[pl.ds(ahead, RIM), lanes]
        gx_ref[:, lanes] = jnp.concatenate([body, edge], axis=0).astype(BF16)
        if slab % group == group - 1:
            at = (slice(None), slice((slab + 1 - group) * LANES, (slab + 1) * LANES))
            sent.append(put(gx_ref, gx_hbm, sems.at[slab // group], at))
    for copy in sent:
        copy.wait()


def dt_kernel(hv_ref, enter_ref, leave_ref, overlap_ref, gdt_ref):
    heads, rows = leave_ref.shape
    step, _, along_dt, z_diff, carry, decay, dt_gate = [hv_ref[at] for at in range(7)]
    leave_term, overlap = leave_ref[...], overlap_ref[...]
    final = jnp.sum(leave_term, axis=1, keepdims=True) + carry * jnp.sum(overlap, axis=1, keepdims=True)
    d_cum = z_diff + enter_ref[...] - leave_term
    d_cum = d_cum + jnp.where(iota((heads, rows), 1) == rows - 1, final, 0.0)
    after = jnp.where(iota((rows, rows), 0) >= iota((rows, rows), 1), 1.0, 0.0)
    d_log = dot(d_cum, after, ((1,), (0,)), HIGHEST)
    gdt_ref[...] = (along_dt + leave_term / step - decay * d_log) * dt_gate


def smem():
    return pl.BlockSpec(memory_space=pltpu.SMEM)


def vmem():
    return pl.BlockSpec(memory_space=pltpu.VMEM)


def hbm():
    return pl.BlockSpec(memory_space=pltpu.HBM)


def call(kernel, name, scalars, far, near, far_out, near_out, scratch=()):
    far = [pltpu.with_memory_space_constraint(a, pltpu.HBM) for a in far]
    out = [pltpu.HBM(s, d) for s, d in far_out] + [jax.ShapeDtypeStruct(s, d) for s, d in near_out]
    specs = [hbm() for _ in far_out] + [vmem() for _ in near_out]
    many = len(out) > 1
    return pl.pallas_call(
        kernel,
        name=name,
        out_shape=out if many else out[0],
        in_specs=[smem() for _ in scalars] + [hbm() for _ in far] + [vmem() for _ in near],
        out_specs=specs if many else specs[0],
        scratch_shapes=list(scratch),
        compiler_params=pltpu.CompilerParams(vmem_limit_bytes=VMEM_LIMIT),
    )(*scalars, *far, *near)


def shift_ctx(values, by):
    size = lax.axis_size("ctx")
    pairs = [(i, i + by) for i in range(size) if 0 <= i + by < size]
    return lax.ppermute(values, "ctx", pairs)


def swap_core(values):
    size = lax.axis_size("head")
    return lax.ppermute(values, "head", [(i, i ^ 1) for i in range(size)])


def around(values, by):
    size = lax.axis_size("head")
    return lax.ppermute(values, "head", [(i, (i + 2 * by) % size) for i in range(size)])


def body(x_raw, bc_raw, conv_x_w, conv_bc_w, dt_raw, a_log, d_skip, doc_starts, grad_y):
    rows, channels = x_raw.shape
    heads = a_log.shape[0]
    head_dim = channels // heads
    wide = bc_raw.shape[1]
    count = lax.axis_size("ctx")
    part = channels // count
    core = (lax.axis_index("head") % 2).astype(jnp.int32).reshape(1)
    halo = shift_ctx(jnp.concatenate([x_raw[rows - RIM :], bc_raw[rows - RIM :]], axis=1), 1)
    wide_bf, wide_f = ((rows, channels), BF16), ((rows, channels), F32)
    sems = pltpu.SemaphoreType.DMA
    two = sems((2,))
    inputs = [pltpu.VMEM(*wide_bf), pltpu.VMEM(*wide_bf), pltpu.VMEM((rows, wide), BF16)]
    input_sems = [two, two, sems((1,))]
    ext = pltpu.VMEM((rows + RIM, channels + wide), F32)
    sent = ((count, 2 * part + RIM, LANES), BF16)
    states = ((count, 2 * part, LANES), BF16)
    sums, leave_top, dy_top, top, tail = call(
        functools.partial(gather_kernel, head_dim),
        "gather",
        [doc_starts, a_log],
        [x_raw, grad_y, bc_raw],
        [conv_x_w, conv_bc_w, dt_raw],
        [],
        [
            ((2, LANES, channels), F32),
            ((RIM, channels), F32),
            ((RIM, channels), F32),
            ((RIM, channels + wide), F32),
            ((RIM, LANES), BF16),
        ],
        [*inputs, ext, *input_sems],
    )
    send = call(
        send_kernel,
        "send",
        [],
        [],
        [halo, sums, leave_top, dy_top, top, tail, conv_x_w, conv_bc_w],
        [],
        [sent],
        [pltpu.VMEM((2 * RIM, channels + wide), F32)],
    )
    got = lax.all_to_all(send, "ctx", 0, 0)
    scanned = call(
        functools.partial(scan_kernel, head_dim),
        "scan",
        [],
        [],
        [got],
        [states],
        [],
        [
            pltpu.VMEM(*states),
            pltpu.VMEM((count * RIM, LANES), F32),
            pltpu.VMEM((count * RIM, channels // 2), F32),
            sems((4,)),
        ],
    )
    scanned, dt_later = lax.optimization_barrier((scanned, dt_raw))
    gs, ls, yi, lx, edy, bcc, gbc, sbc, hv, first = call(
        functools.partial(intra_kernel, head_dim),
        "intra",
        [doc_starts, a_log, d_skip],
        [x_raw, grad_y, bc_raw],
        [halo, conv_x_w, conv_bc_w, dt_later],
        [wide_f, wide_f],
        [
            wide_f,
            wide_bf,
            wide_bf,
            ((rows, wide), BF16),
            ((rows, wide), F32),
            ((rows, wide), F32),
            ((7, heads, rows), F32),
            ((2, RIM, channels), F32),
        ],
        [
            *inputs,
            pltpu.VMEM(*wide_f),
            pltpu.VMEM(*wide_f),
            ext,
            pltpu.VMEM((rows, rows), F32),
            pltpu.VMEM((rows, rows), F32),
            *input_sems,
            sems((4,)),
        ],
    )
    st = lax.all_to_all(scanned, "ctx", 0, 0)
    half = rows // 2
    keep, give, rim = call(
        bc_kernel,
        "grad_bc",
        [core],
        [],
        [st, lx, edy, bcc, gbc, sbc, first, conv_bc_w],
        [],
        [
            ((half, wide), F32),
            ((half, wide), BF16),
            ((RIM, channels + wide), F32),
        ],
        [pltpu.VMEM((rows + RIM, wide), F32), pltpu.VMEM((rows, wide), F32)],
    )
    next_rim = shift_ctx(rim, -1)
    other = swap_core(give)
    st, keep = lax.optimization_barrier((st, keep))
    y_out, enter_term = call(
        functools.partial(y_kernel, head_dim),
        "y_out",
        [],
        [],
        [st, bcc, hv, yi, edy],
        [wide_bf],
        [((heads, rows), F32)],
        [pltpu.VMEM(*wide_bf), pltpu.VMEM(*wide_f), two],
    )
    grad_xc, leave_term, overlap = call(
        functools.partial(xc_kernel, head_dim),
        "grad_xc",
        [],
        [gs, ls],
        [st, bcc, lx],
        [],
        [wide_f, ((heads, rows), F32), ((heads, LANES), F32)],
        [pltpu.VMEM(*wide_f), pltpu.VMEM(*wide_f), two, two],
    )
    other, next_rim, enter_term, leave_term = lax.optimization_barrier(
        (other, next_rim, enter_term, leave_term)
    )
    message = ((half + RIM, wide), BF16)
    joined = call(
        join_kernel,
        "join",
        [],
        [],
        [keep, other, next_rim, conv_bc_w],
        [],
        [message],
        [pltpu.VMEM((2 * RIM, wide), F32)],
    )
    ring = lax.axis_size("head") // 2
    pieces = [joined] + [around(joined, by) for by in range(1, ring)]
    grad_x = call(
        x_kernel,
        "grad_x",
        [],
        [],
        [grad_xc, next_rim, conv_x_w],
        [wide_bf],
        [],
        [pltpu.VMEM(*wide_bf), pltpu.VMEM((2 * RIM, channels), F32), sems((4,))],
    )
    pieces, grad_x = lax.optimization_barrier((pieces, grad_x))
    summed = call(sum_kernel, "sum", [], [], pieces, [], [message])
    summed, leave_term = lax.optimization_barrier((summed, leave_term))
    swapped = swap_core(summed)
    grad_dt = call(
        dt_kernel, "grad_dt", [], [], [hv, enter_term, leave_term, overlap], [], [((heads, rows), F32)]
    )
    swapped, grad_dt = lax.optimization_barrier((swapped, grad_dt))
    grad_bc = call(
        last_kernel,
        "last",
        [core],
        [],
        [summed, swapped],
        [],
        [((rows, wide), BF16)],
        [pltpu.VMEM((rows, wide), F32)],
    )
    return (y_out, grad_x, grad_bc, grad_dt)


def solution(mesh):
    in_specs = (
        P("ctx", "head"),
        P("ctx", None),
        P(None, "head"),
        P(),
        P("head", "ctx"),
        P("head"),
        P("head"),
        P("ctx"),
        P("ctx", "head"),
    )
    out_specs = (P("ctx", "head"), P("ctx", "head"), P("ctx", None), P("head", "ctx"))
    return jax.shard_map(body, mesh=mesh, in_specs=in_specs, out_specs=out_specs, check_vma=False)
```

```python
import functools

import jax
import jax.numpy as jnp
from jax import lax
from jax.experimental import pallas as pl
from jax.experimental.pallas import tpu as pltpu
from jax.sharding import PartitionSpec as P

F32 = jnp.float32
BF16 = jnp.bfloat16
LANES = 128
RIM = 8
VMEM_LIMIT = 24 * 1024 * 1024
HIGHEST = lax.Precision.HIGHEST


def dot(a, b, dims, precision=None):
    return lax.dot_general(a, b, (dims, ((), ())), precision=precision, preferred_element_type=F32)


def iota(shape, axis):
    return lax.broadcasted_iota(jnp.int32, shape, axis)


def halves(values):
    high = values.astype(BF16)
    return high, (values - high.astype(F32)).astype(BF16)


def sigmoid(values):
    return 0.5 * jnp.tanh(0.5 * values) + 0.5


def diagonal(size):
    return jnp.where(iota((size, size), 0) == iota((size, size), 1), 1.0, 0.0).astype(BF16)


def columns(values):
    both = jnp.concatenate(halves(values), axis=0)
    return dot(diagonal(values.shape[1]), both, ((1,), (1,))).astype(BF16)


def spread(pairs, slab, head_dim, width=LANES):
    heads = pairs.shape[1] // 2
    row = iota((2 * heads, width), 0)
    head = iota((2 * heads, width), 1) // head_dim + slab * (width // head_dim)
    chosen = jnp.where((row == head) | (row == head + heads), 1.0, 0.0).astype(BF16)
    return dot(pairs, chosen, ((1,), (0,)))


def head_sum(values, slab, head_dim, heads):
    width = values.shape[1]
    head = (iota((heads, width), 1) % LANES) // head_dim + slab * (LANES // head_dim)
    chosen = jnp.where(iota((heads, width), 0) == head, 1.0, 0.0).astype(BF16)
    return dot(chosen, values.astype(BF16), ((1,), (1,)))


def head_sum_exact(values, slab, head_dim, heads):
    return head_sum(jnp.concatenate(halves(values), axis=1), slab, head_dim, heads)


def per_head(ref, heads, rows):
    at = iota((heads, rows), 0)
    values = jnp.zeros((heads, rows), F32)
    for head in range(heads):
        values = jnp.where(at == head, ref[head], values)
    return values


def head_values(doc_ref, a_log_ref, dt_ref):
    heads, rows = dt_ref.shape
    doc = doc_ref[0]
    raw = dt_ref[...]
    step = jnp.maximum(raw, 0.0) + jnp.log(1.0 + jnp.exp(-jnp.abs(raw)))
    decay = jnp.exp(per_head(a_log_ref, heads, rows))
    upto = jnp.where(iota((rows, rows), 0) <= iota((rows, rows), 1), 1.0, 0.0)
    drop = -decay * step
    cum = dot(drop, upto, ((1,), (0,)), HIGHEST)
    final = cum[:, rows - 1 :]
    segment = iota((heads, rows), 1) >= doc
    entering = jnp.where(segment, 0.0, jnp.exp(cum))
    outside = jnp.logical_and(iota((heads, rows), 1) < doc, doc < rows)
    leaving = jnp.where(outside, 0.0, jnp.exp(final - cum))
    carry = jnp.where(doc >= rows, jnp.exp(jnp.broadcast_to(final, (heads, rows))), 0.0)
    return dict(
        step=step, decay=decay, drop=drop, cum=cum, entering=entering, leaving=leaving, carry=carry
    )


def lanes_of(slab):
    return slice(slab * LANES, (slab + 1) * LANES)


def fetch(source, target, sems):
    pieces = sems.shape[0]
    width = source.shape[1] // pieces
    copies = {}
    for piece in range(pieces):
        at = (slice(None), slice(piece * width, (piece + 1) * width))
        copy = pltpu.make_async_copy(source.at[at], target.at[at], sems.at[piece])
        copy.start()
        copies[piece * width // LANES] = copy
    return copies


def arrived(copies, slab):
    if slab in copies:
        copies[slab].wait()


def put(source, target, sem, at):
    copy = pltpu.make_async_copy(source.at[at], target.at[at], sem)
    copy.start()
    return copy


def load_ext(ext, halo_ref, values, at, lanes):
    if halo_ref is None:
        ext[0:RIM, at] = jnp.zeros((RIM, at.stop - at.start), F32)
    else:
        ext[0:RIM, at] = halo_ref[:, at].astype(F32)
    ext[RIM : RIM + values.shape[0], at] = values[:, lanes].astype(F32)


def filtered(ext, w_ref, at, w_at, rows, width=LANES):
    taps = w_ref.shape[0]
    lanes = pl.ds(at, width)
    w = w_ref[:, w_at : w_at + width].astype(F32)
    total = w[0:1] * ext[pl.ds(RIM - taps + 1, rows), lanes]
    for tap in range(1, taps):
        total = total + w[tap : tap + 1] * ext[pl.ds(RIM - taps + 1 + tap, rows), lanes]
    return total


def gather_kernel(
    head_dim, doc_ref, a_log_ref, x_hbm, dy_hbm, bc_hbm, wx_ref, wbc_ref, dt_ref,
    sum_ref, ls_ref, edy_ref, top_ref, tail_ref,
    x_ref, dy_ref, bc_ref, ext, x_sems, dy_sems, bc_sems,
):
    rows, channels = x_ref.shape
    bc_in = fetch(bc_hbm, bc_ref, bc_sems)
    x_in = fetch(x_hbm, x_ref, x_sems)
    dy_in = fetch(dy_hbm, dy_ref, dy_sems)
    v = head_values(doc_ref, a_log_ref, dt_ref)
    leave_step = columns(v["leaving"] * v["step"])
    entering = columns(v["entering"])
    heads = dt_ref.shape[0]
    own = iota((heads, LANES), 0) == iota((heads, LANES), 1)
    carry = jnp.sum(jnp.where(own, v["carry"][:, 0:LANES], 0.0), axis=0, keepdims=True)
    high, low = [half.astype(F32) for half in halves(carry)]
    at = iota((RIM, LANES), 0)
    tail_ref[...] = jnp.where(at == 0, high, jnp.where(at == 1, low, 0.0)).astype(BF16)
    bc = []
    for half in range(2):
        arrived(bc_in, half)
        load_ext(ext, None, bc_ref, lanes_of(channels // LANES + half), lanes_of(half))
        pre = filtered(ext, wbc_ref, channels + half * LANES, half * LANES, rows)
        bc.append((pre * sigmoid(pre)).T.astype(BF16))
    width = LANES
    below = iota((rows, width), 0) >= RIM
    for slab in range(channels // width):
        lanes = slice(slab * width, (slab + 1) * width)
        arrived(x_in, slab)
        load_ext(ext, None, x_ref, lanes, lanes)
        pre = filtered(ext, wx_ref, slab * width, slab * width, rows, width)
        x_conv = (pre * sigmoid(pre)).astype(BF16).astype(F32)
        leave = spread(leave_step, slab, head_dim, width)
        leaving_x = jnp.where(below, x_conv * leave, 0.0).astype(BF16)
        sum_ref[0, :, lanes] = dot(bc[0], leaving_x, ((1,), (0,)))
        arrived(dy_in, slab)
        enter_dy = dy_ref[:, lanes].astype(F32) * spread(entering, slab, head_dim, width)
        masked = jnp.where(below, enter_dy, 0.0).astype(BF16)
        sum_ref[1, :, lanes] = dot(bc[1], masked, ((1,), (0,)))
        ls_ref[:, lanes] = leave[0:RIM]
        edy_ref[:, lanes] = enter_dy[0:RIM]
    top_ref[...] = ext[RIM : 2 * RIM, :]


def chunk_of(across, side, which):
    return 16 * across + 2 * side + which


def send_kernel(
    halo_ref, sum_ref, ls_ref, edy_ref, top_ref, tail_ref, wx_ref, wbc_ref, send_ref, ext,
):
    channels = ls_ref.shape[1]
    count = send_ref.shape[0]
    tall = 2 * RIM
    ext[0:RIM, :] = halo_ref[...].astype(F32)
    ext[RIM:, :] = top_ref[...]
    none = jnp.zeros((RIM, LANES), F32)

    def conv(w_ref, at, w_at):
        pre = filtered(ext, w_ref, at, w_at, RIM)
        return (pre * sigmoid(pre)).astype(BF16).astype(F32)

    bc = []
    for at in (0, LANES):
        top = jnp.concatenate([conv(wbc_ref, channels + at, at), none], axis=0).astype(BF16)
        bc.append(dot(top, diagonal(tall), ((0,), (0,))).astype(BF16))
    tail = tail_ref[...]
    for chunk in range(count):
        send_ref[chunk, send_ref.shape[1] - RIM :, :] = tail
    slabs = channels // LANES
    for slab in range(slabs):
        lanes = lanes_of(slab)
        across, tile = slab // (slabs // 2), slab % (slabs // 2)
        leaving_x = conv(wx_ref, slab * LANES, slab * LANES) * ls_ref[:, lanes]
        enter_dy = edy_ref[:, lanes]
        for which, top in enumerate((leaving_x, enter_dy)):
            top = jnp.concatenate([top, none], axis=0).astype(BF16)
            total = (sum_ref[which, :, lanes] + dot(bc[which], top, ((1,), (0,)))).astype(BF16)
            for side in range(LANES // tall):
                piece = total[side * tall : (side + 1) * tall]
                send_ref[chunk_of(across, side, which), tile * tall : (tile + 1) * tall, :] = piece


def scan_kernel(head_dim, got_ref, out_hbm, out_ref, tails, carries, sems):
    count, width, lanes = out_ref.shape
    tall = 2 * RIM
    tiles = width // tall
    me = lax.axis_index("ctx")
    backward = lax.rem(me, 2)
    across = me // (count // 2)
    for at in range(count):
        tails[RIM * at : RIM * (at + 1), :] = got_ref[at, width : width + RIM, :].astype(F32)
    shape = (lanes, tiles * lanes)
    head = iota(shape, 1) // head_dim + across * (tiles * lanes // head_dim)
    chosen = jnp.where(iota(shape, 0) == head, 1.0, 0.0).astype(BF16)
    carries[...] = dot(tails[...].astype(BF16), chosen, ((1,), (0,)))
    states = [jnp.zeros((tall, lanes), F32) for _ in range(tiles)]
    sent = []
    pieces = sems.shape[0]
    group = count // pieces
    for step in range(count):
        at = jnp.where(backward == 1, count - 1 - step, step)
        carry = carries[pl.ds(pl.multiple_of(at * RIM, RIM), RIM), :]
        carry = carry[0:1] + carry[1:2]
        for tile in range(tiles):
            rows = slice(tile * tall, (tile + 1) * tall)
            out_ref[at, rows, :] = states[tile].astype(BF16)
            states[tile] = carry[:, lanes_of(tile)] * states[tile] + got_ref[at, rows, :].astype(F32)
        if step % group == group - 1:
            first = jnp.where(backward == 1, count - 1 - step, step + 1 - group)
            sent.append(put(out_ref, out_hbm, sems.at[step // group], (pl.ds(first, group),)))
    for copy in sent:
        copy.wait()


def intra_kernel(
    head_dim, doc_ref, a_log_ref, skip_ref, x_hbm, dy_hbm, bc_hbm, halo_ref, wx_ref, wbc_ref, dt_ref,
    gs_hbm, ls_hbm, yi_ref,
    lx_ref, edy_ref, bcc_ref, gbc_ref, sbc_ref, hv_ref, rim_ref,
    x_ref, dy_ref, bc_ref, gs_ref, ls_ref, ext, bias, dgram,
    x_sems, dy_sems, bc_sems, out_sems,
):
    rows, channels = x_ref.shape
    heads = dt_ref.shape[0]
    doc = doc_ref[0]
    bc_in = fetch(bc_hbm, bc_ref, bc_sems)
    x_in = fetch(x_hbm, x_ref, x_sems)
    dy_in = fetch(dy_hbm, dy_ref, dy_sems)
    v = head_values(doc_ref, a_log_ref, dt_ref)
    for half in range(2):
        lanes = lanes_of(half)
        arrived(bc_in, half)
        load_ext(ext, halo_ref, bc_ref, lanes_of(channels // LANES + half), lanes)
        pre = filtered(ext, wbc_ref, channels + half * LANES, half * LANES, rows)
        gate = sigmoid(pre)
        bcc_ref[:, lanes] = (pre * gate).astype(BF16)
        sbc_ref[:, lanes] = gate * (1.0 + pre * (1.0 - gate))
    b_matrix = bcc_ref[:, 0:LANES]
    c_matrix = bcc_ref[:, LANES:]
    gram = dot(c_matrix, b_matrix, ((1,), (1,)))
    t_at, s_at = iota((rows, rows), 0), iota((rows, rows), 1)
    bias[...] = jnp.where((t_at >= s_at) & ((t_at >= doc) == (s_at >= doc)), 0.0, -1e30)
    dgram[...] = jnp.zeros_like(dgram)
    downto = jnp.where(t_at >= s_at, 1.0, 0.0)
    cum = v["cum"]
    cum_t = dot(downto, v["drop"], ((1,), (1,)), HIGHEST)
    skip = per_head(skip_ref, heads, rows)
    leave_step = columns(v["leaving"] * v["step"])
    entering, steps = columns(v["entering"]), columns(v["step"])
    skip = columns(skip)
    along_dt = jnp.zeros((heads, rows), F32)
    z_diff = jnp.zeros((heads, rows), F32)
    low_half = iota((rows, LANES), 1) < head_dim
    sent = []
    for slab in range(channels // LANES):
        lanes = lanes_of(slab)
        arrived(x_in, slab)
        load_ext(ext, halo_ref, x_ref, lanes, lanes)
        arrived(dy_in, slab)
        pre = filtered(ext, wx_ref, slab * LANES, slab * LANES, rows)
        gate = sigmoid(pre)
        x_bf = (pre * gate).astype(BF16)
        silu_grad = gate * (1.0 + pre * (1.0 - gate))
        x_conv = x_bf.astype(F32)
        step = spread(steps, slab, head_dim)
        leave = spread(leave_step, slab, head_dim)
        enter = spread(entering, slab, head_dim)
        skips = spread(skip, slab, head_dim)
        dy_bf = dy_ref[:, lanes]
        dy = dy_bf.astype(F32)
        lx_ref[:, lanes] = (x_conv * leave).astype(BF16)
        edy_ref[:, lanes] = (dy * enter).astype(BF16)
        scaled = (x_conv * step).astype(BF16)
        intra = jnp.zeros((rows, LANES), F32)
        d_scaled = jnp.zeros((rows, LANES), F32)
        for side in range(LANES // head_dim):
            head = slab * (LANES // head_dim) + side
            mine = low_half if side == 0 else jnp.logical_not(low_half)
            scaled_h = jnp.where(mine, scaled.astype(F32), 0.0).astype(BF16)
            dy_h = jnp.where(mine, dy, 0.0).astype(BF16)
            kernel = jnp.exp((cum_t[:, head : head + 1] - cum[head : head + 1, :]) + bias[...])
            mixing = (gram * kernel).astype(BF16)
            response = dot(dy_h, scaled, ((1,), (1,)))
            dgram[...] += response * kernel
            intra = intra + dot(mixing, scaled_h, ((1,), (0,)))
            d_scaled = d_scaled + dot(mixing, dy_h, ((0,), (0,)))
        yi_ref[:, lanes] = intra + skips * x_conv
        gs_ref[:, lanes] = (step * d_scaled + skips * dy) * silu_grad
        ls_ref[:, lanes] = leave * silu_grad
        rim_ref[0, :, lanes] = gs_ref[0:RIM, lanes]
        rim_ref[1, :, lanes] = ls_ref[0:RIM, lanes]
        group = channels // LANES // (out_sems.shape[0] // 2)
        if slab % group == group - 1:
            at = (slice(None), slice((slab + 1 - group) * LANES, (slab + 1) * LANES))
            sent.append(put(gs_ref, gs_hbm, out_sems.at[slab // group * 2], at))
            sent.append(put(ls_ref, ls_hbm, out_sems.at[slab // group * 2 + 1], at))
        along_dt = along_dt + head_sum_exact(x_conv * d_scaled, slab, head_dim, heads)
        z_diff = z_diff + head_sum_exact(
            dy * intra - scaled.astype(F32) * d_scaled, slab, head_dim, heads
        )
    d_gram = dgram[...]
    gbc_ref[:, 0:LANES] = dot(d_gram, c_matrix.astype(F32), ((0,), (0,)), HIGHEST)
    gbc_ref[:, LANES:] = dot(d_gram, b_matrix.astype(F32), ((1,), (0,)), HIGHEST)
    small = [
        v["step"],
        v["entering"],
        along_dt,
        z_diff,
        v["carry"],
        v["decay"],
        1.0 / (1.0 + jnp.exp(-dt_ref[...])),
    ]
    for at, values in enumerate(small):
        hv_ref[at] = values
    for copy in sent:
        copy.wait()


def state_of(st_ref, which, slab):
    tall = 2 * RIM
    tiles = st_ref.shape[1] // tall
    across, tile = slab // tiles, slab % tiles
    sides = LANES // tall
    rows = slice(tile * tall, (tile + 1) * tall)
    return jnp.concatenate(
        [st_ref[chunk_of(across, side, which), rows, :] for side in range(sides)], axis=0
    )


def bc_kernel(
    core_ref, st_ref, lx_ref, edy_ref, b_ref, gbc_ref, sbc_ref, rim_ref, wbc_ref,
    keep_ref, give_ref, halo_ref, ext, total,
):
    rows = lx_ref.shape[0]
    taps = wbc_ref.shape[0]
    slabs = lx_ref.shape[1] // LANES
    state, dstate = [
        jnp.concatenate([state_of(st_ref, which, slab) for slab in range(slabs)], axis=1)
        for which in range(2)
    ]
    grad_b = gbc_ref[:, 0:LANES] + dot(lx_ref[...], dstate, ((1,), (1,)))
    grad_c = gbc_ref[:, LANES:] + dot(edy_ref[...], state, ((1,), (1,)))
    ext[0:rows, 0:LANES] = grad_b * sbc_ref[:, 0:LANES]
    ext[0:rows, LANES:] = grad_c * sbc_ref[:, LANES:]
    ext[rows:, :] = jnp.zeros((RIM, 2 * LANES), F32)
    w = wbc_ref[...].astype(F32)
    out = w[taps - 1 : taps] * ext[0:rows, :]
    for tap in range(taps - 1):
        out = out + w[tap : tap + 1] * ext[pl.ds(taps - 1 - tap, rows), :]
    total[...] = out
    half = rows // 2
    core = core_ref[0]
    keep_ref[...] = total[pl.ds(pl.multiple_of(core * half, half), half), :]
    give_ref[...] = total[pl.ds(pl.multiple_of((1 - core) * half, half), half), :].astype(BF16)
    d_leaving = dot(b_ref[0 : 2 * RIM, 0:LANES], dstate, ((1,), (0,)))[0:RIM]
    channels = rim_ref.shape[2]
    halo_ref[:, 0:channels] = (rim_ref[0] + rim_ref[1] * d_leaving).astype(BF16)
    halo_ref[:, channels:] = ext[0:RIM, :].astype(BF16)


def join_kernel(keep_ref, got_ref, halo_ref, wbc_ref, out_ref, ext):
    half = keep_ref.shape[0]
    taps = wbc_ref.shape[0]
    wide = keep_ref.shape[1]
    out_ref[0:half, :] = (keep_ref[...] + got_ref[...].astype(F32)).astype(BF16)
    ext[0:RIM, :] = jnp.zeros((RIM, wide), F32)
    ext[RIM:, :] = halo_ref[:, halo_ref.shape[1] - wide :].astype(F32)
    w = wbc_ref[...].astype(F32)
    rim = jnp.zeros((RIM, wide), F32)
    for tap in range(taps - 1):
        rim = rim + w[tap : tap + 1] * ext[pl.ds(taps - 1 - tap, RIM), :]
    out_ref[half:, :] = rim.astype(BF16)


def sum_kernel(*refs):
    out_ref = refs[-1]
    total = refs[0][...].astype(F32)
    for ref in refs[1:-1]:
        total = total + ref[...].astype(F32)
    out_ref[...] = total.astype(BF16)


def last_kernel(core_ref, mine_ref, got_ref, out_ref, total):
    rows = out_ref.shape[0]
    half = rows // 2
    core = core_ref[0]
    total[pl.ds(pl.multiple_of(core * half, half), half), :] = mine_ref[0:half, :].astype(F32)
    total[pl.ds(pl.multiple_of((1 - core) * half, half), half), :] = got_ref[0:half, :].astype(F32)
    total[rows - RIM :, :] += mine_ref[half:, :].astype(F32) + got_ref[half:, :].astype(F32)
    out_ref[...] = total[...].astype(BF16)


def y_kernel(head_dim, st_ref, bcc_ref, hv_ref, yi_ref, edy_ref, y_hbm, enter_ref, y_ref, ys_ref, sems):
    rows, channels = edy_ref.shape
    heads = hv_ref.shape[1]
    slabs = channels // LANES
    group = slabs // sems.shape[0]
    c_matrix = bcc_ref[:, LANES:]
    entering = columns(hv_ref[1])
    sent = []
    for slab in range(slabs):
        lanes = lanes_of(slab)
        y_state = dot(c_matrix, state_of(st_ref, 0, slab), ((1,), (0,)))
        ys_ref[:, lanes] = y_state
        y_ref[:, lanes] = (yi_ref[:, lanes] + spread(entering, slab, head_dim) * y_state).astype(BF16)
        if slab % group == group - 1:
            at = (slice(None), slice((slab + 1 - group) * LANES, (slab + 1) * LANES))
            sent.append(put(y_ref, y_hbm, sems.at[slab // group], at))
    enter_term = jnp.zeros((heads, rows), F32)
    for slab in range(slabs):
        lanes = lanes_of(slab)
        enter_term = enter_term + head_sum(
            edy_ref[:, lanes].astype(F32) * ys_ref[:, lanes], slab, head_dim, heads
        )
    enter_ref[...] = enter_term
    for copy in sent:
        copy.wait()


def xc_kernel(
    head_dim, gs_hbm, ls_hbm, st_ref, bcc_ref, lx_ref,
    g_ref, leave_ref, overlap_ref, gs_ref, ls_ref, gs_sems, ls_sems,
):
    rows, channels = lx_ref.shape
    heads = leave_ref.shape[0]
    slabs = channels // LANES
    gs_in = fetch(gs_hbm, gs_ref, gs_sems)
    ls_in = fetch(ls_hbm, ls_ref, ls_sems)
    b_matrix = bcc_ref[:, 0:LANES]
    leave_term = jnp.zeros((heads, rows), F32)
    overlap = jnp.zeros((heads, LANES), F32)
    for slab in range(slabs):
        lanes = lanes_of(slab)
        dstate = state_of(st_ref, 1, slab)
        product = state_of(st_ref, 0, slab).astype(F32) * dstate.astype(F32)
        head = iota((heads, LANES), 1) // head_dim + slab * (LANES // head_dim)
        own = iota((heads, LANES), 0) == head
        overlap = overlap + jnp.where(own, jnp.sum(product, axis=0, keepdims=True), 0.0)
        d_leaving = dot(b_matrix, dstate, ((1,), (0,)))
        g_ref[:, lanes] = d_leaving
        leave_term = leave_term + head_sum(
            lx_ref[:, lanes].astype(F32) * d_leaving, slab, head_dim, heads
        )
    leave_ref[...] = leave_term
    overlap_ref[...] = overlap
    for slab in range(slabs):
        lanes = lanes_of(slab)
        arrived(gs_in, slab)
        arrived(ls_in, slab)
        g_ref[:, lanes] = gs_ref[:, lanes] + ls_ref[:, lanes] * g_ref[:, lanes]


def x_kernel(g_ref, halo_ref, wx_ref, gx_hbm, gx_ref, ext, sems):
    rows, channels = g_ref.shape
    taps = wx_ref.shape[0]
    slabs = channels // LANES
    group = slabs // sems.shape[0]
    low = rows - RIM
    ext[0:RIM, :] = g_ref[low:, :]
    ext[RIM:, :] = halo_ref[:, 0:channels].astype(F32)
    sent = []
    for slab in range(slabs):
        lanes = lanes_of(slab)
        w = wx_ref[:, lanes].astype(F32)
        body = w[taps - 1 : taps] * g_ref[0:low, lanes]
        edge = w[taps - 1 : taps] * ext[0:RIM, lanes]
        for tap in range(taps - 1):
            ahead = taps - 1 - tap
            body = body + w[tap : tap + 1] * g_ref[pl.ds(ahead, low), lanes]
            edge = edge + w[tap : tap + 1] * ext[pl.ds(ahead, RIM), lanes]
        gx_ref[:, lanes] = jnp.concatenate([body, edge], axis=0).astype(BF16)
        if slab % group == group - 1:
            at = (slice(None), slice((slab + 1 - group) * LANES, (slab + 1) * LANES))
            sent.append(put(gx_ref, gx_hbm, sems.at[slab // group], at))
    for copy in sent:
        copy.wait()


def dt_kernel(hv_ref, enter_ref, leave_ref, overlap_ref, gdt_ref):
    heads, rows = leave_ref.shape
    step, _, along_dt, z_diff, carry, decay, dt_gate = [hv_ref[at] for at in range(7)]
    leave_term, overlap = leave_ref[...], overlap_ref[...]
    final = jnp.sum(leave_term, axis=1, keepdims=True) + carry * jnp.sum(overlap, axis=1, keepdims=True)
    d_cum = z_diff + enter_ref[...] - leave_term
    d_cum = d_cum + jnp.where(iota((heads, rows), 1) == rows - 1, final, 0.0)
    after = jnp.where(iota((rows, rows), 0) >= iota((rows, rows), 1), 1.0, 0.0)
    d_log = dot(d_cum, after, ((1,), (0,)), HIGHEST)
    gdt_ref[...] = (along_dt + leave_term / step - decay * d_log) * dt_gate


def smem():
    return pl.BlockSpec(memory_space=pltpu.SMEM)


def vmem():
    return pl.BlockSpec(memory_space=pltpu.VMEM)


def hbm():
    return pl.BlockSpec(memory_space=pltpu.HBM)


def call(kernel, name, scalars, far, near, far_out, near_out, scratch=()):
    far = [pltpu.with_memory_space_constraint(a, pltpu.HBM) for a in far]
    out = [pltpu.HBM(s, d) for s, d in far_out] + [jax.ShapeDtypeStruct(s, d) for s, d in near_out]
    specs = [hbm() for _ in far_out] + [vmem() for _ in near_out]
    many = len(out) > 1
    return pl.pallas_call(
        kernel,
        name=name,
        out_shape=out if many else out[0],
        in_specs=[smem() for _ in scalars] + [hbm() for _ in far] + [vmem() for _ in near],
        out_specs=specs if many else specs[0],
        scratch_shapes=list(scratch),
        compiler_params=pltpu.CompilerParams(vmem_limit_bytes=VMEM_LIMIT),
    )(*scalars, *far, *near)


def shift_ctx(values, by):
    size = lax.axis_size("ctx")
    pairs = [(i, i + by) for i in range(size) if 0 <= i + by < size]
    return lax.ppermute(values, "ctx", pairs)


def swap_core(values):
    size = lax.axis_size("head")
    return lax.ppermute(values, "head", [(i, i ^ 1) for i in range(size)])


def around(values, by):
    size = lax.axis_size("head")
    return lax.ppermute(values, "head", [(i, (i + 2 * by) % size) for i in range(size)])


def body(x_raw, bc_raw, conv_x_w, conv_bc_w, dt_raw, a_log, d_skip, doc_starts, grad_y):
    rows, channels = x_raw.shape
    heads = a_log.shape[0]
    head_dim = channels // heads
    wide = bc_raw.shape[1]
    count = lax.axis_size("ctx")
    part = channels // count
    core = (lax.axis_index("head") % 2).astype(jnp.int32).reshape(1)
    halo = shift_ctx(jnp.concatenate([x_raw[rows - RIM :], bc_raw[rows - RIM :]], axis=1), 1)
    wide_bf, wide_f = ((rows, channels), BF16), ((rows, channels), F32)
    sems = pltpu.SemaphoreType.DMA
    two = sems((2,))
    inputs = [pltpu.VMEM(*wide_bf), pltpu.VMEM(*wide_bf), pltpu.VMEM((rows, wide), BF16)]
    input_sems = [two, two, sems((1,))]
    ext = pltpu.VMEM((rows + RIM, channels + wide), F32)
    sent = ((count, 2 * part + RIM, LANES), BF16)
    states = ((count, 2 * part, LANES), BF16)
    sums, leave_top, dy_top, top, tail = call(
        functools.partial(gather_kernel, head_dim),
        "gather",
        [doc_starts, a_log],
        [x_raw, grad_y, bc_raw],
        [conv_x_w, conv_bc_w, dt_raw],
        [],
        [
            ((2, LANES, channels), F32),
            ((RIM, channels), F32),
            ((RIM, channels), F32),
            ((RIM, channels + wide), F32),
            ((RIM, LANES), BF16),
        ],
        [*inputs, ext, *input_sems],
    )
    send = call(
        send_kernel,
        "send",
        [],
        [],
        [halo, sums, leave_top, dy_top, top, tail, conv_x_w, conv_bc_w],
        [],
        [sent],
        [pltpu.VMEM((2 * RIM, channels + wide), F32)],
    )
    got = lax.all_to_all(send, "ctx", 0, 0)
    scanned = call(
        functools.partial(scan_kernel, head_dim),
        "scan",
        [],
        [],
        [got],
        [states],
        [],
        [
            pltpu.VMEM(*states),
            pltpu.VMEM((count * RIM, LANES), F32),
            pltpu.VMEM((count * RIM, channels // 2), F32),
            sems((4,)),
        ],
    )
    scanned, dt_later = lax.optimization_barrier((scanned, dt_raw))
    gs, ls, yi, lx, edy, bcc, gbc, sbc, hv, first = call(
        functools.partial(intra_kernel, head_dim),
        "intra",
        [doc_starts, a_log, d_skip],
        [x_raw, grad_y, bc_raw],
        [halo, conv_x_w, conv_bc_w, dt_later],
        [wide_f, wide_f],
        [
            wide_f,
            wide_bf,
            wide_bf,
            ((rows, wide), BF16),
            ((rows, wide), F32),
            ((rows, wide), F32),
            ((7, heads, rows), F32),
            ((2, RIM, channels), F32),
        ],
        [
            *inputs,
            pltpu.VMEM(*wide_f),
            pltpu.VMEM(*wide_f),
            ext,
            pltpu.VMEM((rows, rows), F32),
            pltpu.VMEM((rows, rows), F32),
            *input_sems,
            sems((4,)),
        ],
    )
    st = lax.all_to_all(scanned, "ctx", 0, 0)
    half = rows // 2
    keep, give, rim = call(
        bc_kernel,
        "grad_bc",
        [core],
        [],
        [st, lx, edy, bcc, gbc, sbc, first, conv_bc_w],
        [],
        [
            ((half, wide), F32),
            ((half, wide), BF16),
            ((RIM, channels + wide), BF16),
        ],
        [pltpu.VMEM((rows + RIM, wide), F32), pltpu.VMEM((rows, wide), F32)],
    )
    next_rim = shift_ctx(rim, -1)
    other = swap_core(give)
    st, keep = lax.optimization_barrier((st, keep))
    y_out, enter_term = call(
        functools.partial(y_kernel, head_dim),
        "y_out",
        [],
        [],
        [st, bcc, hv, yi, edy],
        [wide_bf],
        [((heads, rows), F32)],
        [pltpu.VMEM(*wide_bf), pltpu.VMEM(*wide_f), two],
    )
    grad_xc, leave_term, overlap = call(
        functools.partial(xc_kernel, head_dim),
        "grad_xc",
        [],
        [gs, ls],
        [st, bcc, lx],
        [],
        [wide_f, ((heads, rows), F32), ((heads, LANES), F32)],
        [pltpu.VMEM(*wide_f), pltpu.VMEM(*wide_f), two, two],
    )
    other, next_rim, enter_term, leave_term = lax.optimization_barrier(
        (other, next_rim, enter_term, leave_term)
    )
    message = ((half + RIM, wide), BF16)
    joined = call(
        join_kernel,
        "join",
        [],
        [],
        [keep, other, next_rim, conv_bc_w],
        [],
        [message],
        [pltpu.VMEM((2 * RIM, wide), F32)],
    )
    ring = lax.axis_size("head") // 2
    pieces = [joined] + [around(joined, by) for by in range(1, ring)]
    grad_x = call(
        x_kernel,
        "grad_x",
        [],
        [],
        [grad_xc, next_rim, conv_x_w],
        [wide_bf],
        [],
        [pltpu.VMEM(*wide_bf), pltpu.VMEM((2 * RIM, channels), F32), sems((4,))],
    )
    pieces, grad_x = lax.optimization_barrier((pieces, grad_x))
    summed = call(sum_kernel, "sum", [], [], pieces, [], [message])
    summed, leave_term = lax.optimization_barrier((summed, leave_term))
    swapped = swap_core(summed)
    grad_dt = call(
        dt_kernel, "grad_dt", [], [], [hv, enter_term, leave_term, overlap], [], [((heads, rows), F32)]
    )
    swapped, grad_dt = lax.optimization_barrier((swapped, grad_dt))
    grad_bc = call(
        last_kernel,
        "last",
        [core],
        [],
        [summed, swapped],
        [],
        [((rows, wide), BF16)],
        [pltpu.VMEM((rows, wide), F32)],
    )
    return (y_out, grad_x, grad_bc, grad_dt)


def solution(mesh):
    in_specs = (
        P("ctx", "head"),
        P("ctx", None),
        P(None, "head"),
        P(),
        P("head", "ctx"),
        P("head"),
        P("head"),
        P("ctx"),
        P("ctx", "head"),
    )
    out_specs = (P("ctx", "head"), P("ctx", "head"), P("ctx", None), P("head", "ctx"))
    return jax.shard_map(body, mesh=mesh, in_specs=in_specs, out_specs=out_specs, check_vma=False)
```

```python
import functools

import jax
import jax.numpy as jnp
from jax import lax
from jax.experimental import pallas as pl
from jax.experimental.pallas import tpu as pltpu
from jax.sharding import PartitionSpec as P

F32 = jnp.float32
BF16 = jnp.bfloat16
LANES = 128
RIM = 8
VMEM_LIMIT = 24 * 1024 * 1024
HIGHEST = lax.Precision.HIGHEST


def dot(a, b, dims, precision=None):
    return lax.dot_general(a, b, (dims, ((), ())), precision=precision, preferred_element_type=F32)


def iota(shape, axis):
    return lax.broadcasted_iota(jnp.int32, shape, axis)


def halves(values):
    high = values.astype(BF16)
    return high, (values - high.astype(F32)).astype(BF16)


def sigmoid(values):
    return 0.5 * jnp.tanh(0.5 * values) + 0.5


def diagonal(size):
    return jnp.where(iota((size, size), 0) == iota((size, size), 1), 1.0, 0.0).astype(BF16)


def columns(values):
    both = jnp.concatenate(halves(values), axis=0)
    return dot(diagonal(values.shape[1]), both, ((1,), (1,))).astype(BF16)


def spread(pairs, slab, head_dim, width=LANES):
    heads = pairs.shape[1] // 2
    row = iota((2 * heads, width), 0)
    head = iota((2 * heads, width), 1) // head_dim + slab * (width // head_dim)
    chosen = jnp.where((row == head) | (row == head + heads), 1.0, 0.0).astype(BF16)
    return dot(pairs, chosen, ((1,), (0,)))


def head_sum(values, slab, head_dim, heads):
    width = values.shape[1]
    head = (iota((heads, width), 1) % LANES) // head_dim + slab * (LANES // head_dim)
    chosen = jnp.where(iota((heads, width), 0) == head, 1.0, 0.0).astype(BF16)
    return dot(chosen, values.astype(BF16), ((1,), (1,)))


def head_sum_exact(values, slab, head_dim, heads):
    return head_sum(jnp.concatenate(halves(values), axis=1), slab, head_dim, heads)


def per_head(ref, heads, rows):
    at = iota((heads, rows), 0)
    values = jnp.zeros((heads, rows), F32)
    for head in range(heads):
        values = jnp.where(at == head, ref[head], values)
    return values


def head_values(doc_ref, a_log_ref, dt_ref):
    heads, rows = dt_ref.shape
    doc = doc_ref[0]
    raw = dt_ref[...]
    step = jnp.maximum(raw, 0.0) + jnp.log(1.0 + jnp.exp(-jnp.abs(raw)))
    decay = jnp.exp(per_head(a_log_ref, heads, rows))
    upto = jnp.where(iota((rows, rows), 0) <= iota((rows, rows), 1), 1.0, 0.0)
    drop = -decay * step
    cum = dot(drop, upto, ((1,), (0,)), HIGHEST)
    final = cum[:, rows - 1 :]
    segment = iota((heads, rows), 1) >= doc
    entering = jnp.where(segment, 0.0, jnp.exp(cum))
    outside = jnp.logical_and(iota((heads, rows), 1) < doc, doc < rows)
    leaving = jnp.where(outside, 0.0, jnp.exp(final - cum))
    carry = jnp.where(doc >= rows, jnp.exp(jnp.broadcast_to(final, (heads, rows))), 0.0)
    return dict(
        step=step, decay=decay, drop=drop, cum=cum, entering=entering, leaving=leaving, carry=carry
    )


def lanes_of(slab):
    return slice(slab * LANES, (slab + 1) * LANES)


def fetch(source, target, sems):
    pieces = sems.shape[0]
    width = source.shape[1] // pieces
    copies = {}
    for piece in range(pieces):
        at = (slice(None), slice(piece * width, (piece + 1) * width))
        copy = pltpu.make_async_copy(source.at[at], target.at[at], sems.at[piece])
        copy.start()
        copies[piece * width // LANES] = copy
    return copies


def arrived(copies, slab):
    if slab in copies:
        copies[slab].wait()


def put(source, target, sem, at):
    copy = pltpu.make_async_copy(source.at[at], target.at[at], sem)
    copy.start()
    return copy


def load_ext(ext, halo_ref, values, at, lanes):
    if halo_ref is None:
        ext[0:RIM, at] = jnp.zeros((RIM, at.stop - at.start), F32)
    else:
        ext[0:RIM, at] = halo_ref[:, at].astype(F32)
    ext[RIM : RIM + values.shape[0], at] = values[:, lanes].astype(F32)


def filtered(ext, w_ref, at, w_at, rows, width=LANES):
    taps = w_ref.shape[0]
    lanes = pl.ds(at, width)
    w = w_ref[:, w_at : w_at + width].astype(F32)
    total = w[0:1] * ext[pl.ds(RIM - taps + 1, rows), lanes]
    for tap in range(1, taps):
        total = total + w[tap : tap + 1] * ext[pl.ds(RIM - taps + 1 + tap, rows), lanes]
    return total


def gather_kernel(
    head_dim, doc_ref, a_log_ref, x_hbm, dy_hbm, bc_hbm, wx_ref, wbc_ref, dt_ref,
    sum_ref, ls_ref, edy_ref, top_ref, tail_ref,
    x_ref, dy_ref, bc_ref, ext, x_sems, dy_sems, bc_sems,
):
    rows, channels = x_ref.shape
    bc_in = fetch(bc_hbm, bc_ref, bc_sems)
    x_in = fetch(x_hbm, x_ref, x_sems)
    dy_in = fetch(dy_hbm, dy_ref, dy_sems)
    v = head_values(doc_ref, a_log_ref, dt_ref)
    leave_step = columns(v["leaving"] * v["step"])
    entering = columns(v["entering"])
    heads = dt_ref.shape[0]
    own = iota((heads, LANES), 0) == iota((heads, LANES), 1)
    carry = jnp.sum(jnp.where(own, v["carry"][:, 0:LANES], 0.0), axis=0, keepdims=True)
    high, low = [half.astype(F32) for half in halves(carry)]
    at = iota((RIM, LANES), 0)
    tail_ref[...] = jnp.where(at == 0, high, jnp.where(at == 1, low, 0.0)).astype(BF16)
    bc = []
    for half in range(2):
        arrived(bc_in, half)
        load_ext(ext, None, bc_ref, lanes_of(channels // LANES + half), lanes_of(half))
        pre = filtered(ext, wbc_ref, channels + half * LANES, half * LANES, rows)
        bc.append((pre * sigmoid(pre)).T.astype(BF16))
    width = LANES
    below = iota((rows, width), 0) >= RIM
    for slab in range(channels // width):
        lanes = slice(slab * width, (slab + 1) * width)
        arrived(x_in, slab)
        load_ext(ext, None, x_ref, lanes, lanes)
        pre = filtered(ext, wx_ref, slab * width, slab * width, rows, width)
        x_conv = (pre * sigmoid(pre)).astype(BF16).astype(F32)
        leave = spread(leave_step, slab, head_dim, width)
        leaving_x = jnp.where(below, x_conv * leave, 0.0).astype(BF16)
        sum_ref[0, :, lanes] = dot(bc[0], leaving_x, ((1,), (0,)))
        arrived(dy_in, slab)
        enter_dy = dy_ref[:, lanes].astype(F32) * spread(entering, slab, head_dim, width)
        masked = jnp.where(below, enter_dy, 0.0).astype(BF16)
        sum_ref[1, :, lanes] = dot(bc[1], masked, ((1,), (0,)))
        ls_ref[:, lanes] = leave[0:RIM]
        edy_ref[:, lanes] = enter_dy[0:RIM]
    top_ref[...] = ext[RIM : 2 * RIM, :]


def chunk_of(across, side, which):
    return 16 * across + 2 * side + which


def send_kernel(
    halo_ref, sum_ref, ls_ref, edy_ref, top_ref, tail_ref, wx_ref, wbc_ref, send_ref, ext,
):
    channels = ls_ref.shape[1]
    count = send_ref.shape[0]
    tall = 2 * RIM
    ext[0:RIM, :] = halo_ref[...].astype(F32)
    ext[RIM:, :] = top_ref[...]
    none = jnp.zeros((RIM, LANES), F32)

    def conv(w_ref, at, w_at):
        pre = filtered(ext, w_ref, at, w_at, RIM)
        return (pre * sigmoid(pre)).astype(BF16).astype(F32)

    bc = []
    for at in (0, LANES):
        top = jnp.concatenate([conv(wbc_ref, channels + at, at), none], axis=0).astype(BF16)
        bc.append(dot(top, diagonal(tall), ((0,), (0,))).astype(BF16))
    tail = tail_ref[...]
    for chunk in range(count):
        send_ref[chunk, send_ref.shape[1] - RIM :, :] = tail
    slabs = channels // LANES
    for slab in range(slabs):
        lanes = lanes_of(slab)
        across, tile = slab // (slabs // 2), slab % (slabs // 2)
        leaving_x = conv(wx_ref, slab * LANES, slab * LANES) * ls_ref[:, lanes]
        enter_dy = edy_ref[:, lanes]
        for which, top in enumerate((leaving_x, enter_dy)):
            top = jnp.concatenate([top, none], axis=0).astype(BF16)
            total = (sum_ref[which, :, lanes] + dot(bc[which], top, ((1,), (0,)))).astype(BF16)
            for side in range(LANES // tall):
                piece = total[side * tall : (side + 1) * tall]
                send_ref[chunk_of(across, side, which), tile * tall : (tile + 1) * tall, :] = piece


def scan_kernel(head_dim, got_ref, out_hbm, out_ref, tails, carries, sems):
    count, width, lanes = out_ref.shape
    tall = 2 * RIM
    tiles = width // tall
    me = lax.axis_index("ctx")
    backward = lax.rem(me, 2)
    across = me // (count // 2)
    for at in range(count):
        tails[RIM * at : RIM * (at + 1), :] = got_ref[at, width : width + RIM, :].astype(F32)
    shape = (lanes, tiles * lanes)
    head = iota(shape, 1) // head_dim + across * (tiles * lanes // head_dim)
    chosen = jnp.where(iota(shape, 0) == head, 1.0, 0.0).astype(BF16)
    carries[...] = dot(tails[...].astype(BF16), chosen, ((1,), (0,)))
    states = [jnp.zeros((tall, lanes), F32) for _ in range(tiles)]
    sent = []
    pieces = sems.shape[0]
    group = count // pieces
    for step in range(count):
        at = jnp.where(backward == 1, count - 1 - step, step)
        carry = carries[pl.ds(pl.multiple_of(at * RIM, RIM), RIM), :]
        carry = carry[0:1] + carry[1:2]
        for tile in range(tiles):
            rows = slice(tile * tall, (tile + 1) * tall)
            out_ref[at, rows, :] = states[tile].astype(BF16)
            states[tile] = carry[:, lanes_of(tile)] * states[tile] + got_ref[at, rows, :].astype(F32)
        if step % group == group - 1:
            first = jnp.where(backward == 1, count - 1 - step, step + 1 - group)
            sent.append(put(out_ref, out_hbm, sems.at[step // group], (pl.ds(first, group),)))
    for copy in sent:
        copy.wait()


def intra_kernel(
    head_dim, doc_ref, a_log_ref, skip_ref, x_hbm, dy_hbm, bc_hbm, halo_ref, wx_ref, wbc_ref, dt_ref,
    gs_hbm, ls_hbm, yi_ref,
    lx_ref, edy_ref, bcc_ref, gbc_ref, sbc_ref, hv_ref, rim_ref,
    x_ref, dy_ref, bc_ref, gs_ref, ls_ref, ext, bias, dgram,
    x_sems, dy_sems, bc_sems, out_sems,
):
    rows, channels = x_ref.shape
    heads = dt_ref.shape[0]
    doc = doc_ref[0]
    bc_in = fetch(bc_hbm, bc_ref, bc_sems)
    x_in = fetch(x_hbm, x_ref, x_sems)
    dy_in = fetch(dy_hbm, dy_ref, dy_sems)
    v = head_values(doc_ref, a_log_ref, dt_ref)
    for half in range(2):
        lanes = lanes_of(half)
        arrived(bc_in, half)
        load_ext(ext, halo_ref, bc_ref, lanes_of(channels // LANES + half), lanes)
        pre = filtered(ext, wbc_ref, channels + half * LANES, half * LANES, rows)
        gate = sigmoid(pre)
        bcc_ref[:, lanes] = (pre * gate).astype(BF16)
        sbc_ref[:, lanes] = gate * (1.0 + pre * (1.0 - gate))
    b_matrix = bcc_ref[:, 0:LANES]
    c_matrix = bcc_ref[:, LANES:]
    gram = dot(c_matrix, b_matrix, ((1,), (1,)))
    t_at, s_at = iota((rows, rows), 0), iota((rows, rows), 1)
    bias[...] = jnp.where((t_at >= s_at) & ((t_at >= doc) == (s_at >= doc)), 0.0, -1e30)
    dgram[...] = jnp.zeros_like(dgram)
    downto = jnp.where(t_at >= s_at, 1.0, 0.0)
    cum = v["cum"]
    cum_t = dot(downto, v["drop"], ((1,), (1,)), HIGHEST)
    skip = per_head(skip_ref, heads, rows)
    leave_step = columns(v["leaving"] * v["step"])
    entering, steps = columns(v["entering"]), columns(v["step"])
    skip = columns(skip)
    along_dt = jnp.zeros((heads, rows), F32)
    z_diff = jnp.zeros((heads, rows), F32)
    low_half = iota((rows, LANES), 1) < head_dim
    sent = []
    for slab in range(channels // LANES):
        lanes = lanes_of(slab)
        arrived(x_in, slab)
        load_ext(ext, halo_ref, x_ref, lanes, lanes)
        arrived(dy_in, slab)
        pre = filtered(ext, wx_ref, slab * LANES, slab * LANES, rows)
        gate = sigmoid(pre)
        x_bf = (pre * gate).astype(BF16)
        silu_grad = gate * (1.0 + pre * (1.0 - gate))
        x_conv = x_bf.astype(F32)
        step = spread(steps, slab, head_dim)
        leave = spread(leave_step, slab, head_dim)
        enter = spread(entering, slab, head_dim)
        skips = spread(skip, slab, head_dim)
        dy_bf = dy_ref[:, lanes]
        dy = dy_bf.astype(F32)
        lx_ref[:, lanes] = (x_conv * leave).astype(BF16)
        edy_ref[:, lanes] = (dy * enter).astype(BF16)
        scaled = (x_conv * step).astype(BF16)
        intra = jnp.zeros((rows, LANES), F32)
        d_scaled = jnp.zeros((rows, LANES), F32)
        for side in range(LANES // head_dim):
            head = slab * (LANES // head_dim) + side
            mine = low_half if side == 0 else jnp.logical_not(low_half)
            scaled_h = jnp.where(mine, scaled.astype(F32), 0.0).astype(BF16)
            dy_h = jnp.where(mine, dy, 0.0).astype(BF16)
            kernel = jnp.exp((cum_t[:, head : head + 1] - cum[head : head + 1, :]) + bias[...])
            mixing = (gram * kernel).astype(BF16)
            response = dot(dy_h, scaled, ((1,), (1,)))
            dgram[...] += response * kernel
            intra = intra + dot(mixing, scaled_h, ((1,), (0,)))
            d_scaled = d_scaled + dot(mixing, dy_h, ((0,), (0,)))
        yi_ref[:, lanes] = intra + skips * x_conv
        gs_ref[:, lanes] = (step * d_scaled + skips * dy) * silu_grad
        ls_ref[:, lanes] = leave * silu_grad
        rim_ref[0, :, lanes] = gs_ref[0:RIM, lanes]
        rim_ref[1, :, lanes] = ls_ref[0:RIM, lanes]
        group = channels // LANES // (out_sems.shape[0] // 2)
        if slab % group == group - 1:
            at = (slice(None), slice((slab + 1 - group) * LANES, (slab + 1) * LANES))
            sent.append(put(gs_ref, gs_hbm, out_sems.at[slab // group * 2], at))
            sent.append(put(ls_ref, ls_hbm, out_sems.at[slab // group * 2 + 1], at))
        along_dt = along_dt + head_sum_exact(x_conv * d_scaled, slab, head_dim, heads)
        z_diff = z_diff + head_sum_exact(
            dy * intra - scaled.astype(F32) * d_scaled, slab, head_dim, heads
        )
    d_gram = dgram[...]
    gbc_ref[:, 0:LANES] = dot(d_gram, c_matrix.astype(F32), ((0,), (0,)), HIGHEST)
    gbc_ref[:, LANES:] = dot(d_gram, b_matrix.astype(F32), ((1,), (0,)), HIGHEST)
    small = [
        v["step"],
        v["entering"],
        along_dt,
        z_diff,
        v["carry"],
        v["decay"],
        1.0 / (1.0 + jnp.exp(-dt_ref[...])),
    ]
    for at, values in enumerate(small):
        hv_ref[at] = values
    for copy in sent:
        copy.wait()


def state_of(st_ref, which, slab):
    tall = 2 * RIM
    tiles = st_ref.shape[1] // tall
    across, tile = slab // tiles, slab % tiles
    sides = LANES // tall
    rows = slice(tile * tall, (tile + 1) * tall)
    return jnp.concatenate(
        [st_ref[chunk_of(across, side, which), rows, :] for side in range(sides)], axis=0
    )


def bc_kernel(
    core_ref, st_ref, lx_ref, edy_ref, b_ref, gbc_ref, sbc_ref, rim_ref, wbc_ref,
    keep_ref, give_ref, halo_ref, ext, total,
):
    rows = lx_ref.shape[0]
    taps = wbc_ref.shape[0]
    slabs = lx_ref.shape[1] // LANES
    state, dstate = [
        jnp.concatenate([state_of(st_ref, which, slab) for slab in range(slabs)], axis=1)
        for which in range(2)
    ]
    grad_b = gbc_ref[:, 0:LANES] + dot(lx_ref[...], dstate, ((1,), (1,)))
    grad_c = gbc_ref[:, LANES:] + dot(edy_ref[...], state, ((1,), (1,)))
    ext[0:rows, 0:LANES] = grad_b * sbc_ref[:, 0:LANES]
    ext[0:rows, LANES:] = grad_c * sbc_ref[:, LANES:]
    ext[rows:, :] = jnp.zeros((RIM, 2 * LANES), F32)
    w = wbc_ref[...].astype(F32)
    out = w[taps - 1 : taps] * ext[0:rows, :]
    for tap in range(taps - 1):
        out = out + w[tap : tap + 1] * ext[pl.ds(taps - 1 - tap, rows), :]
    total[...] = out
    half = rows // 2
    core = core_ref[0]
    keep_ref[...] = total[pl.ds(pl.multiple_of(core * half, half), half), :]
    give_ref[...] = total[pl.ds(pl.multiple_of((1 - core) * half, half), half), :].astype(BF16)
    d_leaving = dot(b_ref[0 : 2 * RIM, 0:LANES], dstate, ((1,), (0,)))[0:RIM]
    channels = rim_ref.shape[2]
    halo_ref[:, 0:channels] = (rim_ref[0] + rim_ref[1] * d_leaving).astype(BF16)
    halo_ref[:, channels:] = ext[0:RIM, :].astype(BF16)


def join_kernel(keep_ref, got_ref, halo_ref, wbc_ref, out_ref, ext):
    half = keep_ref.shape[0]
    taps = wbc_ref.shape[0]
    wide = keep_ref.shape[1]
    out_ref[0:half, :] = (keep_ref[...] + got_ref[...].astype(F32)).astype(BF16)
    ext[0:RIM, :] = jnp.zeros((RIM, wide), F32)
    ext[RIM:, :] = halo_ref[:, halo_ref.shape[1] - wide :].astype(F32)
    w = wbc_ref[...].astype(F32)
    rim = jnp.zeros((RIM, wide), F32)
    for tap in range(taps - 1):
        rim = rim + w[tap : tap + 1] * ext[pl.ds(taps - 1 - tap, RIM), :]
    out_ref[half:, :] = rim.astype(BF16)


def sum_kernel(*refs):
    out_ref = refs[-1]
    total = refs[0][...].astype(F32)
    for ref in refs[1:-1]:
        total = total + ref[...].astype(F32)
    out_ref[...] = total.astype(BF16)


def last_kernel(core_ref, mine_ref, got_ref, out_ref, total):
    rows = out_ref.shape[0]
    half = rows // 2
    core = core_ref[0]
    total[pl.ds(pl.multiple_of(core * half, half), half), :] = mine_ref[0:half, :].astype(F32)
    total[pl.ds(pl.multiple_of((1 - core) * half, half), half), :] = got_ref[0:half, :].astype(F32)
    total[rows - RIM :, :] += mine_ref[half:, :].astype(F32) + got_ref[half:, :].astype(F32)
    out_ref[...] = total[...].astype(BF16)


def y_kernel(head_dim, st_ref, bcc_ref, hv_ref, yi_ref, edy_ref, y_hbm, enter_ref, y_ref, ys_ref, sems):
    rows, channels = edy_ref.shape
    heads = hv_ref.shape[1]
    slabs = channels // LANES
    group = slabs // sems.shape[0]
    c_matrix = bcc_ref[:, LANES:]
    entering = columns(hv_ref[1])
    sent = []
    for slab in range(slabs):
        lanes = lanes_of(slab)
        y_state = dot(c_matrix, state_of(st_ref, 0, slab), ((1,), (0,)))
        ys_ref[:, lanes] = y_state
        y_ref[:, lanes] = (yi_ref[:, lanes] + spread(entering, slab, head_dim) * y_state).astype(BF16)
        if slab % group == group - 1:
            at = (slice(None), slice((slab + 1 - group) * LANES, (slab + 1) * LANES))
            sent.append(put(y_ref, y_hbm, sems.at[slab // group], at))
    enter_term = jnp.zeros((heads, rows), F32)
    for slab in range(slabs):
        lanes = lanes_of(slab)
        enter_term = enter_term + head_sum(
            edy_ref[:, lanes].astype(F32) * ys_ref[:, lanes], slab, head_dim, heads
        )
    enter_ref[...] = enter_term
    for copy in sent:
        copy.wait()


def xc_kernel(
    head_dim, gs_hbm, ls_hbm, st_ref, bcc_ref, lx_ref,
    g_ref, leave_ref, overlap_ref, gs_ref, ls_ref, gs_sems, ls_sems,
):
    rows, channels = lx_ref.shape
    heads = leave_ref.shape[0]
    slabs = channels // LANES
    gs_in = fetch(gs_hbm, gs_ref, gs_sems)
    ls_in = fetch(ls_hbm, ls_ref, ls_sems)
    b_matrix = bcc_ref[:, 0:LANES]
    leave_term = jnp.zeros((heads, rows), F32)
    overlap = jnp.zeros((heads, LANES), F32)
    for slab in range(slabs):
        lanes = lanes_of(slab)
        dstate = state_of(st_ref, 1, slab)
        product = state_of(st_ref, 0, slab).astype(F32) * dstate.astype(F32)
        head = iota((heads, LANES), 1) // head_dim + slab * (LANES // head_dim)
        own = iota((heads, LANES), 0) == head
        overlap = overlap + jnp.where(own, jnp.sum(product, axis=0, keepdims=True), 0.0)
        d_leaving = dot(b_matrix, dstate, ((1,), (0,)))
        g_ref[:, lanes] = d_leaving
        leave_term = leave_term + head_sum(
            lx_ref[:, lanes].astype(F32) * d_leaving, slab, head_dim, heads
        )
    leave_ref[...] = leave_term
    overlap_ref[...] = overlap
    for slab in range(slabs):
        lanes = lanes_of(slab)
        arrived(gs_in, slab)
        arrived(ls_in, slab)
        g_ref[:, lanes] = gs_ref[:, lanes] + ls_ref[:, lanes] * g_ref[:, lanes]


def x_kernel(g_ref, halo_ref, wx_ref, gx_hbm, gx_ref, ext, sems):
    rows, channels = g_ref.shape
    taps = wx_ref.shape[0]
    slabs = channels // LANES
    group = slabs // sems.shape[0]
    low = rows - RIM
    ext[0:RIM, :] = g_ref[low:, :]
    ext[RIM:, :] = halo_ref[:, 0:channels].astype(F32)
    sent = []
    for slab in range(slabs):
        lanes = lanes_of(slab)
        w = wx_ref[:, lanes].astype(F32)
        body = w[taps - 1 : taps] * g_ref[0:low, lanes]
        edge = w[taps - 1 : taps] * ext[0:RIM, lanes]
        for tap in range(taps - 1):
            ahead = taps - 1 - tap
            body = body + w[tap : tap + 1] * g_ref[pl.ds(ahead, low), lanes]
            edge = edge + w[tap : tap + 1] * ext[pl.ds(ahead, RIM), lanes]
        gx_ref[:, lanes] = jnp.concatenate([body, edge], axis=0).astype(BF16)
        if slab % group == group - 1:
            at = (slice(None), slice((slab + 1 - group) * LANES, (slab + 1) * LANES))
            sent.append(put(gx_ref, gx_hbm, sems.at[slab // group], at))
    for copy in sent:
        copy.wait()


def dt_kernel(hv_ref, enter_ref, leave_ref, overlap_ref, gdt_ref):
    heads, rows = leave_ref.shape
    step, _, along_dt, z_diff, carry, decay, dt_gate = [hv_ref[at] for at in range(7)]
    leave_term, overlap = leave_ref[...], overlap_ref[...]
    final = jnp.sum(leave_term, axis=1, keepdims=True) + carry * jnp.sum(overlap, axis=1, keepdims=True)
    d_cum = z_diff + enter_ref[...] - leave_term
    d_cum = d_cum + jnp.where(iota((heads, rows), 1) == rows - 1, final, 0.0)
    after = jnp.where(iota((rows, rows), 0) >= iota((rows, rows), 1), 1.0, 0.0)
    d_log = dot(d_cum, after, ((1,), (0,)), HIGHEST)
    gdt_ref[...] = (along_dt + leave_term / step - decay * d_log) * dt_gate


def smem():
    return pl.BlockSpec(memory_space=pltpu.SMEM)


def vmem():
    return pl.BlockSpec(memory_space=pltpu.VMEM)


def hbm():
    return pl.BlockSpec(memory_space=pltpu.HBM)


def call(kernel, name, scalars, far, near, far_out, near_out, scratch=()):
    far = [pltpu.with_memory_space_constraint(a, pltpu.HBM) for a in far]
    out = [pltpu.HBM(s, d) for s, d in far_out] + [jax.ShapeDtypeStruct(s, d) for s, d in near_out]
    specs = [hbm() for _ in far_out] + [vmem() for _ in near_out]
    many = len(out) > 1
    return pl.pallas_call(
        kernel,
        name=name,
        out_shape=out if many else out[0],
        in_specs=[smem() for _ in scalars] + [hbm() for _ in far] + [vmem() for _ in near],
        out_specs=specs if many else specs[0],
        scratch_shapes=list(scratch),
        compiler_params=pltpu.CompilerParams(vmem_limit_bytes=VMEM_LIMIT),
    )(*scalars, *far, *near)


def shift_ctx(values, by):
    size = lax.axis_size("ctx")
    pairs = [(i, i + by) for i in range(size) if 0 <= i + by < size]
    return lax.ppermute(values, "ctx", pairs)


def swap_core(values):
    size = lax.axis_size("head")
    return lax.ppermute(values, "head", [(i, i ^ 1) for i in range(size)])


def around(values, by):
    size = lax.axis_size("head")
    return lax.ppermute(values, "head", [(i, (i + 2 * by) % size) for i in range(size)])


def body(x_raw, bc_raw, conv_x_w, conv_bc_w, dt_raw, a_log, d_skip, doc_starts, grad_y):
    rows, channels = x_raw.shape
    heads = a_log.shape[0]
    head_dim = channels // heads
    wide = bc_raw.shape[1]
    count = lax.axis_size("ctx")
    part = channels // count
    core = (lax.axis_index("head") % 2).astype(jnp.int32).reshape(1)
    halo = shift_ctx(jnp.concatenate([x_raw[rows - RIM :], bc_raw[rows - RIM :]], axis=1), 1)
    wide_bf, wide_f = ((rows, channels), BF16), ((rows, channels), F32)
    sems = pltpu.SemaphoreType.DMA
    two = sems((2,))
    inputs = [pltpu.VMEM(*wide_bf), pltpu.VMEM(*wide_bf), pltpu.VMEM((rows, wide), BF16)]
    input_sems = [two, two, sems((1,))]
    ext = pltpu.VMEM((rows + RIM, channels + wide), F32)
    sent = ((count, 2 * part + RIM, LANES), BF16)
    states = ((count, 2 * part, LANES), BF16)
    sums, leave_top, dy_top, top, tail = call(
        functools.partial(gather_kernel, head_dim),
        "gather",
        [doc_starts, a_log],
        [x_raw, grad_y, bc_raw],
        [conv_x_w, conv_bc_w, dt_raw],
        [],
        [
            ((2, LANES, channels), F32),
            ((RIM, channels), F32),
            ((RIM, channels), F32),
            ((RIM, channels + wide), F32),
            ((RIM, LANES), BF16),
        ],
        [*inputs, ext, *input_sems],
    )
    send = call(
        send_kernel,
        "send",
        [],
        [],
        [halo, sums, leave_top, dy_top, top, tail, conv_x_w, conv_bc_w],
        [],
        [sent],
        [pltpu.VMEM((2 * RIM, channels + wide), F32)],
    )
    got = lax.all_to_all(send, "ctx", 0, 0)
    scanned = call(
        functools.partial(scan_kernel, head_dim),
        "scan",
        [],
        [],
        [got],
        [states],
        [],
        [
            pltpu.VMEM(*states),
            pltpu.VMEM((count * RIM, LANES), F32),
            pltpu.VMEM((count * RIM, channels // 2), F32),
            sems((8,)),
        ],
    )
    scanned, dt_later = lax.optimization_barrier((scanned, dt_raw))
    gs, ls, yi, lx, edy, bcc, gbc, sbc, hv, first = call(
        functools.partial(intra_kernel, head_dim),
        "intra",
        [doc_starts, a_log, d_skip],
        [x_raw, grad_y, bc_raw],
        [halo, conv_x_w, conv_bc_w, dt_later],
        [wide_f, wide_f],
        [
            wide_f,
            wide_bf,
            wide_bf,
            ((rows, wide), BF16),
            ((rows, wide), F32),
            ((rows, wide), F32),
            ((7, heads, rows), F32),
            ((2, RIM, channels), F32),
        ],
        [
            *inputs,
            pltpu.VMEM(*wide_f),
            pltpu.VMEM(*wide_f),
            ext,
            pltpu.VMEM((rows, rows), F32),
            pltpu.VMEM((rows, rows), F32),
            *input_sems,
            sems((4,)),
        ],
    )
    st = lax.all_to_all(scanned, "ctx", 0, 0)
    half = rows // 2
    keep, give, rim = call(
        bc_kernel,
        "grad_bc",
        [core],
        [],
        [st, lx, edy, bcc, gbc, sbc, first, conv_bc_w],
        [],
        [
            ((half, wide), F32),
            ((half, wide), BF16),
            ((RIM, channels + wide), BF16),
        ],
        [pltpu.VMEM((rows + RIM, wide), F32), pltpu.VMEM((rows, wide), F32)],
    )
    next_rim = shift_ctx(rim, -1)
    other = swap_core(give)
    st, keep = lax.optimization_barrier((st, keep))
    y_out, enter_term = call(
        functools.partial(y_kernel, head_dim),
        "y_out",
        [],
        [],
        [st, bcc, hv, yi, edy],
        [wide_bf],
        [((heads, rows), F32)],
        [pltpu.VMEM(*wide_bf), pltpu.VMEM(*wide_f), sems((4,))],
    )
    grad_xc, leave_term, overlap = call(
        functools.partial(xc_kernel, head_dim),
        "grad_xc",
        [],
        [gs, ls],
        [st, bcc, lx],
        [],
        [wide_f, ((heads, rows), F32), ((heads, LANES), F32)],
        [pltpu.VMEM(*wide_f), pltpu.VMEM(*wide_f), two, two],
    )
    other, next_rim, enter_term, leave_term = lax.optimization_barrier(
        (other, next_rim, enter_term, leave_term)
    )
    message = ((half + RIM, wide), BF16)
    joined = call(
        join_kernel,
        "join",
        [],
        [],
        [keep, other, next_rim, conv_bc_w],
        [],
        [message],
        [pltpu.VMEM((2 * RIM, wide), F32)],
    )
    ring = lax.axis_size("head") // 2
    pieces = [joined] + [around(joined, by) for by in range(1, ring)]
    grad_x = call(
        x_kernel,
        "grad_x",
        [],
        [],
        [grad_xc, next_rim, conv_x_w],
        [wide_bf],
        [],
        [pltpu.VMEM(*wide_bf), pltpu.VMEM((2 * RIM, channels), F32), sems((4,))],
    )
    pieces, grad_x = lax.optimization_barrier((pieces, grad_x))
    summed = call(sum_kernel, "sum", [], [], pieces, [], [message])
    summed, leave_term = lax.optimization_barrier((summed, leave_term))
    swapped = swap_core(summed)
    grad_dt = call(
        dt_kernel, "grad_dt", [], [], [hv, enter_term, leave_term, overlap], [], [((heads, rows), F32)]
    )
    swapped, grad_dt = lax.optimization_barrier((swapped, grad_dt))
    grad_bc = call(
        last_kernel,
        "last",
        [core],
        [],
        [summed, swapped],
        [],
        [((rows, wide), BF16)],
        [pltpu.VMEM((rows, wide), F32)],
    )
    return (y_out, grad_x, grad_bc, grad_dt)


def solution(mesh):
    in_specs = (
        P("ctx", "head"),
        P("ctx", None),
        P(None, "head"),
        P(),
        P("head", "ctx"),
        P("head"),
        P("head"),
        P("ctx"),
        P("ctx", "head"),
    )
    out_specs = (P("ctx", "head"), P("ctx", "head"), P("ctx", None), P("head", "ctx"))
    return jax.shard_map(body, mesh=mesh, in_specs=in_specs, out_specs=out_specs, check_vma=False)
```
